128 devices in a mesh: seq: 32 (over y, x, core), head: 4 (over z).
Axes of the slice: x: 4, y: 4, z: 4, core: 2. Of those that a mesh axis runs over, the one named last changes fastest.
Arguments:
- byte_in: bfloat16 [4096, 8, 1024], P('seq'), may hold values from -6 to 6
- local_gain: float32 [1024], replicated, may hold values from 0.25 to 1.75
- local_qkv: bfloat16 [1024, 3, 1024], P(None, None, 'head'), may hold values from -0.1875 to 0.1875
- local_out: bfloat16 [1024, 1024], P('head'), may hold values from -0.1875 to 0.1875
- mlp_up: bfloat16 [1024, 4096], P(None, 'head'), may hold values from -0.1875 to 0.1875
- mlp_down: bfloat16 [4096, 1024], P('head'), may hold values from -0.09375 to 0.09375
- local_scale: float32 [8], P('head'), may hold values from 1 to 40
- patch_proj: bfloat16 [1024, 256], replicated, may hold values from -0.1875 to 0.1875
- global_gain: float32 [2048], replicated, may hold values from 0.25 to 1.75
- global_qkv: bfloat16 [2048, 3, 2048], P(None, None, 'head'), may hold values from -0.125 to 0.125
- global_out: bfloat16 [2048, 2048], P('head'), may hold values from -0.125 to 0.125
- global_scale: float32 [16], P('head'), may hold values from 1 to 40
- back_proj: bfloat16 [256, 1024], replicated, may hold values from -0.375 to 0.375
- owners: int32 [32, 64], replicated, may hold values from 0 to 31, as said below
Outputs:
- byte_out: bfloat16 [4096, 8, 1024], P('seq', 'head')
- global_state: bfloat16 [4096, 2048], P('seq', 'head')
The draws below stay inside these ranges and needn't reach their ends.
Inputs may be any that keep to these rules, and one draw needn't show every extreme that they name: `owners`: row s names, for each of the 64 blocks of 2 patches of byte range s in order, its owner; each row names every owner exactly twice.
All inputs are finite; a program needn't handle non-finite values.
Results may differ from the reference program's by a relative error of at most 0.028.
The reference program's roundings to bfloat16 on the way count: a program that leaves them out, or rounds other values in their place, can miss the bound.
Values may be sent and summed in bfloat16 or wider, within the bound.
A program may use at most 128 MiB of HBM per device.

```python
import math
import jax
import jax.numpy as jnp
from jax import lax

DL = 1024
FF = 4096
LHEADS = 8
GHEADS = 16
HEAD = 128
G = 2048
GP = 256
PATCH = 8
PATCH_DEV = 128
BLOCK = 2
SOURCES = 32
PATCHES = 4096


def draw_owners(key, part):
    subkeys = jax.random.split(jax.random.fold_in(key, 11), SOURCES)
    listed = jax.vmap(lambda subkey: jax.random.permutation(subkey, 2 * SOURCES))(subkeys)
    return (listed // 2).astype(jnp.int32)


def draw_local_scale(key, part):
    return jax.random.uniform(jax.random.fold_in(key, 22), (LHEADS,), jnp.float32, 1.0, 4.0)


def draw_global_scale(key, part):
    return jax.random.uniform(jax.random.fold_in(key, 32), (GHEADS,), jnp.float32, 1.0, 4.0)


def steps_of(stream_key, extent, shards, low, largest):
    loudness, own = 1.0, jax.random.fold_in(stream_key, 6)
    for axis_at, blocks in shards:
        steps = jnp.exp(jax.random.uniform(jax.random.fold_in(own, axis_at), (blocks,), jnp.float32, low / len(shards), largest / len(shards)))
        loudness = loudness * jnp.repeat(steps, extent[axis_at] // blocks).reshape([-1 if axis == axis_at else 1 for axis in range(len(extent))])
    return loudness


def centred(own_key, extent, scale, bound, cuts=(), kind=jnp.bfloat16):
    drawn = jax.random.normal(own_key, extent, jnp.float32) * scale
    if len(cuts) > 0:
        drawn = steps_of(own_key, extent, cuts, -0.22, 0.18) * drawn
    return jnp.clip(drawn, min=-bound, max=bound).astype(kind)


def setup_inputs(seed: int = 0) -> dict:
    streams_of = jax.random.split(jax.random.key(seed), 15)
    byte_in = centred(streams_of[0], (PATCHES, PATCH, DL), 1.0, 6.0, ((0, 32),))
    local_gain = jnp.clip(1.0 + 0.15 * jax.random.normal(streams_of[1], (DL,), jnp.float32), 0.25, 1.75)
    local_qkv = centred(streams_of[2], (DL, 3, DL), DL ** -0.5, 0.1875, ((2, 4),))
    local_out = centred(streams_of[3], (DL, DL), DL ** -0.5, 0.1875, ((0, 4),))
    mlp_up = centred(streams_of[4], (DL, FF), DL ** -0.5, 0.1875, ((1, 4),))
    mlp_down = centred(streams_of[5], (FF, DL), FF ** -0.5, 0.09375, ((0, 4),))
    local_scale = draw_local_scale(jax.random.fold_in(streams_of[14], 71), 0)
    patch_proj = centred(streams_of[7], (DL, GP), DL ** -0.5, 0.1875)
    global_gain = jnp.clip(1.0 + 0.15 * jax.random.normal(streams_of[8], (G,), jnp.float32), 0.25, 1.75)
    global_qkv = centred(streams_of[9], (G, 3, G), G ** -0.5, 0.125, ((2, 4),))
    global_out = centred(streams_of[10], (G, G), G ** -0.5, 0.125, ((0, 4),))
    global_scale = draw_global_scale(jax.random.fold_in(streams_of[14], 71), 0)
    back_proj = centred(streams_of[12], (GP, DL), GP ** -0.5, 0.375)
    owners = draw_owners(jax.random.fold_in(streams_of[14], 71), 0)
    return {"byte_in": byte_in, "local_gain": local_gain, "local_qkv": local_qkv, "local_out": local_out, "mlp_up": mlp_up, "mlp_down": mlp_down, "local_scale": local_scale, "patch_proj": patch_proj, "global_gain": global_gain, "global_qkv": global_qkv, "global_out": global_out, "global_scale": global_scale, "back_proj": back_proj, "owners": owners}


EPSILON = 1e-06
NEGATIVE = -1e+30

def rms_norm(values, gain):
    mean_square = lax.optimization_barrier(jnp.mean(values * values, axis=-1, keepdims=True))
    return values * lax.rsqrt(mean_square + EPSILON) * gain

def unit_heads(values, head_count):
    shaped = values.reshape(values.shape[0], head_count, -1)
    mean_square = lax.optimization_barrier(jnp.mean(shaped * shaped, axis=-1, keepdims=True))
    return shaped * lax.rsqrt(mean_square + EPSILON)

def through_bf16(values):
    return lax.optimization_barrier(values.astype(jnp.bfloat16)).astype(jnp.float32)

def patch_attention(queries, key_rows, values, head_scale):
    patch_span = queries.shape[1]
    scores = jnp.einsum('pihd,pjhd->phij', queries.astype(jnp.float32), key_rows.astype(jnp.float32))
    scores = scores * (head_scale[:, None, None] / math.sqrt(HEAD))
    causal = jnp.tril(jnp.ones((patch_span, patch_span), dtype=bool))
    scores = jnp.where(causal, scores, NEGATIVE)
    row_max = lax.optimization_barrier(jnp.max(scores, axis=-1, keepdims=True))
    weights = jnp.where(causal, jnp.exp(scores - row_max), 0.0)
    weight_sum = lax.optimization_barrier(jnp.sum(weights, axis=-1))
    summed = jnp.einsum('phij,pjhd->pihd', through_bf16(weights), values.astype(jnp.float32))
    return (summed / jnp.transpose(weight_sum, (0, 2, 1))[..., None]).astype(jnp.bfloat16)

def local_section(byte_block, local_gain, local_qkv, local_out, mlp_up, mlp_down, local_scale, patch_proj):
    patch_count = byte_block.shape[0]
    byte_rows = byte_block.reshape(-1, DL).astype(jnp.float32)
    normed = rms_norm(byte_rows, local_gain).astype(jnp.bfloat16)
    projected = jnp.dot(normed, local_qkv.reshape(DL, 3 * DL), preferred_element_type=jnp.float32)
    queries = unit_heads(projected[:, :DL], LHEADS).astype(jnp.bfloat16).reshape(patch_count, PATCH, LHEADS, HEAD)
    key_rows = unit_heads(projected[:, DL:2 * DL], LHEADS).astype(jnp.bfloat16).reshape(patch_count, PATCH, LHEADS, HEAD)
    values = projected[:, 2 * DL:].astype(jnp.bfloat16).reshape(patch_count, PATCH, LHEADS, HEAD)
    attended = patch_attention(queries, key_rows, values, local_scale).reshape(-1, DL)
    attn_term = jnp.dot(attended, local_out, preferred_element_type=jnp.float32)
    activated = jax.nn.gelu(jnp.dot(normed, mlp_up, preferred_element_type=jnp.float32), approximate=True).astype(jnp.bfloat16)
    mlp_term = jnp.dot(activated, mlp_down, preferred_element_type=jnp.float32)
    byte_state = (byte_rows + attn_term + mlp_term).astype(jnp.bfloat16)
    patch_in = jnp.dot(byte_state, patch_proj, preferred_element_type=jnp.float32).reshape(patch_count, PATCH * GP).astype(jnp.bfloat16)
    return (byte_state.reshape(patch_count, PATCH, DL), patch_in)

def global_head(arguments):
    head_query, head_keys, head_values, head_scale = arguments
    positions = jnp.arange(PATCHES, dtype=jnp.int32)

    def query_block(block_args):
        block_query, block_pos = block_args
        scores = jnp.dot(block_query, head_keys.T, preferred_element_type=jnp.float32) * (head_scale / math.sqrt(HEAD))
        visible = positions[None, :] <= block_pos[:, None]
        scores = jnp.where(visible, scores, NEGATIVE)
        row_max = lax.optimization_barrier(jnp.max(scores, axis=-1, keepdims=True))
        weights = jnp.where(visible, jnp.exp(scores - row_max), 0.0)
        weight_sum = lax.optimization_barrier(jnp.sum(weights, axis=-1))
        summed = jnp.dot(weights.astype(jnp.bfloat16), head_values, preferred_element_type=jnp.float32)
        return (summed / weight_sum[:, None]).astype(jnp.bfloat16)
    outputs = lax.map(query_block, (head_query.reshape(-1, PATCH_DEV, HEAD), positions.reshape(-1, PATCH_DEV)))
    return outputs.reshape(PATCHES, HEAD)

def reference(byte_in, local_gain, local_qkv, local_out, mlp_up, mlp_down, local_scale, patch_proj, global_gain, global_qkv, global_out, global_scale, back_proj, owners):

    def local_part(byte_block):
        return local_section(byte_block, local_gain, local_qkv, local_out, mlp_up, mlp_down, local_scale, patch_proj)
    byte_state, patch_in = lax.map(local_part, byte_in.reshape(-1, PATCH_DEV, PATCH, DL))
    byte_state = byte_state.reshape(PATCHES, PATCH, DL)
    patch_in = patch_in.reshape(PATCHES, G)
    gnormed = rms_norm(patch_in.astype(jnp.float32), global_gain).astype(jnp.bfloat16)
    global_proj = jnp.dot(gnormed, global_qkv.reshape(G, 3 * G), preferred_element_type=jnp.float32)
    gquery = unit_heads(global_proj[:, :G], GHEADS).astype(jnp.bfloat16)
    global_keys = unit_heads(global_proj[:, G:2 * G], GHEADS).astype(jnp.bfloat16)
    gvalues = global_proj[:, 2 * G:].astype(jnp.bfloat16).reshape(PATCHES, GHEADS, HEAD)
    attended = lax.map(global_head, (jnp.transpose(gquery, (1, 0, 2)), jnp.transpose(global_keys, (1, 0, 2)), jnp.transpose(gvalues, (1, 0, 2)), global_scale))
    attended = jnp.transpose(attended, (1, 0, 2)).reshape(PATCHES, G)
    result = (patch_in.astype(jnp.float32) + jnp.dot(attended, global_out, preferred_element_type=jnp.float32)).astype(jnp.bfloat16)
    position = jnp.arange(PATCHES, dtype=jnp.int32)
    source = (position // PATCH_DEV).astype(jnp.int32)
    column = (position % PATCH_DEV // BLOCK).astype(jnp.int32)
    listed = owners[source, column].astype(jnp.int32)
    ordering = jnp.argsort(listed * PATCHES + position)
    global_state = result[ordering]
    back_term = jnp.dot(result.reshape(PATCHES * PATCH, GP), back_proj, preferred_element_type=jnp.float32)
    byte_out = (byte_state.reshape(-1, DL).astype(jnp.float32) + back_term).reshape(PATCHES, PATCH, DL).astype(jnp.bfloat16)
    return (byte_out, global_state)
```

```python
import functools
import math

import jax
import jax.numpy as jnp
from jax import lax
from jax.experimental import pallas as pl
from jax.experimental.pallas import tpu as pltpu
from jax.sharding import PartitionSpec as P

EPS = 1e-06
NEG = -1e30
MESH = pl.DeviceIdType.MESH
F32 = jnp.float32
BF16 = jnp.bfloat16
XN = 4
YN = 4
ZN = 4
CHUNKS = 4
EARLY = 2
HD = 128


def dot(a, b):
    return jnp.dot(a, b, preferred_element_type=F32)


def dot_t(a, b):
    return lax.dot_general(a, b, (((1,), (1,)), ((), ())), preferred_element_type=F32)


def unit(v):
    return v * lax.rsqrt(jnp.mean(v * v, axis=-1, keepdims=True) + EPS)


def kernel(
    x_hbm, wqkv_hbm, wo_hbm, up_hbm, down_hbm, pp_hbm, gqkv_hbm, gout_hbm, back_hbm,
    gain_ref, ggain_ref, owners_ref, lscale_ref, gscale_ref,
    byte_ref, perm_ref,
    xv, wqkv, wo, up, down, ppw, gqkv, gout, back,
    act, part, ppf, bsend, brecv, ownf, ppsend, pprecv, ppown, pin,
    gn, qkvs, kvbuf, qbuf, m_ref, l_ref, acc, osend, orecv, rsend, rrecv, bst,
    lsem, pp_s, pp_r, ag_s, ag_r, bk_s, bk_r, xk_s, xk_r, xq_s, xq_r,
    y_s, y_r, c_s, c_r, o_s, o_r, r_s, r_r,
):
    s = lax.axis_index("seq")
    z = lax.axis_index("head")
    core = lax.rem(s, 2)
    x = lax.rem(s // 2, XN)
    y = s // (2 * XN)
    rows = xv.shape[0] // CHUNKS
    span = rows // 8
    own = 2 * span

    def seq_of(yy, xx, cc):
        return (yy * XN + xx) * 2 + cc

    def zpeer(d):
        return (s, lax.rem(z + d, ZN))

    def xpeer(d):
        return (seq_of(y, lax.rem(x + d, XN), core), z)

    y_up = (seq_of(lax.rem(y + 1, YN), x, core), z)
    y_down = (seq_of(lax.rem(y + YN - 1, YN), x, core), z)
    sibling = (seq_of(y, x, 1 - core), z)

    loads = [
        pltpu.make_async_copy(a, b, lsem.at[i])
        for i, (a, b) in enumerate(
            ((x_hbm, xv), (wqkv_hbm, wqkv), (up_hbm, up), (wo_hbm, wo), (down_hbm, down),
             (pp_hbm, ppw), (gqkv_hbm, gqkv), (gout_hbm, gout), (back_hbm, back))
        )
    ]
    for load in loads:
        load.start()

    barrier = pltpu.get_barrier_semaphore()
    peers = [zpeer(d) for d in (1, 2, 3)] + [xpeer(d) for d in (1, 2, 3)] + [y_up, y_down, sibling]
    for peer in peers:
        pl.semaphore_signal(barrier, inc=1, device_id=peer, device_id_type=MESH)
    pl.semaphore_wait(barrier, len(peers))

    def remote(src, dst, ss, rs, peer):
        return pltpu.make_async_remote_copy(
            src_ref=src, dst_ref=dst, send_sem=ss, recv_sem=rs, device_id=peer, device_id_type=MESH
        )

    def pp_copy(c, d):
        return remote(
            ppsend.at[c, lax.rem(z + d, ZN)], pprecv.at[c, d - 1], pp_s.at[c, d - 1], pp_r.at[c, d - 1], zpeer(d)
        )

    def ag_copy(c, d):
        return remote(pin.at[z, c], pin.at[z, c], ag_s.at[c, d - 1], ag_r.at[c, d - 1], zpeer(d))

    def ag_arrival(c, d):
        piece = pin.at[lax.rem(z + ZN - d, ZN), c]
        return remote(piece, piece, ag_s.at[c, d - 1], ag_r.at[c, d - 1], zpeer(d))

    def bulk_copy(c, d):
        return remote(
            bsend.at[c, lax.rem(z + d, ZN)], brecv.at[c, d - 1], bk_s.at[c, d - 1], bk_r.at[c, d - 1], zpeer(d)
        )

    def finish_patches(c):
        total = ppown[c]
        for d in (1, 2, 3):
            pp_copy(c, d).wait_recv()
            total = total + pprecv[c, d - 1].astype(F32)
        pin[z, c] = total.astype(BF16)
        for d in (2, 1, 3):
            ag_copy(c, d).start()

    row_i = lax.broadcasted_iota(jnp.int32, (rows, rows), 0)
    col_i = lax.broadcasted_iota(jnp.int32, (rows, rows), 1)
    to_byte_major = jnp.where(
        col_i == lax.rem(row_i, span) * 8 + row_i // span, 1.0, 0.0
    ).astype(BF16)

    def chunk(c, carry):
        @pl.when(c == 0)
        def _():
            loads[0].wait()
            loads[1].wait()

        xp = dot(to_byte_major, xv[pl.ds(pl.multiple_of(c * rows, rows), rows), :])
        normed = (
            xp * lax.rsqrt(jnp.mean(xp * xp, axis=-1, keepdims=True) + EPS) * gain_ref[...]
        ).astype(BF16)
        q2 = dot(normed, wqkv[0])
        k2 = dot(normed, wqkv[1])
        v2 = dot(normed, wqkv[2]).astype(BF16)
        rr = lax.broadcasted_iota(jnp.int32, (rows, rows), 0)
        cc = lax.broadcasted_iota(jnp.int32, (rows, rows), 1)
        seen = (lax.rem(rr, span) == lax.rem(cc, span)) & (cc // span <= rr // span)
        heads = []
        for h in range(2):
            cut = slice(h * HD, (h + 1) * HD)
            scores = dot_t(unit(q2[:, cut]).astype(BF16), unit(k2[:, cut]).astype(BF16))
            scores = jnp.where(seen, scores * (lscale_ref[h] / math.sqrt(HD)), NEG)
            e = jnp.exp(scores - jnp.max(scores, axis=-1, keepdims=True))
            total = jnp.sum(e, axis=-1, keepdims=True)
            heads.append((dot(e.astype(BF16), v2[:, cut]) / total).astype(BF16))
        lo = jnp.concatenate(heads, axis=1)

        @pl.when(c == 0)
        def _():
            loads[2].wait()

        for n in range(up.shape[1] // 256):
            cut = slice(n * 256, (n + 1) * 256)
            act[:, cut] = jax.nn.gelu(dot(normed, up[:, cut]), approximate=True).astype(BF16)

        @pl.when(c == 0)
        def _():
            loads[3].wait()
            loads[4].wait()
            loads[5].wait()

        mine = lax.broadcasted_iota(jnp.int32, (rows, 1), 0) // own == z
        a = act[...]
        for n in range(part.shape[1] // 256):
            cut = slice(n * 256, (n + 1) * 256)
            t = dot(lo, wo[:, cut]) + dot(a, down[:, cut])
            t = t + jnp.where(mine, xp[:, cut], 0.0)
            part[:, cut] = t
            tb = t.astype(BF16)
            for h in range(ZN):
                bsend[c, h, :, cut] = tb[h * own : (h + 1) * own]
        ownf[c] = part[pl.ds(pl.multiple_of(z * own, own), own), :]
        pp = dot(bsend[c].reshape(rows, part.shape[1]), ppw[...])
        ppf[...] = pp
        pb = pp.astype(BF16)
        gp = pp.shape[1]
        for h in range(ZN):
            for b in range(2):
                at = (2 * h + b) * span
                ppsend[c, h, :, b * gp : (b + 1) * gp] = pb[at : at + span]
        for b in range(2):
            at = pl.multiple_of(z * own + b * span, span)
            ppown[c, :, b * gp : (b + 1) * gp] = ppf[pl.ds(at, span), :]
        for d in (2, 1, 3):
            pp_copy(c, d).start()

        @pl.when(c >= 1)
        def _():
            finish_patches(c - 1)

        @pl.when(c < EARLY)
        def _():
            for d in (2, 1, 3):
                bulk_copy(c, d).start()

        return carry

    lax.fori_loop(0, CHUNKS, chunk, 0)
    finish_patches(CHUNKS - 1)
    for c in range(EARLY, CHUNKS):
        for d in (2, 1, 3):
            bulk_copy(c, d).start()

    loads[6].wait()
    for c in range(CHUNKS):
        for d in (1, 2, 3):
            ag_arrival(c, d).wait_recv()
    patches = CHUNKS * span
    piece = pin.shape[3]
    square = jnp.zeros((patches, 1), F32)
    for h in range(ZN):
        v = pin[h].reshape(patches, piece).astype(F32)
        square = square + jnp.sum(v * v, axis=-1, keepdims=True)
    inv = lax.rsqrt(square / (ZN * piece) + EPS)
    for h in range(ZN):
        cut = slice(h * piece, (h + 1) * piece)
        v = pin[h].reshape(patches, piece).astype(F32)
        gn[:, cut] = (v * inv * ggain_ref[:, cut]).astype(BF16)
    g = gn[...]

    def project(j):
        for half in range(2):
            r = dot(g, gqkv[j, :, half * 256 : (half + 1) * 256])
            for t in range(2):
                v = r[:, t * HD : (t + 1) * HD]
                if j < 2:
                    v = unit(v)
                qkvs[half * 2 + t, j] = v.astype(BF16)

    def xk_copy(d):
        h = lax.rem(x + d, XN)
        return remote(qkvs.at[h, pl.ds(1, 2)], kvbuf.at[y, core, x], xk_s.at[d - 1], xk_r.at[d - 1], xpeer(d))

    def xk_arrival(d):
        at = kvbuf.at[y, core, lax.rem(x + XN - d, XN)]
        return remote(at, at, xk_s.at[d - 1], xk_r.at[d - 1], xpeer(d))

    def xq_copy(d):
        h = lax.rem(x + d, XN)
        return remote(qkvs.at[h, 0], qbuf.at[x], xq_s.at[d - 1], xq_r.at[d - 1], xpeer(d))

    def xq_arrival(d):
        at = qbuf.at[lax.rem(x + XN - d, XN)]
        return remote(at, at, xq_s.at[d - 1], xq_r.at[d - 1], xpeer(d))

    project(1)
    project(2)
    for d in (2, 1, 3):
        xk_copy(d).start()
    kvbuf[y, core, x] = qkvs[x, 1:3]
    project(0)
    for d in (2, 1, 3):
        xq_copy(d).start()
    qbuf[x] = qkvs[x, 0]
    y1 = lax.rem(y + 1, YN)
    y2 = lax.rem(y + 2, YN)
    y3 = lax.rem(y + 3, YN)
    other = 1 - core
    low, high = pl.ds(0, 2), pl.ds(2, 2)

    def same(ref, ss, rs, peer):
        return remote(ref, ref, ss, rs, peer)

    own_up = same(kvbuf.at[y, core], y_s.at[0], y_r.at[0], y_up)
    own_down = same(kvbuf.at[y, core], y_s.at[1], y_r.at[1], y_down)
    relay_up = same(kvbuf.at[y3, core, low], y_s.at[2], y_r.at[2], y_up)
    relay_down = same(kvbuf.at[y1, core, high], y_s.at[3], y_r.at[3], y_down)
    from_down = same(kvbuf.at[y3, core], y_s.at[0], y_r.at[0], y_up)
    from_up = same(kvbuf.at[y1, core], y_s.at[1], y_r.at[1], y_down)
    far_low = same(kvbuf.at[y2, core, low], y_s.at[2], y_r.at[2], y_up)
    far_high = same(kvbuf.at[y2, core, high], y_s.at[3], y_r.at[3], y_down)
    give = [
        same(kvbuf.at[y, core], c_s.at[0], c_r.at[0], sibling),
        same(kvbuf.at[y3, core], c_s.at[1], c_r.at[1], sibling),
        same(kvbuf.at[y1, core], c_s.at[2], c_r.at[2], sibling),
        same(kvbuf.at[y2, core, low], c_s.at[3], c_r.at[3], sibling),
        same(kvbuf.at[y2, core, high], c_s.at[4], c_r.at[4], sibling),
    ]
    get = [
        same(kvbuf.at[y, other], c_s.at[0], c_r.at[0], sibling),
        same(kvbuf.at[y3, other], c_s.at[1], c_r.at[1], sibling),
        same(kvbuf.at[y1, other], c_s.at[2], c_r.at[2], sibling),
        same(kvbuf.at[y2, other, low], c_s.at[3], c_r.at[3], sibling),
        same(kvbuf.at[y2, other, high], c_s.at[4], c_r.at[4], sibling),
    ]

    for d in (1, 3, 2):
        xk_arrival(d).wait_recv()
    own_up.start()
    own_down.start()
    give[0].start()
    for d in (1, 3, 2):
        xq_arrival(d).wait_recv()

    m_ref[...] = jnp.full(m_ref.shape, NEG, F32)
    l_ref[...] = jnp.zeros(l_ref.shape, F32)
    acc[...] = jnp.zeros(acc.shape, F32)
    factor = gscale_ref[x] / math.sqrt(HD)
    keys = XN * patches

    def attend(yb, masked):
        def one(cb, qb):
            k = kvbuf[yb, cb, :, 0].reshape(keys, HD)
            v = kvbuf[yb, cb, :, 1].reshape(keys, HD)
            scores = dot_t(qbuf[qb], k)
            if masked:
                kk = lax.broadcasted_iota(jnp.int32, scores.shape, 1)
                qq = lax.broadcasted_iota(jnp.int32, scores.shape, 0)
                k_at = (2 * (kk // patches) + cb) * patches + lax.rem(kk, patches)
                q_at = (2 * qb + core) * patches + qq
                scores = jnp.where(k_at <= q_at, scores, NEG)
            old = m_ref[qb]
            new = jnp.maximum(old, jnp.max(scores, axis=-1, keepdims=True))
            keep = jnp.exp((old - new) * factor)
            e = jnp.exp((scores - new) * factor)
            m_ref[qb] = new
            l_ref[qb] = l_ref[qb] * keep + jnp.sum(e, axis=-1, keepdims=True)
            acc[qb] = acc[qb] * keep + dot(e.astype(BF16), v)

        return one

    def run(yb, cb, masked):
        one = attend(yb, masked)

        def body(qb, carry):
            one(cb, qb)
            return carry

        lax.fori_loop(0, XN, body, 0)

    def run_both(yb):
        one = attend(yb, False)

        def body(i, carry):
            one(i // XN, lax.rem(i, XN))
            return carry

        @pl.when(yb < y)
        def _():
            lax.fori_loop(0, 2 * XN, body, 0)

    run(y, core, True)
    get[0].wait_recv()
    from_down.wait_recv()
    relay_up.start()
    give[1].start()
    from_up.wait_recv()
    relay_down.start()
    give[2].start()
    run(y, other, True)
    get[1].wait_recv()
    run_both(y3)
    get[2].wait_recv()
    run_both(y1)
    far_low.wait_recv()
    give[3].start()
    far_high.wait_recv()
    give[4].start()
    get[3].wait_recv()
    get[4].wait_recv()
    run_both(y2)

    def o_copy(d):
        h = lax.rem(x + d, XN)
        return remote(osend.at[h], orecv.at[x], o_s.at[d - 1], o_r.at[d - 1], xpeer(d))

    def o_arrival(d):
        at = orecv.at[lax.rem(x + XN - d, XN)]
        return remote(at, at, o_s.at[d - 1], o_r.at[d - 1], xpeer(d))

    for qb in range(XN):
        osend[qb] = (acc[qb] / l_ref[qb]).astype(BF16)
    for d in (2, 1, 3):
        o_copy(d).start()
    orecv[x] = osend[x]
    loads[7].wait()
    for d in (1, 3, 2):
        o_arrival(d).wait_recv()
    gattn = jnp.concatenate([orecv[h] for h in range(XN)], axis=1)

    def out_part(zz):
        return dot(gattn, gout[:, pl.ds(pl.multiple_of(zz * piece, piece), piece)])

    def r_copy(d):
        return remote(rsend.at[d - 1], rrecv.at[d - 1], r_s.at[d - 1], r_r.at[d - 1], zpeer(d))

    for d in (2, 1, 3):
        rsend[d - 1] = out_part(lax.rem(z + d, ZN)).astype(BF16)
        r_copy(d).start()
    update = out_part(z)

    for c in range(CHUNKS):
        state = ownf[c]
        for d in (1, 2, 3):
            bulk_copy(c, d).wait_recv()
            state = state + brecv[c, d - 1].astype(F32)
        state = state.astype(BF16)
        for b in range(2):
            bst[b, c * span : (c + 1) * span] = state[b * span : (b + 1) * span]

    sources, blocks = owners_ref.shape
    spread = jnp.where(
        lax.broadcasted_iota(jnp.int32, (blocks, patches), 1) // 2
        == lax.broadcasted_iota(jnp.int32, (blocks, patches), 0),
        1.0,
        0.0,
    ).astype(BF16)
    listed = dot(owners_ref[...].astype(F32).astype(BF16), spread)
    is_mine = lax.broadcasted_iota(jnp.int32, listed.shape, 0) == s
    listed_row = jnp.sum(jnp.where(is_mine, listed, 0.0), axis=0, keepdims=True)
    pr = lax.broadcasted_iota(jnp.int32, (patches, patches), 0)
    pc = lax.broadcasted_iota(jnp.int32, (patches, patches), 1)
    listed_col = jnp.sum(jnp.where(pr == pc, listed_row, 0.0), axis=1, keepdims=True)
    earlier = (listed_col == listed_row) & (pr < pc) & (lax.rem(pr, 2) == lax.rem(pc, 2))
    rank = jnp.sum(jnp.where(earlier, 1.0, 0.0), axis=0, keepdims=True)
    slot = listed_row * 4.0 + rank * 2.0 + lax.rem(pc, 2).astype(F32)
    pick = jnp.where(slot == pr.astype(F32), 1.0, 0.0).astype(BF16)

    loads[8].wait()
    total = update + pin[z].reshape(patches, piece).astype(F32)
    for d in (1, 3, 2):
        r_copy(d).wait_recv()
        total = total + rrecv[d - 1].astype(F32)
    result = total.astype(BF16)
    perm_ref[...] = dot(pick, result).astype(BF16)
    gp = back.shape[0]
    for b in range(2):
        byte_ref[b] = (
            bst[b].astype(F32) + dot(result[:, b * gp : (b + 1) * gp], back[...])
        ).astype(BF16)

    def drain(c, carry):
        for d in (1, 2, 3):
            pp_copy(c, d).wait_send()
            ag_copy(c, d).wait_send()
            bulk_copy(c, d).wait_send()
        return carry

    lax.fori_loop(0, CHUNKS, drain, 0)
    for d in (1, 2, 3):
        xk_copy(d).wait_send()
        xq_copy(d).wait_send()
        o_copy(d).wait_send()
        r_copy(d).wait_send()
    for copy in (own_up, own_down, relay_up, relay_down, *give):
        copy.wait_send()


def on_device(
    byte_in, local_gain, local_qkv, local_out, mlp_up, mlp_down, local_scale, patch_proj,
    global_gain, global_qkv, global_out, global_scale, back_proj, owners,
):
    patches, span8, dl = byte_in.shape
    gw = global_out.shape[1]
    piece = gw // ZN
    ff = mlp_up.shape[1]
    rows = patches * span8 // CHUNKS
    span = patches // CHUNKS
    own = 2 * span
    gp = back_proj.shape[0]
    wqkv3 = jnp.transpose(local_qkv, (1, 0, 2))
    gqkv3 = jnp.transpose(global_qkv, (1, 0, 2))
    hbm = pl.BlockSpec(memory_space=pl.ANY)
    vm = pl.BlockSpec(memory_space=pltpu.VMEM)
    sm = pl.BlockSpec(memory_space=pltpu.SMEM)
    dma = pltpu.SemaphoreType.DMA

    def buf(*shape, dtype=BF16):
        return pltpu.VMEM(shape, dtype)

    big = [byte_in.reshape(patches * span8, dl), wqkv3, local_out, mlp_up, mlp_down, patch_proj, gqkv3, global_out, back_proj]
    scratch = [buf(*a.shape) for a in big] + [
        buf(rows, ff),
        buf(rows, dl, dtype=F32),
        buf(rows, gp, dtype=F32),
        buf(CHUNKS, ZN, own, dl),
        buf(CHUNKS, ZN - 1, own, dl),
        buf(CHUNKS, own, dl, dtype=F32),
        buf(CHUNKS, ZN, span, 2 * gp),
        buf(CHUNKS, ZN - 1, span, 2 * gp),
        buf(CHUNKS, span, 2 * gp, dtype=F32),
        buf(ZN, CHUNKS, span, piece),
        buf(patches, gw),
        buf(XN, 3, patches, HD),
        buf(YN, 2, XN, 2, patches, HD),
        buf(XN, patches, HD),
        buf(XN, patches, 1, dtype=F32),
        buf(XN, patches, 1, dtype=F32),
        buf(XN, patches, HD, dtype=F32),
        buf(XN, patches, HD),
        buf(XN, patches, HD),
        buf(ZN - 1, patches, piece),
        buf(ZN - 1, patches, piece),
        buf(2, patches, dl),
        dma((9,)),
    ]
    scratch += [dma((CHUNKS, 3))] * 6 + [dma((3,))] * 4 + [dma((4,))] * 2 + [dma((5,))] * 2 + [dma((3,))] * 4
    byte_out, permuted = pl.pallas_call(
        kernel,
        out_shape=(
            jax.ShapeDtypeStruct((2, patches, dl), BF16),
            jax.ShapeDtypeStruct((patches, piece), BF16),
        ),
        in_specs=[hbm] * 9 + [vm] * 3 + [sm] * 2,
        out_specs=(vm, vm),
        scratch_shapes=scratch,
        compiler_params=pltpu.CompilerParams(
            collective_id=0, has_side_effects=True, vmem_limit_bytes=60 * 1024 * 1024
        ),
    )(*big, local_gain.reshape(1, dl), global_gain.reshape(1, gw), owners, local_scale, global_scale)
    global_state = lax.all_to_all(permuted, "seq", split_axis=0, concat_axis=0, tiled=True)
    return (jnp.transpose(byte_out, (1, 0, 2)), global_state)


def solution(mesh):
    placed = (
        P("seq", None, None),
        P(),
        P(None, None, "head"),
        P("head", None),
        P(None, "head"),
        P("head", None),
        P("head"),
        P(),
        P(),
        P(None, None, "head"),
        P("head", None),
        P("head"),
        P(),
        P(),
    )
    return jax.shard_map(
        on_device,
        mesh=mesh,
        in_specs=placed,
        out_specs=(P("seq", "head", None), P("seq", "head")),
        check_vma=False,
    )
```

```python
import functools
import math

import jax
import jax.numpy as jnp
from jax import lax
from jax.experimental import pallas as pl
from jax.experimental.pallas import tpu as pltpu
from jax.sharding import PartitionSpec as P

EPS = 1e-06
NEG = -1e30
MESH = pl.DeviceIdType.MESH
F32 = jnp.float32
BF16 = jnp.bfloat16
XN = 4
YN = 4
ZN = 4
CHUNKS = 4
EARLY = 2
HD = 128


def dot(a, b):
    return jnp.dot(a, b, preferred_element_type=F32)


def dot_t(a, b):
    return lax.dot_general(a, b, (((1,), (1,)), ((), ())), preferred_element_type=F32)


def unit(v):
    return v * lax.rsqrt(jnp.mean(v * v, axis=-1, keepdims=True) + EPS)


def kernel(
    x_hbm, wqkv_hbm, wo_hbm, up_hbm, down_hbm, pp_hbm, gqkv_hbm, gout_hbm, back_hbm,
    gain_ref, ggain_ref, owners_ref, lscale_ref, gscale_ref,
    byte_ref, state_ref,
    xv, wqkv, wo, up, down, ppw, gqkv, gout, back,
    act, part, ppf, bsend, brecv, ownf, ppsend, pprecv, ppown, pin,
    gn, qkvs, kvbuf, qbuf, m_ref, l_ref, acc, osend, orecv, rsend, rrecv, bst, psend,
    lsem, pp_s, pp_r, ag_s, ag_r, bk_s, bk_r, xk_s, xk_r, xq_s, xq_r,
    y_s, y_r, c_s, c_r, o_s, o_r, r_s, r_r, p_s, p_r,
):
    s = lax.axis_index("seq")
    z = lax.axis_index("head")
    core = lax.rem(s, 2)
    x = lax.rem(s // 2, XN)
    y = s // (2 * XN)
    rows = xv.shape[0] // CHUNKS
    span = rows // 8
    own = 2 * span

    def seq_of(yy, xx, cc):
        return (yy * XN + xx) * 2 + cc

    def zpeer(d):
        return (s, lax.rem(z + d, ZN))

    def xpeer(d):
        return (seq_of(y, lax.rem(x + d, XN), core), z)

    y_up = (seq_of(lax.rem(y + 1, YN), x, core), z)
    y_down = (seq_of(lax.rem(y + YN - 1, YN), x, core), z)
    sibling = (seq_of(y, x, 1 - core), z)

    loads = [
        pltpu.make_async_copy(a, b, lsem.at[i])
        for i, (a, b) in enumerate(
            ((x_hbm, xv), (wqkv_hbm, wqkv), (up_hbm, up), (wo_hbm, wo), (down_hbm, down),
             (pp_hbm, ppw), (gqkv_hbm, gqkv), (gout_hbm, gout), (back_hbm, back))
        )
    ]
    for load in loads:
        load.start()

    barrier = pltpu.get_barrier_semaphore()
    plane = 2 * XN * YN

    def greet(peer):
        pl.semaphore_signal(barrier, inc=1, device_id=peer, device_id_type=MESH)

    def greet_plane(d, carry):
        greet((lax.rem(s + d, plane), z))
        return carry

    for d in (1, 2, 3):
        greet(zpeer(d))
    lax.fori_loop(1, plane, greet_plane, 0)
    pl.semaphore_wait(barrier, ZN - 1 + plane - 1)

    def remote(src, dst, ss, rs, peer):
        return pltpu.make_async_remote_copy(
            src_ref=src, dst_ref=dst, send_sem=ss, recv_sem=rs, device_id=peer, device_id_type=MESH
        )

    def pp_copy(c, d):
        return remote(
            ppsend.at[c, lax.rem(z + d, ZN)], pprecv.at[c, d - 1], pp_s.at[c, d - 1], pp_r.at[c, d - 1], zpeer(d)
        )

    def ag_copy(c, d):
        return remote(pin.at[z, c], pin.at[z, c], ag_s.at[c, d - 1], ag_r.at[c, d - 1], zpeer(d))

    def ag_arrival(c, d):
        piece = pin.at[lax.rem(z + ZN - d, ZN), c]
        return remote(piece, piece, ag_s.at[c, d - 1], ag_r.at[c, d - 1], zpeer(d))

    def bulk_copy(c, d):
        return remote(
            bsend.at[c, lax.rem(z + d, ZN)], brecv.at[c, d - 1], bk_s.at[c, d - 1], bk_r.at[c, d - 1], zpeer(d)
        )

    def finish_patches(c):
        total = ppown[c]
        for d in (1, 2, 3):
            pp_copy(c, d).wait_recv()
            total = total + pprecv[c, d - 1].astype(F32)
        pin[z, c] = total.astype(BF16)
        for d in (2, 1, 3):
            ag_copy(c, d).start()

    row_i = lax.broadcasted_iota(jnp.int32, (rows, rows), 0)
    col_i = lax.broadcasted_iota(jnp.int32, (rows, rows), 1)
    to_byte_major = jnp.where(
        col_i == lax.rem(row_i, span) * 8 + row_i // span, 1.0, 0.0
    ).astype(BF16)

    def chunk(c, carry):
        @pl.when(c == 0)
        def _():
            loads[0].wait()
            loads[1].wait()

        xp = dot(to_byte_major, xv[pl.ds(pl.multiple_of(c * rows, rows), rows), :])
        normed = (
            xp * lax.rsqrt(jnp.mean(xp * xp, axis=-1, keepdims=True) + EPS) * gain_ref[...]
        ).astype(BF16)
        q2 = dot(normed, wqkv[0])
        k2 = dot(normed, wqkv[1])
        v2 = dot(normed, wqkv[2]).astype(BF16)
        rr = lax.broadcasted_iota(jnp.int32, (rows, rows), 0)
        cc = lax.broadcasted_iota(jnp.int32, (rows, rows), 1)
        seen = (lax.rem(rr, span) == lax.rem(cc, span)) & (cc // span <= rr // span)
        heads = []
        for h in range(2):
            cut = slice(h * HD, (h + 1) * HD)
            scores = dot_t(unit(q2[:, cut]).astype(BF16), unit(k2[:, cut]).astype(BF16))
            scores = jnp.where(seen, scores * (lscale_ref[h] / math.sqrt(HD)), NEG)
            e = jnp.exp(scores - jnp.max(scores, axis=-1, keepdims=True))
            total = jnp.sum(e, axis=-1, keepdims=True)
            heads.append((dot(e.astype(BF16), v2[:, cut]) / total).astype(BF16))
        lo = jnp.concatenate(heads, axis=1)

        @pl.when(c == 0)
        def _():
            loads[2].wait()

        for n in range(up.shape[1] // 256):
            cut = slice(n * 256, (n + 1) * 256)
            act[:, cut] = jax.nn.gelu(dot(normed, up[:, cut]), approximate=True).astype(BF16)

        @pl.when(c == 0)
        def _():
            loads[3].wait()
            loads[4].wait()
            loads[5].wait()

        mine = lax.broadcasted_iota(jnp.int32, (rows, 1), 0) // own == z
        a = act[...]
        for n in range(part.shape[1] // 256):
            cut = slice(n * 256, (n + 1) * 256)
            t = dot(lo, wo[:, cut]) + dot(a, down[:, cut])
            t = t + jnp.where(mine, xp[:, cut], 0.0)
            part[:, cut] = t
            tb = t.astype(BF16)
            for h in range(ZN):
                bsend[c, h, :, cut] = tb[h * own : (h + 1) * own]
        ownf[c] = part[pl.ds(pl.multiple_of(z * own, own), own), :]
        pp = dot(bsend[c].reshape(rows, part.shape[1]), ppw[...])
        ppf[...] = pp
        pb = pp.astype(BF16)
        gp = pp.shape[1]
        for h in range(ZN):
            for b in range(2):
                at = (2 * h + b) * span
                ppsend[c, h, :, b * gp : (b + 1) * gp] = pb[at : at + span]
        for b in range(2):
            at = pl.multiple_of(z * own + b * span, span)
            ppown[c, :, b * gp : (b + 1) * gp] = ppf[pl.ds(at, span), :]
        for d in (2, 1, 3):
            pp_copy(c, d).start()

        @pl.when(c >= 1)
        def _():
            finish_patches(c - 1)

        @pl.when(c < EARLY)
        def _():
            for d in (2, 1, 3):
                bulk_copy(c, d).start()

        return carry

    lax.fori_loop(0, CHUNKS, chunk, 0)
    finish_patches(CHUNKS - 1)
    for c in range(EARLY, CHUNKS):
        for d in (2, 1, 3):
            bulk_copy(c, d).start()

    loads[6].wait()
    for c in range(CHUNKS):
        for d in (1, 2, 3):
            ag_arrival(c, d).wait_recv()
    patches = CHUNKS * span
    piece = pin.shape[3]
    square = jnp.zeros((patches, 1), F32)
    for h in range(ZN):
        v = pin[h].reshape(patches, piece).astype(F32)
        square = square + jnp.sum(v * v, axis=-1, keepdims=True)
    inv = lax.rsqrt(square / (ZN * piece) + EPS)
    for h in range(ZN):
        cut = slice(h * piece, (h + 1) * piece)
        v = pin[h].reshape(patches, piece).astype(F32)
        gn[:, cut] = (v * inv * ggain_ref[:, cut]).astype(BF16)
    g = gn[...]

    def project(j):
        for half in range(2):
            r = dot(g, gqkv[j, :, half * 256 : (half + 1) * 256])
            for t in range(2):
                v = r[:, t * HD : (t + 1) * HD]
                if j < 2:
                    v = unit(v)
                qkvs[half * 2 + t, j] = v.astype(BF16)

    def xk_copy(d):
        h = lax.rem(x + d, XN)
        return remote(qkvs.at[h, pl.ds(1, 2)], kvbuf.at[y, core, x], xk_s.at[d - 1], xk_r.at[d - 1], xpeer(d))

    def xk_arrival(d):
        at = kvbuf.at[y, core, lax.rem(x + XN - d, XN)]
        return remote(at, at, xk_s.at[d - 1], xk_r.at[d - 1], xpeer(d))

    def xq_copy(d):
        h = lax.rem(x + d, XN)
        return remote(qkvs.at[h, 0], qbuf.at[x], xq_s.at[d - 1], xq_r.at[d - 1], xpeer(d))

    def xq_arrival(d):
        at = qbuf.at[lax.rem(x + XN - d, XN)]
        return remote(at, at, xq_s.at[d - 1], xq_r.at[d - 1], xpeer(d))

    project(1)
    project(2)
    for d in (2, 1, 3):
        xk_copy(d).start()
    kvbuf[y, core, x] = qkvs[x, 1:3]
    project(0)
    for d in (2, 1, 3):
        xq_copy(d).start()
    qbuf[x] = qkvs[x, 0]
    y1 = lax.rem(y + 1, YN)
    y2 = lax.rem(y + 2, YN)
    y3 = lax.rem(y + 3, YN)
    other = 1 - core
    low, high = pl.ds(0, 2), pl.ds(2, 2)

    def same(ref, ss, rs, peer):
        return remote(ref, ref, ss, rs, peer)

    own_up = same(kvbuf.at[y, core], y_s.at[0], y_r.at[0], y_up)
    own_down = same(kvbuf.at[y, core], y_s.at[1], y_r.at[1], y_down)
    relay_up = same(kvbuf.at[y3, core, low], y_s.at[2], y_r.at[2], y_up)
    relay_down = same(kvbuf.at[y1, core, high], y_s.at[3], y_r.at[3], y_down)
    from_down = same(kvbuf.at[y3, core], y_s.at[0], y_r.at[0], y_up)
    from_up = same(kvbuf.at[y1, core], y_s.at[1], y_r.at[1], y_down)
    far_low = same(kvbuf.at[y2, core, low], y_s.at[2], y_r.at[2], y_up)
    far_high = same(kvbuf.at[y2, core, high], y_s.at[3], y_r.at[3], y_down)
    give = [
        same(kvbuf.at[y, core], c_s.at[0], c_r.at[0], sibling),
        same(kvbuf.at[y3, core], c_s.at[1], c_r.at[1], sibling),
        same(kvbuf.at[y1, core], c_s.at[2], c_r.at[2], sibling),
        same(kvbuf.at[y2, core, low], c_s.at[3], c_r.at[3], sibling),
        same(kvbuf.at[y2, core, high], c_s.at[4], c_r.at[4], sibling),
    ]
    get = [
        same(kvbuf.at[y, other], c_s.at[0], c_r.at[0], sibling),
        same(kvbuf.at[y3, other], c_s.at[1], c_r.at[1], sibling),
        same(kvbuf.at[y1, other], c_s.at[2], c_r.at[2], sibling),
        same(kvbuf.at[y2, other, low], c_s.at[3], c_r.at[3], sibling),
        same(kvbuf.at[y2, other, high], c_s.at[4], c_r.at[4], sibling),
    ]

    for d in (1, 3, 2):
        xk_arrival(d).wait_recv()
    own_up.start()
    own_down.start()
    give[0].start()
    for d in (1, 3, 2):
        xq_arrival(d).wait_recv()

    m_ref[...] = jnp.full(m_ref.shape, NEG, F32)
    l_ref[...] = jnp.zeros(l_ref.shape, F32)
    acc[...] = jnp.zeros(acc.shape, F32)
    factor = gscale_ref[x] / math.sqrt(HD)
    keys = XN * patches

    def attend(yb, masked):
        def one(cb, qb):
            k = kvbuf[yb, cb, :, 0].reshape(keys, HD)
            v = kvbuf[yb, cb, :, 1].reshape(keys, HD)
            scores = dot_t(qbuf[qb], k)
            if masked:
                kk = lax.broadcasted_iota(jnp.int32, scores.shape, 1)
                qq = lax.broadcasted_iota(jnp.int32, scores.shape, 0)
                k_at = (2 * (kk // patches) + cb) * patches + lax.rem(kk, patches)
                q_at = (2 * qb + core) * patches + qq
                scores = jnp.where(k_at <= q_at, scores, NEG)
            old = m_ref[qb]
            new = jnp.maximum(old, jnp.max(scores, axis=-1, keepdims=True))
            keep = jnp.exp((old - new) * factor)
            e = jnp.exp((scores - new) * factor)
            m_ref[qb] = new
            l_ref[qb] = l_ref[qb] * keep + jnp.sum(e, axis=-1, keepdims=True)
            acc[qb] = acc[qb] * keep + dot(e.astype(BF16), v)

        return one

    def run(yb, cb, masked):
        one = attend(yb, masked)

        def body(qb, carry):
            one(cb, qb)
            return carry

        lax.fori_loop(0, XN, body, 0)

    def run_both(yb):
        one = attend(yb, False)

        def body(i, carry):
            one(i // XN, lax.rem(i, XN))
            return carry

        @pl.when(yb < y)
        def _():
            lax.fori_loop(0, 2 * XN, body, 0)

    run(y, core, True)
    get[0].wait_recv()
    from_down.wait_recv()
    relay_up.start()
    give[1].start()
    from_up.wait_recv()
    relay_down.start()
    give[2].start()
    run(y, other, True)
    get[1].wait_recv()
    run_both(y3)
    get[2].wait_recv()
    run_both(y1)
    far_low.wait_recv()
    give[3].start()
    far_high.wait_recv()
    give[4].start()
    get[3].wait_recv()
    get[4].wait_recv()
    run_both(y2)

    def o_copy(d):
        h = lax.rem(x + d, XN)
        return remote(osend.at[h], orecv.at[x], o_s.at[d - 1], o_r.at[d - 1], xpeer(d))

    def o_arrival(d):
        at = orecv.at[lax.rem(x + XN - d, XN)]
        return remote(at, at, o_s.at[d - 1], o_r.at[d - 1], xpeer(d))

    for qb in range(XN):
        osend[qb] = (acc[qb] / l_ref[qb]).astype(BF16)
    for d in (2, 1, 3):
        o_copy(d).start()
    orecv[x] = osend[x]
    loads[7].wait()
    for d in (1, 3, 2):
        o_arrival(d).wait_recv()
    gattn = jnp.concatenate([orecv[h] for h in range(XN)], axis=1)

    def out_part(zz):
        return dot(gattn, gout[:, pl.ds(pl.multiple_of(zz * piece, piece), piece)])

    def r_copy(d):
        return remote(rsend.at[d - 1], rrecv.at[d - 1], r_s.at[d - 1], r_r.at[d - 1], zpeer(d))

    for d in (2, 1, 3):
        rsend[d - 1] = out_part(lax.rem(z + d, ZN)).astype(BF16)
        r_copy(d).start()
    update = out_part(z)

    ri = lax.broadcasted_iota(jnp.int32, (own, own), 0)
    ci = lax.broadcasted_iota(jnp.int32, (own, own), 1)
    to_patch_major = jnp.where(ci == lax.rem(ri, 2) * span + ri // 2, 1.0, 0.0).astype(BF16)
    for c in range(CHUNKS):
        state = ownf[c]
        for d in (1, 2, 3):
            bulk_copy(c, d).wait_recv()
            state = state + brecv[c, d - 1].astype(F32)
        bst[c * own : (c + 1) * own] = dot(to_patch_major, state.astype(BF16)).astype(BF16)

    sources, blocks = owners_ref.shape
    spread = jnp.where(
        lax.broadcasted_iota(jnp.int32, (blocks, patches), 1) // 2
        == lax.broadcasted_iota(jnp.int32, (blocks, patches), 0),
        1.0,
        0.0,
    ).astype(BF16)
    listed = dot(owners_ref[...].astype(F32).astype(BF16), spread)
    is_mine = lax.broadcasted_iota(jnp.int32, listed.shape, 0) == s
    listed_row = jnp.sum(jnp.where(is_mine, listed, 0.0), axis=0, keepdims=True)
    pr = lax.broadcasted_iota(jnp.int32, (patches, patches), 0)
    pc = lax.broadcasted_iota(jnp.int32, (patches, patches), 1)
    listed_col = jnp.sum(jnp.where(pr == pc, listed_row, 0.0), axis=1, keepdims=True)
    earlier = (listed_col == listed_row) & (pr < pc) & (lax.rem(pr, 2) == lax.rem(pc, 2))
    rank = jnp.sum(jnp.where(earlier, 1.0, 0.0), axis=0, keepdims=True)
    slot = listed_row * 4.0 + rank * 2.0 + lax.rem(pc, 2).astype(F32)
    pick = jnp.where(slot == pr.astype(F32), 1.0, 0.0).astype(BF16)

    per = patches // plane
    loads[8].wait()
    total = update + pin[z].reshape(patches, piece).astype(F32)
    for d in (1, 3, 2):
        r_copy(d).wait_recv()
        total = total + rrecv[d - 1].astype(F32)
    result = total.astype(BF16)
    sorted_rows = dot(pick, result)
    for o in range(plane):
        psend[o] = sorted_rows[o * per : (o + 1) * per].astype(BF16)

    def p_copy(d):
        return remote(
            psend.at[lax.rem(s + d, plane)], state_ref.at[s], p_s.at[d - 1], p_r.at[d - 1], (lax.rem(s + d, plane), z)
        )

    def p_start(d, carry):
        p_copy(d).start()
        return carry

    lax.fori_loop(1, plane, p_start, 0)
    state_ref[s] = psend[s]
    gp = back.shape[0]
    re = lax.broadcasted_iota(jnp.int32, (2 * patches, patches), 0)
    ce = lax.broadcasted_iota(jnp.int32, (2 * patches, patches), 1)
    shares = jnp.zeros((2 * patches, gp), F32)
    for b in range(2):
        lift = jnp.where(re == 2 * ce + b, 1.0, 0.0).astype(BF16)
        shares = shares + dot(lift, result[:, b * gp : (b + 1) * gp])
    shares = shares.astype(BF16)
    for n in range(bst.shape[1] // 256):
        cut = slice(n * 256, (n + 1) * 256)
        byte_ref[:, cut] = (bst[:, cut].astype(F32) + dot(shares, back[:, cut])).astype(BF16)

    def p_wait(d, carry):
        at = state_ref.at[lax.rem(s + plane - d, plane)]
        remote(at, at, p_s.at[d - 1], p_r.at[d - 1], (lax.rem(s + d, plane), z)).wait_recv()
        p_copy(d).wait_send()
        return carry

    lax.fori_loop(1, plane, p_wait, 0)

    def drain(c, carry):
        for d in (1, 2, 3):
            pp_copy(c, d).wait_send()
            ag_copy(c, d).wait_send()
            bulk_copy(c, d).wait_send()
        return carry

    lax.fori_loop(0, CHUNKS, drain, 0)
    for d in (1, 2, 3):
        xk_copy(d).wait_send()
        xq_copy(d).wait_send()
        o_copy(d).wait_send()
        r_copy(d).wait_send()
    for copy in (own_up, own_down, relay_up, relay_down, *give):
        copy.wait_send()


def on_device(
    byte_in, local_gain, local_qkv, local_out, mlp_up, mlp_down, local_scale, patch_proj,
    global_gain, global_qkv, global_out, global_scale, back_proj, owners,
):
    patches, span8, dl = byte_in.shape
    gw = global_out.shape[1]
    piece = gw // ZN
    ff = mlp_up.shape[1]
    rows = patches * span8 // CHUNKS
    span = patches // CHUNKS
    own = 2 * span
    gp = back_proj.shape[0]
    plane = 2 * XN * YN
    wqkv3 = jnp.transpose(local_qkv, (1, 0, 2))
    gqkv3 = jnp.transpose(global_qkv, (1, 0, 2))
    hbm = pl.BlockSpec(memory_space=pl.ANY)
    vm = pl.BlockSpec(memory_space=pltpu.VMEM)
    sm = pl.BlockSpec(memory_space=pltpu.SMEM)
    dma = pltpu.SemaphoreType.DMA

    def buf(*shape, dtype=BF16):
        return pltpu.VMEM(shape, dtype)

    big = [byte_in.reshape(patches * span8, dl), wqkv3, local_out, mlp_up, mlp_down, patch_proj, gqkv3, global_out, back_proj]
    scratch = [buf(*a.shape) for a in big] + [
        buf(rows, ff),
        buf(rows, dl, dtype=F32),
        buf(rows, gp, dtype=F32),
        buf(CHUNKS, ZN, own, dl),
        buf(CHUNKS, ZN - 1, own, dl),
        buf(CHUNKS, own, dl, dtype=F32),
        buf(CHUNKS, ZN, span, 2 * gp),
        buf(CHUNKS, ZN - 1, span, 2 * gp),
        buf(CHUNKS, span, 2 * gp, dtype=F32),
        buf(ZN, CHUNKS, span, piece),
        buf(patches, gw),
        buf(XN, 3, patches, HD),
        buf(YN, 2, XN, 2, patches, HD),
        buf(XN, patches, HD),
        buf(XN, patches, 1, dtype=F32),
        buf(XN, patches, 1, dtype=F32),
        buf(XN, patches, HD, dtype=F32),
        buf(XN, patches, HD),
        buf(XN, patches, HD),
        buf(ZN - 1, patches, piece),
        buf(ZN - 1, patches, piece),
        buf(2 * patches, dl),
        buf(plane, patches // plane, piece),
        dma((9,)),
    ]
    scratch += [dma((CHUNKS, 3))] * 6 + [dma((3,))] * 4 + [dma((4,))] * 2 + [dma((5,))] * 2 + [dma((3,))] * 4 + [dma((plane - 1,))] * 2
    byte_out, global_state = pl.pallas_call(
        kernel,
        out_shape=(
            jax.ShapeDtypeStruct((2 * patches, dl), BF16),
            jax.ShapeDtypeStruct((plane, patches // plane, piece), BF16),
        ),
        in_specs=[hbm] * 9 + [vm] * 3 + [sm] * 2,
        out_specs=(vm, vm),
        scratch_shapes=scratch,
        compiler_params=pltpu.CompilerParams(
            collective_id=0, has_side_effects=True, vmem_limit_bytes=60 * 1024 * 1024
        ),
    )(*big, local_gain.reshape(1, dl), global_gain.reshape(1, gw), owners, local_scale, global_scale)
    return (byte_out.reshape(patches, 2, dl), global_state.reshape(patches, piece))


def solution(mesh):
    placed = (
        P("seq", None, None),
        P(),
        P(None, None, "head"),
        P("head", None),
        P(None, "head"),
        P("head", None),
        P("head"),
        P(),
        P(),
        P(None, None, "head"),
        P("head", None),
        P("head"),
        P(),
        P(),
    )
    return jax.shard_map(
        on_device,
        mesh=mesh,
        in_specs=placed,
        out_specs=(P("seq", "head", None), P("seq", "head")),
        check_vma=False,
    )
```

```python
import functools
import math

import jax
import jax.numpy as jnp
from jax import lax
from jax.experimental import pallas as pl
from jax.experimental.pallas import tpu as pltpu
from jax.sharding import PartitionSpec as P

EPS = 1e-06
NEG = -1e30
MESH = pl.DeviceIdType.MESH
F32 = jnp.float32
BF16 = jnp.bfloat16
XN = 4
YN = 4
ZN = 4
CHUNKS = 4
HD = 128


def dot(a, b):
    return jnp.dot(a, b, preferred_element_type=F32)


def dot_t(a, b):
    return lax.dot_general(a, b, (((1,), (1,)), ((), ())), preferred_element_type=F32)


def unit(v):
    return v * lax.rsqrt(jnp.mean(v * v, axis=-1, keepdims=True) + EPS)


def kernel(
    x_hbm, wqkv_hbm, wo_hbm, up_hbm, down_hbm, pp_hbm, gqkv_hbm, gout_hbm, back_hbm,
    gain_ref, ggain_ref, owners_ref, lscale_ref, gscale_ref,
    byte_ref, state_ref,
    xv, wqkv, wo, up, down, ppw, gqkv, gout, back,
    act, part, ppf, bsend, bfar, brecv, ownf, ppsend, pprecv, ppown, pin,
    gn, qkvs, kvbuf, qbuf, m_ref, l_ref, acc, opart, oget, stpart, stget, osend, orecv, rfs, rfar, rsend, rrecv, bst, psend,
    lsem, pp_s, pp_r, ag_s, ag_r, bf_s, bf_r, bk_s, bk_r, xk_s, xk_r, xq_s, xq_r,
    yu_s, yu_r, yd_s, yd_r, ru_s, ru_r, rd_s, rd_r, c_s, c_r, o_s, o_r, rf_s, rf_r, r_s, r_r, p_s, p_r,
):
    s = lax.axis_index("seq")
    z = lax.axis_index("head")
    core = lax.rem(s, 2)
    x = lax.rem(s // 2, XN)
    y = s // (2 * XN)
    rows = xv.shape[0] // CHUNKS
    span = rows // 8
    own = 2 * span

    def seq_of(yy, xx, cc):
        return (yy * XN + xx) * 2 + cc

    def zpeer(d):
        return (s, lax.rem(z + d, ZN))

    def xpeer(d):
        return (seq_of(y, lax.rem(x + d, XN), core), z)

    y_up = (seq_of(lax.rem(y + 1, YN), x, core), z)
    y_down = (seq_of(lax.rem(y + YN - 1, YN), x, core), z)
    sibling = (seq_of(y, x, 1 - core), z)

    loads = [
        pltpu.make_async_copy(a, b, lsem.at[i])
        for i, (a, b) in enumerate(
            ((x_hbm, xv), (wqkv_hbm, wqkv), (up_hbm, up), (wo_hbm, wo), (down_hbm, down),
             (pp_hbm, ppw), (gqkv_hbm, gqkv), (gout_hbm, gout), (back_hbm, back))
        )
    ]
    for load in loads:
        load.start()

    barrier = pltpu.get_barrier_semaphore()
    plane = 2 * XN * YN

    def greet(peer):
        pl.semaphore_signal(barrier, inc=1, device_id=peer, device_id_type=MESH)

    def greet_plane(d, carry):
        greet((lax.rem(s + d, plane), z))
        return carry

    for d in (1, 2, 3):
        greet(zpeer(d))
    lax.fori_loop(1, plane, greet_plane, 0)

    def remote(src, dst, ss, rs, peer):
        return pltpu.make_async_remote_copy(
            src_ref=src, dst_ref=dst, send_sem=ss, recv_sem=rs, device_id=peer, device_id_type=MESH
        )

    def pp_copy(c, d):
        return remote(
            ppsend.at[c, lax.rem(z + d, ZN)], pprecv.at[c, d - 1], pp_s.at[c, d - 1], pp_r.at[c, d - 1], zpeer(d)
        )

    def ag_copy(c, d):
        return remote(pin.at[z, c], pin.at[z, c], ag_s.at[c, d - 1], ag_r.at[c, d - 1], zpeer(d))

    def ag_arrival(c, d):
        piece = pin.at[lax.rem(z + ZN - d, ZN), c]
        return remote(piece, piece, ag_s.at[c, d - 1], ag_r.at[c, d - 1], zpeer(d))

    z_up = zpeer(1)
    z_down = zpeer(ZN - 1)
    up_at = lax.rem(z + 1, ZN)
    down_at = lax.rem(z + ZN - 1, ZN)
    far_at = lax.rem(z + 2, ZN)

    def bulk_far(c):
        return (
            remote(bsend.at[c, far_at, 0], bfar.at[c, 0], bf_s.at[c, 0], bf_r.at[c, 0], z_up),
            remote(bsend.at[c, far_at, 1], bfar.at[c, 1], bf_s.at[c, 1], bf_r.at[c, 1], z_down),
        )

    def bulk_up(c, b):
        return remote(bsend.at[c, up_at, b], brecv.at[c, 0, b], bk_s.at[c, b], bk_r.at[c, b], z_up)

    def bulk_down(c, b):
        return remote(bsend.at[c, down_at, b], brecv.at[c, 1, b], bk_s.at[c, 2 + b], bk_r.at[c, 2 + b], z_down)

    def bulk_combine(c, carry):
        far_up, far_down = bulk_far(c)
        far_up.wait_recv()
        bsend[c, up_at, 0] = (bsend[c, up_at, 0].astype(F32) + bfar[c, 0].astype(F32)).astype(BF16)
        bulk_up(c, 0).start()
        far_down.wait_recv()
        bsend[c, down_at, 1] = (bsend[c, down_at, 1].astype(F32) + bfar[c, 1].astype(F32)).astype(BF16)
        bulk_down(c, 1).start()
        return carry

    def finish_patches(c):
        total = ppown[c]
        for d in (1, 2, 3):
            pp_copy(c, d).wait_recv()
            total = total + pprecv[c, d - 1].astype(F32)
        pin[z, c] = total.astype(BF16)
        for d in (2, 1, 3):
            ag_copy(c, d).start()

    loads[0].wait()
    loads[1].wait()
    row_i = lax.broadcasted_iota(jnp.int32, (rows, rows), 0)
    col_i = lax.broadcasted_iota(jnp.int32, (rows, rows), 1)
    to_byte_major = jnp.where(
        col_i == lax.rem(row_i, span) * 8 + row_i // span, 1.0, 0.0
    ).astype(BF16)

    def chunk(c, carry):
        xp = dot(to_byte_major, xv[pl.ds(pl.multiple_of(c * rows, rows), rows), :])
        normed = (
            xp * lax.rsqrt(jnp.mean(xp * xp, axis=-1, keepdims=True) + EPS) * gain_ref[...]
        ).astype(BF16)
        q2 = dot(normed, wqkv[0])
        k2 = dot(normed, wqkv[1])
        v2 = dot(normed, wqkv[2]).astype(BF16)

        @pl.when(c == 0)
        def _():
            for load in loads[2:6]:
                load.wait()

        rr = lax.broadcasted_iota(jnp.int32, (rows, rows), 0)
        cc = lax.broadcasted_iota(jnp.int32, (rows, rows), 1)
        seen = (lax.rem(rr, span) == lax.rem(cc, span)) & (cc // span <= rr // span)
        heads = []
        for h in range(2):
            cut = slice(h * HD, (h + 1) * HD)
            scores = dot_t(unit(q2[:, cut]).astype(BF16), unit(k2[:, cut]).astype(BF16))
            scores = jnp.where(seen, scores * (lscale_ref[h] / math.sqrt(HD)), NEG)
            e = jnp.exp(scores - jnp.max(scores, axis=-1, keepdims=True))
            total = jnp.sum(e, axis=-1, keepdims=True)
            heads.append((dot(e.astype(BF16), v2[:, cut]) / total).astype(BF16))
        lo = jnp.concatenate(heads, axis=1)

        for n in range(up.shape[1] // 256):
            cut = slice(n * 256, (n + 1) * 256)
            act[:, cut] = jax.nn.gelu(dot(normed, up[:, cut]), approximate=True).astype(BF16)

        mine = lax.broadcasted_iota(jnp.int32, (rows, 1), 0) // own == z
        a = act[...]
        for n in range(part.shape[1] // 256):
            cut = slice(n * 256, (n + 1) * 256)
            t = dot(lo, wo[:, cut]) + dot(a, down[:, cut])
            t = t + jnp.where(mine, xp[:, cut], 0.0)
            part[:, cut] = t
            tb = t.astype(BF16)
            for h in range(ZN):
                for b in range(2):
                    at = h * own + b * span
                    bsend[c, h, b, :, cut] = tb[at : at + span]
        ownf[c] = part[pl.ds(pl.multiple_of(z * own, own), own), :]
        pp = dot(bsend[c].reshape(rows, part.shape[1]), ppw[...])
        ppf[...] = pp
        pb = pp.astype(BF16)
        gp = pp.shape[1]
        for h in range(ZN):
            for b in range(2):
                at = (2 * h + b) * span
                ppsend[c, h, :, b * gp : (b + 1) * gp] = pb[at : at + span]
        for b in range(2):
            at = pl.multiple_of(z * own + b * span, span)
            ppown[c, :, b * gp : (b + 1) * gp] = ppf[pl.ds(at, span), :]

        @pl.when(c == 0)
        def _():
            pl.semaphore_wait(barrier, ZN - 1 + plane - 1)

        for d in (2, 1, 3):
            pp_copy(c, d).start()

        @pl.when(c >= 1)
        def _():
            finish_patches(c - 1)

        return carry

    lax.fori_loop(0, CHUNKS, chunk, 0)
    finish_patches(CHUNKS - 1)
    loads[6].wait()
    for c in range(CHUNKS):
        for d in (1, 2, 3):
            ag_arrival(c, d).wait_recv()
    for c in range(CHUNKS):
        for copy in bulk_far(c):
            copy.start()
    for c in range(CHUNKS):
        bulk_up(c, 1).start()
        bulk_down(c, 0).start()
    patches = CHUNKS * span
    piece = pin.shape[3]
    square = jnp.zeros((patches, 1), F32)
    for h in range(ZN):
        v = pin[h].reshape(patches, piece).astype(F32)
        square = square + jnp.sum(v * v, axis=-1, keepdims=True)
    inv = lax.rsqrt(square / (ZN * piece) + EPS)
    for h in range(ZN):
        cut = slice(h * piece, (h + 1) * piece)
        v = pin[h].reshape(patches, piece).astype(F32)
        gn[:, cut] = (v * inv * ggain_ref[:, cut]).astype(BF16)
    g = gn[...]

    def project(j):
        for half in range(2):
            r = dot(g, gqkv[j, :, half * 256 : (half + 1) * 256])
            for t in range(2):
                v = r[:, t * HD : (t + 1) * HD]
                if j < 2:
                    v = unit(v)
                if j == 2:
                    v = jnp.transpose(v)
                qkvs[half * 2 + t, j] = v.astype(BF16)

    def xk_copy(d):
        h = lax.rem(x + d, XN)
        return remote(qkvs.at[h, pl.ds(1, 2)], kvbuf.at[y, x], xk_s.at[d - 1], xk_r.at[d - 1], xpeer(d))

    def src(d):
        return lax.rem(x + XN - d, XN)

    def xk_arrival(d):
        at = kvbuf.at[y, src(d)]
        return remote(at, at, xk_s.at[d - 1], xk_r.at[d - 1], xpeer(d))

    def xq_copy(d):
        h = lax.rem(x + d, XN)
        return remote(qkvs.at[h, 0], qbuf.at[0, x], xq_s.at[d - 1], xq_r.at[d - 1], xpeer(d))

    def xq_arrival(d):
        at = qbuf.at[0, src(d)]
        return remote(at, at, xq_s.at[d - 1], xq_r.at[d - 1], xpeer(d))

    y1 = lax.rem(y + 1, YN)
    y2 = lax.rem(y + 2, YN)
    y3 = lax.rem(y + 3, YN)

    def up_copy(row, d, ss, rs):
        at = kvbuf.at[row, src(d)]
        return remote(at, at, ss.at[d], rs.at[d], y_up)

    def down_copy(row, d, ss, rs):
        at = kvbuf.at[row, src(d)]
        return remote(at, at, ss.at[d], rs.at[d], y_down)

    last = YN - 1
    inner = (y >= 1) & (y < last)
    outer = (y == 0) | (y == last)

    def spread_piece(d, act_on):
        @pl.when(y < last)
        def _():
            act_on(up_copy(y, d, yu_s, yu_r))

        @pl.when((y == 0) | ((y == 1) & (d % 2 == 1)))
        def _():
            act_on(down_copy(y, d, yd_s, yd_r))

    def start(copy):
        copy.start()

    def sent(copy):
        copy.wait_send()

    def take_down(d):
        @pl.when(y >= 1)
        def _():
            up_copy(y3, d, yu_s, yu_r).wait_recv()

        if d % 2 == 0:

            @pl.when(inner)
            def _():
                up_copy(y3, d, ru_s, ru_r).start()

    def take_up(d):
        @pl.when((y == last) | ((y == 0) & (d % 2 == 1)))
        def _():
            down_copy(y1, d, yd_s, yd_r).wait_recv()

        if d % 2 == 1:

            @pl.when(outer)
            def _():
                down_copy(y1, d, rd_s, rd_r).start()

    def take_far():
        @pl.when(y >= 2)
        def _():
            for d in (0, 2):
                up_copy(y2, d, ru_s, ru_r).wait_recv()
            for d in (1, 3):
                down_copy(y2, d, rd_s, rd_r).wait_recv()

    q_give = remote(qbuf.at[0], qbuf.at[1], c_s.at[0], c_r.at[0], sibling)
    o_give = remote(opart, oget, c_s.at[1], c_r.at[1], sibling)
    st_give = remote(stpart, stget, c_s.at[2], c_r.at[2], sibling)

    project(1)
    project(2)
    for d in (2, 1, 3):
        xk_copy(d).start()
    kvbuf[y, x] = qkvs[x, 1:3]
    spread_piece(0, start)
    project(0)
    for d in (2, 1, 3):
        xq_copy(d).start()
    qbuf[0, x] = qkvs[x, 0]
    m_ref[...] = jnp.full(m_ref.shape, NEG, F32)
    l_ref[...] = jnp.zeros(l_ref.shape, F32)
    acc[...] = jnp.zeros(acc.shape, F32)
    factor = gscale_ref[x] * (math.log2(math.e) / math.sqrt(HD))

    for d in (1, 3, 2):
        xk_arrival(d).wait_recv()
        spread_piece(d, start)
    for d in (1, 3, 2):
        xq_arrival(d).wait_recv()
    q_give.start()

    half_q = XN * patches // 2

    def attend(yb, rel, masked):
        queries = qbuf[rel].reshape(XN * patches, HD)
        for part_q in range(2):
            cut = slice(part_q * half_q, (part_q + 1) * half_q)
            wide = (part_q + 1) * XN // 2 if masked else XN
            k = kvbuf[yb, 0:wide, 0].reshape(wide * patches, HD)
            vt = jnp.concatenate([kvbuf[yb, i, 1] for i in range(wide)], axis=1)
            scores = dot_t(k, queries[cut])
            if masked:
                kk = lax.broadcasted_iota(jnp.int32, scores.shape, 0)
                qq = lax.broadcasted_iota(jnp.int32, scores.shape, 1) + part_q * half_q
                theirs = core + rel * (1 - 2 * core)
                k_at = kk + (kk // patches + core) * patches
                q_at = qq + (qq // patches + theirs) * patches
                scores = jnp.where(k_at <= q_at, scores, NEG)
            old = m_ref[rel, :, cut]
            new = jnp.maximum(old, jnp.max(scores, axis=0, keepdims=True))
            keep = jnp.exp2((old - new) * factor)
            e = jnp.exp2((scores - new) * factor)
            m_ref[rel, :, cut] = new
            l_ref[rel, :, cut] = l_ref[rel, :, cut] * keep + jnp.sum(e, axis=0, keepdims=True)
            acc[rel, :, cut] = acc[rel, :, cut] * keep + dot(vt, e.astype(BF16))

    def run_both(yb):
        @pl.when(yb < y)
        def _():
            def body(i, carry):
                attend(yb, 1 - i, False)
                return carry

            lax.fori_loop(0, 2, body, 0)


    def own_body(rel, carry):
        @pl.when(rel == 1)
        def _():
            take_down(0)
            q_give.wait_recv()

        attend(y, rel, True)
        return carry

    lax.fori_loop(0, 2, own_body, 0)
    for d in (1, 3, 2):
        take_down(d)
    for d in (0, 1, 3, 2):
        take_up(d)
    run_both(y3)
    run_both(y1)
    lax.fori_loop(0, CHUNKS, bulk_combine, 0)
    take_far()
    run_both(y2)
    opart[...] = (acc[1] / l_ref[1]).astype(BF16)
    stpart[...] = jnp.zeros(stpart.shape, F32)
    stpart[0:1] = m_ref[1]
    stpart[1:2] = l_ref[1]
    o_give.start()
    st_give.start()
    o_give.wait_recv()
    st_give.wait_recv()
    m0, m1 = m_ref[0], stget[0:1]
    top = jnp.maximum(m0, m1)
    w0 = jnp.exp2((m0 - top) * factor)
    w1 = jnp.exp2((m1 - top) * factor) * stget[1:2]
    mixed = (acc[0] * w0 + oget[...].astype(F32) * w1) / (l_ref[0] * w0 + w1)
    for qb in range(XN):
        osend[qb] = jnp.transpose(mixed[:, qb * patches : (qb + 1) * patches]).astype(BF16)

    def o_copy(d):
        h = lax.rem(x + d, XN)
        return remote(osend.at[h], orecv.at[x], o_s.at[d - 1], o_r.at[d - 1], xpeer(d))

    def o_arrival(d):
        at = orecv.at[lax.rem(x + XN - d, XN)]
        return remote(at, at, o_s.at[d - 1], o_r.at[d - 1], xpeer(d))

    for d in (2, 1, 3):
        o_copy(d).start()
    orecv[x] = osend[x]
    loads[7].wait()
    for d in (1, 3, 2):
        o_arrival(d).wait_recv()
    gattn = jnp.concatenate([orecv[h] for h in range(XN)], axis=1)

    def out_part(zz):
        return dot(gattn, gout[:, pl.ds(pl.multiple_of(zz * piece, piece), piece)])

    half_p = patches // 2
    low, high = slice(0, half_p), slice(half_p, patches)
    far_up = remote(rfs.at[0], rfar.at[0], rf_s.at[0], rf_r.at[0], z_up)
    far_down = remote(rfs.at[1], rfar.at[1], rf_s.at[1], rf_r.at[1], z_down)

    def r_up(b):
        return remote(rsend.at[0, b], rrecv.at[0, b], r_s.at[b], r_r.at[b], z_up)

    def r_down(b):
        return remote(rsend.at[1, b], rrecv.at[1, b], r_s.at[2 + b], r_r.at[2 + b], z_down)

    far_part = out_part(far_at).astype(BF16)
    rfs[0] = far_part[low]
    far_up.start()
    rfs[1] = far_part[high]
    far_down.start()
    up_part = out_part(up_at)
    rsend[0, 1] = up_part[high].astype(BF16)
    r_up(1).start()
    down_part = out_part(down_at)
    rsend[1, 0] = down_part[low].astype(BF16)
    r_down(0).start()
    update = out_part(z)
    far_up.wait_recv()
    rsend[0, 0] = (up_part[low] + rfar[0].astype(F32)).astype(BF16)
    r_up(0).start()
    far_down.wait_recv()
    rsend[1, 1] = (down_part[high] + rfar[1].astype(F32)).astype(BF16)
    r_down(1).start()

    ri = lax.broadcasted_iota(jnp.int32, (own, own), 0)
    ci = lax.broadcasted_iota(jnp.int32, (own, own), 1)
    to_patch_major = jnp.where(ci == lax.rem(ri, 2) * span + ri // 2, 1.0, 0.0).astype(BF16)
    for c in range(CHUNKS):
        for b in range(2):
            bulk_up(c, b).wait_recv()
            bulk_down(c, b).wait_recv()
        state = jnp.concatenate(
            [
                ownf[c, b * span : (b + 1) * span] + brecv[c, 0, b].astype(F32) + brecv[c, 1, b].astype(F32)
                for b in range(2)
            ],
            axis=0,
        ).astype(BF16)
        bst[c * own : (c + 1) * own] = dot(to_patch_major, state).astype(BF16)

    sources, blocks = owners_ref.shape
    spread = jnp.where(
        lax.broadcasted_iota(jnp.int32, (blocks, patches), 1) // 2
        == lax.broadcasted_iota(jnp.int32, (blocks, patches), 0),
        1.0,
        0.0,
    ).astype(BF16)
    listed = dot(owners_ref[...].astype(F32).astype(BF16), spread)
    is_mine = lax.broadcasted_iota(jnp.int32, listed.shape, 0) == s
    listed_row = jnp.sum(jnp.where(is_mine, listed, 0.0), axis=0, keepdims=True)
    pr = lax.broadcasted_iota(jnp.int32, (patches, patches), 0)
    pc = lax.broadcasted_iota(jnp.int32, (patches, patches), 1)
    listed_col = jnp.sum(jnp.where(pr == pc, listed_row, 0.0), axis=1, keepdims=True)
    earlier = (listed_col == listed_row) & (pr < pc) & (lax.rem(pr, 2) == lax.rem(pc, 2))
    rank = jnp.sum(jnp.where(earlier, 1.0, 0.0), axis=0, keepdims=True)
    slot = listed_row * 4.0 + rank * 2.0 + lax.rem(pc, 2).astype(F32)
    pick = jnp.where(slot == pr.astype(F32), 1.0, 0.0).astype(BF16)

    per = patches // plane
    loads[8].wait()
    for b in range(2):
        r_up(b).wait_recv()
        r_down(b).wait_recv()
    total = update + pin[z].reshape(patches, piece).astype(F32)
    total = total + jnp.concatenate(
        [rrecv[0, b].astype(F32) + rrecv[1, b].astype(F32) for b in range(2)], axis=0
    )
    result = total.astype(BF16)
    sorted_rows = dot(pick, result)
    for o in range(plane):
        psend[o] = sorted_rows[o * per : (o + 1) * per].astype(BF16)

    def p_copy(d):
        return remote(
            psend.at[lax.rem(s + d, plane)], state_ref.at[s], p_s.at[d - 1], p_r.at[d - 1], (lax.rem(s + d, plane), z)
        )

    def p_start(d, carry):
        p_copy(d).start()
        return carry

    lax.fori_loop(1, plane, p_start, 0)
    state_ref[s] = psend[s]
    gp = back.shape[0]
    re = lax.broadcasted_iota(jnp.int32, (2 * patches, patches), 0)
    ce = lax.broadcasted_iota(jnp.int32, (2 * patches, patches), 1)
    shares = jnp.zeros((2 * patches, gp), F32)
    for b in range(2):
        lift = jnp.where(re == 2 * ce + b, 1.0, 0.0).astype(BF16)
        shares = shares + dot(lift, result[:, b * gp : (b + 1) * gp])
    shares = shares.astype(BF16)
    for n in range(bst.shape[1] // 256):
        cut = slice(n * 256, (n + 1) * 256)
        byte_ref[:, cut] = (bst[:, cut].astype(F32) + dot(shares, back[:, cut])).astype(BF16)

    def p_wait(d, carry):
        at = state_ref.at[lax.rem(s + plane - d, plane)]
        remote(at, at, p_s.at[d - 1], p_r.at[d - 1], (lax.rem(s + d, plane), z)).wait_recv()
        p_copy(d).wait_send()
        return carry

    lax.fori_loop(1, plane, p_wait, 0)

    def drain(c, carry):
        for d in (1, 2, 3):
            pp_copy(c, d).wait_send()
            ag_copy(c, d).wait_send()
        for copy in (*bulk_far(c), bulk_up(c, 0), bulk_up(c, 1), bulk_down(c, 0), bulk_down(c, 1)):
            copy.wait_send()
        return carry

    lax.fori_loop(0, CHUNKS, drain, 0)
    for d in (1, 2, 3):
        xk_copy(d).wait_send()
        xq_copy(d).wait_send()
        o_copy(d).wait_send()
    for d in range(XN):
        spread_piece(d, sent)

    @pl.when(inner)
    def _():
        for d in (0, 2):
            up_copy(y3, d, ru_s, ru_r).wait_send()

    @pl.when(outer)
    def _():
        for d in (1, 3):
            down_copy(y1, d, rd_s, rd_r).wait_send()

    for copy in (q_give, o_give, st_give, far_up, far_down, r_up(0), r_up(1), r_down(0), r_down(1)):
        copy.wait_send()


def on_device(
    byte_in, local_gain, local_qkv, local_out, mlp_up, mlp_down, local_scale, patch_proj,
    global_gain, global_qkv, global_out, global_scale, back_proj, owners,
):
    patches, span8, dl = byte_in.shape
    gw = global_out.shape[1]
    piece = gw // ZN
    ff = mlp_up.shape[1]
    rows = patches * span8 // CHUNKS
    span = patches // CHUNKS
    own = 2 * span
    gp = back_proj.shape[0]
    plane = 2 * XN * YN
    wqkv3 = jnp.transpose(local_qkv, (1, 0, 2))
    gqkv3 = jnp.transpose(global_qkv, (1, 0, 2))
    hbm = pl.BlockSpec(memory_space=pl.ANY)
    vm = pl.BlockSpec(memory_space=pltpu.VMEM)
    sm = pl.BlockSpec(memory_space=pltpu.SMEM)
    dma = pltpu.SemaphoreType.DMA

    def buf(*shape, dtype=BF16):
        return pltpu.VMEM(shape, dtype)

    big = [byte_in.reshape(patches * span8, dl), wqkv3, local_out, mlp_up, mlp_down, patch_proj, gqkv3, global_out, back_proj]
    scratch = [buf(*a.shape) for a in big] + [
        buf(rows, ff),
        buf(rows, dl, dtype=F32),
        buf(rows, gp, dtype=F32),
        buf(CHUNKS, ZN, 2, span, dl),
        buf(CHUNKS, 2, span, dl),
        buf(CHUNKS, 2, 2, span, dl),
        buf(CHUNKS, own, dl, dtype=F32),
        buf(CHUNKS, ZN, span, 2 * gp),
        buf(CHUNKS, ZN - 1, span, 2 * gp),
        buf(CHUNKS, span, 2 * gp, dtype=F32),
        buf(ZN, CHUNKS, span, piece),
        buf(patches, gw),
        buf(XN, 3, patches, HD),
        buf(YN, XN, 2, patches, HD),
        buf(2, XN, patches, HD),
        buf(2, 1, XN * patches, dtype=F32),
        buf(2, 1, XN * patches, dtype=F32),
        buf(2, HD, XN * patches, dtype=F32),
        buf(HD, XN * patches),
        buf(HD, XN * patches),
        buf(8, XN * patches, dtype=F32),
        buf(8, XN * patches, dtype=F32),
        buf(XN, patches, HD),
        buf(XN, patches, HD),
        buf(2, patches // 2, piece),
        buf(2, patches // 2, piece),
        buf(2, 2, patches // 2, piece),
        buf(2, 2, patches // 2, piece),
        buf(2 * patches, dl),
        buf(plane, patches // plane, piece),
        dma((9,)),
    ]
    scratch += [dma((CHUNKS, 3))] * 4 + [dma((CHUNKS, 2))] * 2 + [dma((CHUNKS, 4))] * 2
    scratch += [dma((3,))] * 4 + [dma((4,))] * 8 + [dma((3,))] * 4 + [dma((2,))] * 2 + [dma((4,))] * 2 + [dma((plane - 1,))] * 2
    byte_out, global_state = pl.pallas_call(
        kernel,
        out_shape=(
            jax.ShapeDtypeStruct((2 * patches, dl), BF16),
            jax.ShapeDtypeStruct((plane, patches // plane, piece), BF16),
        ),
        in_specs=[hbm] * 9 + [vm] * 3 + [sm] * 2,
        out_specs=(vm, vm),
        scratch_shapes=scratch,
        compiler_params=pltpu.CompilerParams(
            collective_id=0, has_side_effects=True, vmem_limit_bytes=60 * 1024 * 1024
        ),
    )(*big, local_gain.reshape(1, dl), global_gain.reshape(1, gw), owners, local_scale, global_scale)
    return (byte_out.reshape(patches, 2, dl), global_state.reshape(patches, piece))


def solution(mesh):
    placed = (
        P("seq", None, None),
        P(),
        P(None, None, "head"),
        P("head", None),
        P(None, "head"),
        P("head", None),
        P("head"),
        P(),
        P(),
        P(None, None, "head"),
        P("head", None),
        P("head"),
        P(),
        P(),
    )
    return jax.shard_map(
        on_device,
        mesh=mesh,
        in_specs=placed,
        out_specs=(P("seq", "head", None), P("seq", "head")),
        check_vma=False,
    )
```

```python
import functools
import math

import jax
import jax.numpy as jnp
from jax import lax
from jax.experimental import pallas as pl
from jax.experimental.pallas import tpu as pltpu
from jax.sharding import PartitionSpec as P

EPS = 1e-06
NEG = -1e30
MESH = pl.DeviceIdType.MESH
F32 = jnp.float32
BF16 = jnp.bfloat16
XN = 4
YN = 4
ZN = 4
CHUNKS = 4
HD = 128


def dot(a, b):
    return jnp.dot(a, b, preferred_element_type=F32)


def dot_t(a, b):
    return lax.dot_general(a, b, (((1,), (1,)), ((), ())), preferred_element_type=F32)


def unit(v):
    return v * lax.rsqrt(jnp.mean(v * v, axis=-1, keepdims=True) + EPS)


def kernel(
    x_hbm, wqkv_hbm, wo_hbm, up_hbm, down_hbm, pp_hbm, gqkv_hbm, gout_hbm, back_hbm,
    gain_ref, ggain_ref, owners_ref, lscale_ref, gscale_ref,
    byte_hbm, state_ref,
    xv, wqkv, wo, up, down, ppw, gqkv, gout, back,
    xps, normed, act, part, ppf, bsend, bfar, brecv, ownf, ppsend, pprecv, ppown, pin,
    mixed_qkv, qkvs, kvbuf, qbuf, m_ref, l_ref, acc, opart, oget, stpart, stget, osend, orecv, rfar, rsend, rrecv, bst, psend, byte_ref,
    lsem, x_sem, pp_s, pp_r, ag_s, ag_r, bf_r, bk_s, bk_r, x_s, xk_r, xq_r,
    yu_s, yu_r, yd_s, yd_r, ru_s, ru_r, rd_s, rd_r, c_s, c_r, o_r, rf_r, r_s, r_r, p_s, p_r,
):
    s = lax.axis_index("seq")
    z = lax.axis_index("head")
    core = lax.rem(s, 2)
    x = lax.rem(s // 2, XN)
    y = s // (2 * XN)
    rows = xv.shape[0] // CHUNKS
    span = rows // 8
    own = 2 * span

    def seq_of(yy, xx, cc):
        return (yy * XN + xx) * 2 + cc

    def zpeer(d):
        return (s, lax.rem(z + d, ZN))

    def xpeer(d):
        return (seq_of(y, lax.rem(x + d, XN), core), z)

    y_up = (seq_of(lax.rem(y + 1, YN), x, core), z)
    y_down = (seq_of(lax.rem(y + YN - 1, YN), x, core), z)
    sibling = (seq_of(y, x, 1 - core), z)

    loads = [
        pltpu.make_async_copy(a, b, lsem.at[i])
        for i, (a, b) in enumerate(
            ((wqkv_hbm, wqkv), (up_hbm, up), (wo_hbm, wo), (down_hbm, down), (pp_hbm, ppw),
             (gqkv_hbm, gqkv), (gout_hbm, gout), (back_hbm, back))
        )
    ]
    def xload(c):
        at = pl.ds(pl.multiple_of(c * rows, rows), rows)
        return pltpu.make_async_copy(x_hbm.at[at], xv.at[at], x_sem.at[c])

    xload(0).start()
    loads[0].start()

    barrier = pltpu.get_barrier_semaphore()
    plane = 2 * XN * YN

    def greet(peer):
        pl.semaphore_signal(barrier, inc=1, device_id=peer, device_id_type=MESH)

    def greet_plane(d, carry):
        greet((lax.rem(s + d, plane), z))
        return carry

    for d in (1, 2, 3):
        greet(zpeer(d))
    lax.fori_loop(1, plane, greet_plane, 0)

    def remote(src, dst, ss, rs, peer):
        return pltpu.make_async_remote_copy(
            src_ref=src, dst_ref=dst, send_sem=ss, recv_sem=rs, device_id=peer, device_id_type=MESH
        )

    def pp_copy(c, d):
        return remote(
            ppsend.at[c, lax.rem(z + d, ZN)], pprecv.at[c, d - 1], pp_s.at[0], pp_r.at[c], zpeer(d)
        )

    def ag_copy(c, d):
        return remote(pin.at[z, c], pin.at[z, c], ag_s.at[0], ag_r.at[d - 1], zpeer(d))

    z_up = zpeer(1)
    z_down = zpeer(ZN - 1)
    up_at = lax.rem(z + 1, ZN)
    down_at = lax.rem(z + ZN - 1, ZN)
    far_at = lax.rem(z + 2, ZN)

    def bulk_far(c):
        return (
            remote(bsend.at[c, far_at, 0], bfar.at[c, 0], bk_s.at[0], bf_r.at[0], z_up),
            remote(bsend.at[c, far_at, 1], bfar.at[c, 1], bk_s.at[0], bf_r.at[0], z_down),
        )

    def bulk_up(c, b):
        return remote(bsend.at[c, up_at, b], brecv.at[c, 0, b], bk_s.at[0], bk_r.at[0], z_up)

    def bulk_down(c, b):
        return remote(bsend.at[c, down_at, b], brecv.at[c, 1, b], bk_s.at[0], bk_r.at[0], z_down)

    def bulk_combine(c, carry):
        bsend[c, up_at, 0] = (bsend[c, up_at, 0].astype(F32) + bfar[c, 0].astype(F32)).astype(BF16)
        bulk_up(c, 0).start()
        bsend[c, down_at, 1] = (bsend[c, down_at, 1].astype(F32) + bfar[c, 1].astype(F32)).astype(BF16)
        bulk_down(c, 1).start()
        return carry

    def arrived(ref, sem):
        pltpu.make_async_copy(ref, ref, sem).wait()

    def finish_patches(c):
        total = ppown[c]
        arrived(pprecv.at[c], pp_r.at[c])
        for d in (1, 2, 3):
            total = total + pprecv[c, d - 1].astype(F32)
        pin[z, c] = total.astype(BF16)
        for d in (2, 1, 3):
            ag_copy(c, d).start()

    row_i = lax.broadcasted_iota(jnp.int32, (rows, rows), 0)
    col_i = lax.broadcasted_iota(jnp.int32, (rows, rows), 1)
    to_byte_major = jnp.where(
        col_i == lax.rem(row_i, span) * 8 + row_i // span, 1.0, 0.0
    ).astype(BF16)

    def prepare(c, slot):
        xp = dot(to_byte_major, xv[pl.ds(pl.multiple_of(c * rows, rows), rows), :])
        xps[slot] = xp.astype(BF16)
        normed[slot] = (
            xp * lax.rsqrt(jnp.mean(xp * xp, axis=-1, keepdims=True) + EPS) * gain_ref[...]
        ).astype(BF16)

    def gelu(v):
        inner = v * (0.7978845608028654 + (0.7978845608028654 * 0.044715) * (v * v))
        half = 0.5 * v
        return (half + half * jnp.tanh(inner)).astype(BF16)

    rr = lax.broadcasted_iota(jnp.int32, (rows, rows), 0)
    cc = lax.broadcasted_iota(jnp.int32, (rows, rows), 1)
    seen = (lax.rem(rr, span) == lax.rem(cc, span)) & (cc // span <= rr // span)

    def chunk(c, ahead):
        slot = lax.rem(c, 2)
        nv = normed[slot]
        tiles = [slice(n * 256, (n + 1) * 256) for n in range(up.shape[1] // 256)]
        cuts = [slice(h * HD, (h + 1) * HD) for h in range(2)]
        q2 = dot(nv, wqkv[0])
        k2 = dot(nv, wqkv[1])
        v2 = dot(nv, wqkv[2]).astype(BF16)
        hidden = dot(nv, up[:, tiles[0]])
        qs = [unit(q2[:, cut]).astype(BF16) for cut in cuts]
        ks = [unit(k2[:, cut]).astype(BF16) for cut in cuts]
        later = dot(nv, up[:, tiles[1]])
        scores = [dot_t(qs[h], ks[h]) for h in range(2)]
        act[:, tiles[0]] = gelu(hidden)
        hidden = dot(nv, up[:, tiles[2]])
        es, totals = [], []
        for h in range(2):
            sc = jnp.where(seen, scores[h] * (lscale_ref[h] / math.sqrt(HD)), NEG)
            e = jnp.exp(sc - jnp.max(sc, axis=-1, keepdims=True))
            totals.append(jnp.sum(e, axis=-1, keepdims=True))
            es.append(e.astype(BF16))
        act[:, tiles[1]] = gelu(later)
        later = dot(nv, up[:, tiles[3]])
        heads = [(dot(es[h], v2[:, cuts[h]]) / totals[h]).astype(BF16) for h in range(2)]
        lo = jnp.concatenate(heads, axis=1)
        act[:, tiles[2]] = gelu(hidden)
        act[:, tiles[3]] = gelu(later)
        if ahead is not None:
            xload(ahead).wait()
            prepare(ahead, 1 - slot)
        mine = lax.broadcasted_iota(jnp.int32, (rows, 1), 0) // own == z
        a = act[...]
        for cut in tiles:
            t = dot(lo, wo[:, cut]) + dot(a, down[:, cut])
            t = t + jnp.where(mine, xps[slot, :, cut].astype(F32), 0.0)
            part[:, cut] = t
            tb = t.astype(BF16)
            for h in range(ZN):
                for b in range(2):
                    at = h * own + b * span
                    bsend[c, h, b, :, cut] = tb[at : at + span]
        ownf[c] = part[pl.ds(pl.multiple_of(z * own, own), own), :]
        pp = dot(bsend[c].reshape(rows, part.shape[1]), ppw[...])
        ppf[...] = pp
        pb = pp.astype(BF16)
        gp = pp.shape[1]
        for h in range(ZN):
            for b in range(2):
                at = (2 * h + b) * span
                ppsend[c, h, :, b * gp : (b + 1) * gp] = pb[at : at + span]
        for b in range(2):
            at = pl.multiple_of(z * own + b * span, span)
            ppown[c, :, b * gp : (b + 1) * gp] = ppf[pl.ds(at, span), :]

        @pl.when(c == 0)
        def _():
            pl.semaphore_wait(barrier, ZN - 1 + plane - 1)

        for d in (2, 1, 3):
            pp_copy(c, d).start()

        @pl.when(c >= 1)
        def _():
            finish_patches(c - 1)


    xload(0).wait()
    for load in loads[1:4]:
        load.start()
    for c in range(1, CHUNKS):
        xload(c).start()
    for load in loads[4:]:
        load.start()
    prepare(jnp.int32(0), 0)
    for load in loads[:5]:
        load.wait()

    def chunk_step(c, carry):
        chunk(c, c + 1)
        return carry

    lax.fori_loop(0, CHUNKS - 1, chunk_step, 0)
    chunk(jnp.int32(CHUNKS - 1), None)
    finish_patches(CHUNKS - 1)
    loads[5].wait()
    patches = CHUNKS * span
    piece = pin.shape[3]
    square = jnp.zeros((patches, 1), F32)
    for d in (0, 1, 3, 2):
        h = lax.rem(z + ZN - d, ZN)
        if d:
            arrived(pin.at[h], ag_r.at[d - 1])
        if d == 2:
            for c in range(CHUNKS):
                for copy in bulk_far(c):
                    copy.start()
            for c in range(CHUNKS):
                bulk_up(c, 1).start()
                bulk_down(c, 0).start()
        at = pl.ds(pl.multiple_of(h * piece, piece), piece)
        v = pin[h].reshape(patches, piece).astype(F32)
        square = square + jnp.sum(v * v, axis=-1, keepdims=True)
        g = (v * ggain_ref[:, at]).astype(BF16)
        for j in (1, 2, 0):
            for half in range(2):
                cut = slice(half * 256, (half + 1) * 256)
                r = dot(g, gqkv[j, at, cut])
                mixed_qkv[j, :, cut] = r if d == 0 else mixed_qkv[j, :, cut] + r
    inv = lax.rsqrt(square / (ZN * piece) + EPS)

    def project(j):
        for t in range(XN):
            v = mixed_qkv[j, :, t * HD : (t + 1) * HD] * inv
            if j < 2:
                v = unit(v)
            if j == 2:
                v = jnp.transpose(v)
            qkvs[t, j] = v.astype(BF16)

    def xk_copy(d):
        h = lax.rem(x + d, XN)
        return remote(qkvs.at[h, pl.ds(1, 2)], kvbuf.at[y, x], x_s.at[0], xk_r.at[d - 1], xpeer(d))

    def src(d):
        return lax.rem(x + XN - d, XN)

    def xk_arrival(d):
        at = kvbuf.at[y, src(d)]
        return pltpu.make_async_copy(at, at, xk_r.at[d - 1])

    def xq_copy(d):
        h = lax.rem(x + d, XN)
        return remote(qkvs.at[h, 0], qbuf.at[0, x], x_s.at[0], xq_r.at[0], xpeer(d))

    y1 = lax.rem(y + 1, YN)
    y2 = lax.rem(y + 2, YN)
    y3 = lax.rem(y + 3, YN)

    def up_copy(row, d, ss, rs):
        at = kvbuf.at[row, src(d)]
        return remote(at, at, ss.at[d], rs.at[d], y_up)

    def down_copy(row, d, ss, rs):
        at = kvbuf.at[row, src(d)]
        return remote(at, at, ss.at[d], rs.at[d], y_down)

    def relay_up(row, d):
        at = kvbuf.at[row, src(d)]
        return remote(at, at, ru_s.at[d // 2], ru_r.at[d // 2], y_up)

    def relay_down(row, d):
        at = kvbuf.at[row, src(d)]
        return remote(at, at, rd_s.at[d // 2], rd_r.at[d // 2], y_down)

    last = YN - 1
    inner = (y >= 1) & (y < last)
    outer = (y == 0) | (y == last)

    def spread_piece(d, act_on):
        @pl.when(y < last)
        def _():
            act_on(up_copy(y, d, yu_s, yu_r))

        @pl.when((y == 0) | ((y == 1) & (d % 2 == 1)))
        def _():
            act_on(down_copy(y, d, yd_s, yd_r))

    def start(copy):
        copy.start()

    def sent(copy):
        copy.wait_send()

    def take_down(d):
        @pl.when(y >= 1)
        def _():
            up_copy(y3, d, yu_s, yu_r).wait_recv()

        if d % 2 == 0:

            @pl.when(inner)
            def _():
                relay_up(y3, d).start()

    def take_up(d):
        @pl.when((y == last) | ((y == 0) & (d % 2 == 1)))
        def _():
            down_copy(y1, d, yd_s, yd_r).wait_recv()

        if d % 2 == 1:

            @pl.when(outer)
            def _():
                relay_down(y1, d).start()

    def take_far():
        @pl.when(y >= 2)
        def _():
            for d in (0, 2):
                relay_up(y2, d).wait_recv()
            for d in (1, 3):
                relay_down(y2, d).wait_recv()

    q_give = remote(qbuf.at[0], qbuf.at[1], c_s.at[0], c_r.at[0], sibling)
    o_give = remote(opart, oget, c_s.at[1], c_r.at[1], sibling)
    st_give = remote(stpart, stget, c_s.at[2], c_r.at[2], sibling)

    project(1)
    project(2)
    for d in (2, 1, 3):
        xk_copy(d).start()
    kvbuf[y, x] = qkvs[x, 1:3]
    spread_piece(0, start)
    project(0)
    for d in (2, 1, 3):
        xq_copy(d).start()
    qbuf[0, x] = qkvs[x, 0]
    m_ref[...] = jnp.full(m_ref.shape, NEG, F32)
    l_ref[...] = jnp.zeros(l_ref.shape, F32)
    acc[...] = jnp.zeros(acc.shape, F32)
    factor = gscale_ref[x] * (math.log2(math.e) / math.sqrt(HD))

    for d in (3, 1, 2):
        xk_arrival(d).wait()
        spread_piece(d, start)
    arrived(qbuf.at[0, pl.ds(0, XN - 1)], xq_r.at[0])
    q_give.start()

    half_q = XN * patches // 2

    def attend(yb, rels, masked):
        chains = [(rel, part_q) for rel in rels for part_q in range(2)]

        def raw(chain):
            rel, part_q = chain
            wide = (part_q + 1) * XN // 2 if masked else XN
            queries = qbuf[rel].reshape(XN * patches, HD)[part_q * half_q : (part_q + 1) * half_q]
            scores = dot_t(kvbuf[yb, 0:wide, 0].reshape(wide * patches, HD), queries)
            if masked:
                kk = lax.broadcasted_iota(jnp.int32, scores.shape, 0)
                qq = lax.broadcasted_iota(jnp.int32, scores.shape, 1) + part_q * half_q
                theirs = core + rel * (1 - 2 * core)
                k_at = kk + (kk // patches + core) * patches
                q_at = qq + (qq // patches + theirs) * patches
                scores = jnp.where(k_at <= q_at, scores, NEG)
            return scores

        def fold(op, v):
            return op(op(v.reshape(8, v.shape[0] // 8, v.shape[1]), axis=0), axis=0, keepdims=True)

        upcoming = raw(chains[0])
        for i, (rel, part_q) in enumerate(chains):
            scores = upcoming
            if i + 1 < len(chains):
                upcoming = raw(chains[i + 1])
            cut = slice(part_q * half_q, (part_q + 1) * half_q)
            old = m_ref[rel, :, cut]
            new = jnp.maximum(old, fold(jnp.max, scores))
            keep = jnp.exp2((old - new) * factor)
            e = jnp.exp2((scores - new) * factor)
            m_ref[rel, :, cut] = new
            l_ref[rel, :, cut] = l_ref[rel, :, cut] * keep + fold(jnp.sum, e)
            wide = scores.shape[0] // patches
            vt = jnp.concatenate([kvbuf[yb, k, 1] for k in range(wide)], axis=1)
            acc[rel, :, cut] = acc[rel, :, cut] * keep + dot(vt, e.astype(BF16))

    def run(yb, rels):
        @pl.when(yb < y)
        def _():
            attend(yb, rels, False)


    attend(y, (0,), True)
    take_down(0)
    take_up(0)
    q_give.wait_recv()
    attend(y, (1,), True)
    for d in (3, 1, 2):
        take_up(d)
        take_down(d)
    run(y3, (1, 0))
    run(y1, (1, 0))
    arrived(bfar, bf_r.at[0])
    lax.fori_loop(0, CHUNKS, bulk_combine, 0)
    take_far()
    run(y2, (1,))
    opart[...] = (acc[1] / l_ref[1]).astype(BF16)
    stpart[...] = jnp.zeros(stpart.shape, F32)
    stpart[0:1] = m_ref[1]
    stpart[1:2] = l_ref[1]
    o_give.start()
    st_give.start()
    run(y2, (0,))
    o_give.wait_recv()
    st_give.wait_recv()
    m0, m1 = m_ref[0], stget[0:1]
    top = jnp.maximum(m0, m1)
    w0 = jnp.exp2((m0 - top) * factor)
    w1 = jnp.exp2((m1 - top) * factor) * stget[1:2]
    mixed = (acc[0] * w0 + oget[...].astype(F32) * w1) / (l_ref[0] * w0 + w1)
    for qb in range(XN):
        osend[qb] = jnp.transpose(mixed[:, qb * patches : (qb + 1) * patches]).astype(BF16)

    def o_copy(d):
        h = lax.rem(x + d, XN)
        return remote(osend.at[h], orecv.at[x], x_s.at[0], o_r.at[0], xpeer(d))

    for d in (2, 1, 3):
        o_copy(d).start()
    orecv[x] = osend[x]
    loads[6].wait()
    arrived(orecv.at[pl.ds(0, XN - 1)], o_r.at[0])
    gattn = jnp.concatenate([orecv[h] for h in range(XN)], axis=1)

    def out_part(zz):
        return dot(gattn, gout[:, pl.ds(pl.multiple_of(zz * piece, piece), piece)])

    half_p = patches // 2
    low, high = slice(0, half_p), slice(half_p, patches)
    far_up = remote(rsend.at[2, 0], rfar.at[0], r_s.at[0], rf_r.at[0], z_up)
    far_down = remote(rsend.at[2, 1], rfar.at[1], r_s.at[0], rf_r.at[1], z_down)

    def r_up(b):
        return remote(rsend.at[0, b], rrecv.at[0, b], r_s.at[0], r_r.at[0], z_up)

    def r_down(b):
        return remote(rsend.at[1, b], rrecv.at[1, b], r_s.at[0], r_r.at[0], z_down)

    far_part = out_part(far_at).astype(BF16)
    rsend[2, 0] = far_part[low]
    far_up.start()
    rsend[2, 1] = far_part[high]
    far_down.start()
    up_part = out_part(up_at)
    rsend[0, 1] = up_part[high].astype(BF16)
    down_part = out_part(down_at)
    rsend[1, 0] = down_part[low].astype(BF16)
    update = out_part(z)

    ri = lax.broadcasted_iota(jnp.int32, (own, own), 0)
    ci = lax.broadcasted_iota(jnp.int32, (own, own), 1)
    to_patch_major = jnp.where(ci == lax.rem(ri, 2) * span + ri // 2, 1.0, 0.0).astype(BF16)
    arrived(brecv, bk_r.at[0])
    for c in range(CHUNKS):
        state = jnp.concatenate(
            [
                ownf[c, b * span : (b + 1) * span] + brecv[c, 0, b].astype(F32) + brecv[c, 1, b].astype(F32)
                for b in range(2)
            ],
            axis=0,
        ).astype(BF16)
        bst[c * own : (c + 1) * own] = dot(to_patch_major, state).astype(BF16)

    r_up(1).start()
    r_down(0).start()
    sources, blocks = owners_ref.shape
    spread = jnp.where(
        lax.broadcasted_iota(jnp.int32, (blocks, patches), 1) // 2
        == lax.broadcasted_iota(jnp.int32, (blocks, patches), 0),
        1.0,
        0.0,
    ).astype(BF16)
    listed = dot(owners_ref[...].astype(F32).astype(BF16), spread)
    is_mine = lax.broadcasted_iota(jnp.int32, listed.shape, 0) == s
    listed_row = jnp.sum(jnp.where(is_mine, listed, 0.0), axis=0, keepdims=True)
    pr = lax.broadcasted_iota(jnp.int32, (patches, patches), 0)
    pc = lax.broadcasted_iota(jnp.int32, (patches, patches), 1)
    listed_col = jnp.sum(jnp.where(pr == pc, listed_row, 0.0), axis=1, keepdims=True)
    earlier = (listed_col == listed_row) & (pr < pc) & (lax.rem(pr, 2) == lax.rem(pc, 2))
    rank = jnp.sum(jnp.where(earlier, 1.0, 0.0), axis=0, keepdims=True)
    slot = listed_row * 4.0 + rank * 2.0 + lax.rem(pc, 2).astype(F32)
    pick = jnp.where(slot == pr.astype(F32), 1.0, 0.0).astype(BF16)

    per = patches // plane
    loads[7].wait()
    far_up.wait_recv()
    rsend[0, 0] = (up_part[low] + rfar[0].astype(F32)).astype(BF16)
    r_up(0).start()
    far_down.wait_recv()
    rsend[1, 1] = (down_part[high] + rfar[1].astype(F32)).astype(BF16)
    r_down(1).start()
    arrived(rrecv, r_r.at[0])
    total = update + pin[z].reshape(patches, piece).astype(F32)
    total = total + jnp.concatenate(
        [rrecv[0, b].astype(F32) + rrecv[1, b].astype(F32) for b in range(2)], axis=0
    )
    result = total.astype(BF16)
    sorted_rows = dot(pick, result)
    for o in range(plane):
        psend[o] = sorted_rows[o * per : (o + 1) * per].astype(BF16)

    def p_copy(d):
        return remote(
            psend.at[lax.rem(s + d, plane)], state_ref.at[s], p_s.at[0], p_r.at[0], (lax.rem(s + d, plane), z)
        )

    def p_start(d, carry):
        p_copy(d).start()
        return carry

    lax.fori_loop(1, plane, p_start, 0)
    keep_own = pltpu.make_async_copy(psend.at[s], state_ref.at[s], lsem.at[9])
    keep_own.start()
    gp = back.shape[0]
    re = lax.broadcasted_iota(jnp.int32, (2 * patches, patches), 0)
    ce = lax.broadcasted_iota(jnp.int32, (2 * patches, patches), 1)
    shares = jnp.zeros((2 * patches, gp), F32)
    for b in range(2):
        lift = jnp.where(re == 2 * ce + b, 1.0, 0.0).astype(BF16)
        shares = shares + dot(lift, result[:, b * gp : (b + 1) * gp])
    shares = shares.astype(BF16)
    for n in range(bst.shape[1] // 256):
        cut = slice(n * 256, (n + 1) * 256)
        both = bst[:, cut].astype(F32) + dot(shares, back[:, cut])
        byte_ref[:, :, cut] = both.astype(BF16).reshape(patches, 2, 256)

    byte_put = pltpu.make_async_copy(byte_ref, byte_hbm, lsem.at[8])
    byte_put.start()
    arrived(state_ref.at[pl.ds(0, plane - 1)], p_r.at[0])

    byte_put.wait()
    keep_own.wait()
    arrived(psend.at[pl.ds(0, plane - 1)], p_s.at[0])
    arrived(ppsend.at[pl.ds(0, ZN - 1)], pp_s.at[0])
    arrived(pin.at[pl.ds(0, ZN - 1)], ag_s.at[0])
    arrived(bsend.at[pl.ds(0, ZN - 1)], bk_s.at[0])
    arrived(qkvs, x_s.at[0])
    arrived(rsend, r_s.at[0])
    for d in range(XN):
        spread_piece(d, sent)

    @pl.when(inner)
    def _():
        for d in (0, 2):
            relay_up(y3, d).wait_send()

    @pl.when(outer)
    def _():
        for d in (1, 3):
            relay_down(y1, d).wait_send()

    for copy in (q_give, o_give, st_give):
        copy.wait_send()


def settle(a_hbm, b_hbm, a_out, b_out, va, vb, wb, in_sem, out_sem):
    cut = va.shape[0] // 4
    takes, puts = [], []
    for i in range(4):
        at = pl.ds(i * cut, cut)
        takes.append(pltpu.make_async_copy(a_hbm.at[at], va.at[at], in_sem.at[i]))
        puts.append(pltpu.make_async_copy(va.at[at], a_out.at[at], out_sem.at[i]))
    last = pltpu.make_async_copy(b_hbm, vb, in_sem.at[4])
    put_last = pltpu.make_async_copy(wb, b_out, out_sem.at[4])
    last.start()
    for take in takes:
        take.start()
    last.wait()
    wb[...] = jnp.concatenate([vb[o].astype(F32) for o in range(vb.shape[0])], axis=0).astype(BF16)
    put_last.start()
    for take, put in zip(takes, puts):
        take.wait()
        put.start()
    for put in puts:
        put.wait()
    put_last.wait()


def on_device(
    byte_in, local_gain, local_qkv, local_out, mlp_up, mlp_down, local_scale, patch_proj,
    global_gain, global_qkv, global_out, global_scale, back_proj, owners,
):
    patches, span8, dl = byte_in.shape
    gw = global_out.shape[1]
    piece = gw // ZN
    ff = mlp_up.shape[1]
    rows = patches * span8 // CHUNKS
    span = patches // CHUNKS
    own = 2 * span
    gp = back_proj.shape[0]
    plane = 2 * XN * YN
    wqkv3 = jnp.transpose(local_qkv, (1, 0, 2))
    gqkv3 = jnp.transpose(global_qkv, (1, 0, 2))
    hbm = pl.BlockSpec(memory_space=pl.ANY)
    vm = pl.BlockSpec(memory_space=pltpu.VMEM)
    sm = pl.BlockSpec(memory_space=pltpu.SMEM)
    dma = pltpu.SemaphoreType.DMA

    def buf(*shape, dtype=BF16):
        return pltpu.VMEM(shape, dtype)

    big = [byte_in.reshape(patches * span8, dl), wqkv3, local_out, mlp_up, mlp_down, patch_proj, gqkv3, global_out, back_proj]
    scratch = [buf(*a.shape) for a in big] + [
        buf(2, rows, dl),
        buf(2, rows, dl),
        buf(rows, ff),
        buf(rows, dl, dtype=F32),
        buf(rows, gp, dtype=F32),
        buf(CHUNKS, ZN, 2, span, dl),
        buf(CHUNKS, 2, span, dl),
        buf(CHUNKS, 2, 2, span, dl),
        buf(CHUNKS, own, dl, dtype=F32),
        buf(CHUNKS, ZN, span, 2 * gp),
        buf(CHUNKS, ZN - 1, span, 2 * gp),
        buf(CHUNKS, span, 2 * gp, dtype=F32),
        buf(ZN, CHUNKS, span, piece),
        buf(3, patches, piece, dtype=F32),
        buf(XN, 3, patches, HD),
        buf(YN, XN, 2, patches, HD),
        buf(2, XN, patches, HD),
        buf(2, 1, XN * patches, dtype=F32),
        buf(2, 1, XN * patches, dtype=F32),
        buf(2, HD, XN * patches, dtype=F32),
        buf(HD, XN * patches),
        buf(HD, XN * patches),
        buf(8, XN * patches, dtype=F32),
        buf(8, XN * patches, dtype=F32),
        buf(XN, patches, HD),
        buf(XN, patches, HD),
        buf(2, patches // 2, piece),
        buf(3, 2, patches // 2, piece),
        buf(2, 2, patches // 2, piece),
        buf(2 * patches, dl),
        buf(plane, patches // plane, piece),
        buf(patches, 2, dl),
        dma((10,)),
        dma((CHUNKS,)),
    ]
    counts = (1, CHUNKS, 1, 3, 1, 1, 1, 1, 3, 1, 4, 4, 4, 4, 2, 2, 2, 2, 3, 3, 1, 2, 1, 1, 1, 1)
    scratch += [dma((n,)) for n in counts]
    byte_out, global_state = pl.pallas_call(
        kernel,
        out_shape=(
            jax.ShapeDtypeStruct((patches, 2, dl), BF16),
            jax.ShapeDtypeStruct((plane, patches // plane, piece), BF16),
        ),
        in_specs=[hbm] * 9 + [vm] * 3 + [sm] * 2,
        out_specs=(hbm, hbm),
        scratch_shapes=scratch,
        compiler_params=pltpu.CompilerParams(
            collective_id=0, has_side_effects=True, vmem_limit_bytes=60 * 1024 * 1024
        ),
    )(*big, local_gain.reshape(1, dl), global_gain.reshape(1, gw), owners, local_scale, global_scale)
    return pl.pallas_call(
        settle,
        out_shape=(
            jax.ShapeDtypeStruct(byte_out.shape, BF16),
            jax.ShapeDtypeStruct((patches, piece), BF16),
        ),
        in_specs=[hbm] * 2,
        out_specs=(hbm, hbm),
        scratch_shapes=[buf(*byte_out.shape), buf(*global_state.shape), buf(patches, piece), dma((5,)), dma((5,))],
    )(byte_out, global_state)


def solution(mesh):
    placed = (
        P("seq", None, None),
        P(),
        P(None, None, "head"),
        P("head", None),
        P(None, "head"),
        P("head", None),
        P("head"),
        P(),
        P(),
        P(None, None, "head"),
        P("head", None),
        P("head"),
        P(),
        P(),
    )
    return jax.shard_map(
        on_device,
        mesh=mesh,
        in_specs=placed,
        out_specs=(P("seq", "head", None), P("seq", "head")),
        check_vma=False,
    )
```

```python
import functools
import math

import jax
import jax.numpy as jnp
from jax import lax
from jax.experimental import pallas as pl
from jax.experimental.pallas import tpu as pltpu
from jax.sharding import PartitionSpec as P

EPS = 1e-06
NEG = -1e30
MESH = pl.DeviceIdType.MESH
F32 = jnp.float32
BF16 = jnp.bfloat16
XN = 4
YN = 4
ZN = 4
CHUNKS = 4
HD = 128


def dot(a, b):
    return jnp.dot(a, b, preferred_element_type=F32)


def dot_t(a, b):
    return lax.dot_general(a, b, (((1,), (1,)), ((), ())), preferred_element_type=F32)


def unit(v):
    return v * lax.rsqrt(jnp.mean(v * v, axis=-1, keepdims=True) + EPS)


def kernel(
    x_hbm, wqkv_hbm, wo_hbm, up_hbm, down_hbm, pp_hbm, gqkv_hbm, gout_hbm, back_hbm,
    gain_ref, ggain_ref, owners_ref, lscale_ref, gscale_ref,
    byte_hbm, state_ref,
    xv, wqkv, wo, up, down, ppw, gqkv, gout, back,
    xps, normed, act, part, ppf, bsend, bfar, brecv, ownf, ppsend, pprecv, ppown, pin,
    mixed_qkv, qkvs, kvbuf, qbuf, m_ref, l_ref, acc, opart, oget, stpart, stget, osend, orecv, rfar, rsend, rrecv, bst, psend, byte_ref,
    lsem, x_sem, pp_s, pp_r, ag_s, ag_r, an_r, bf_r, bk_s, bk_r, x_s, xk_r, xq_r,
    yu_s, yu_r, yd_s, yd_r, ru_s, ru_r, rd_s, rd_r, c_s, c_r, o_r, rf_r, r_s, r_r, p_s, p_r,
):
    s = lax.axis_index("seq")
    z = lax.axis_index("head")
    core = lax.rem(s, 2)
    x = lax.rem(s // 2, XN)
    y = s // (2 * XN)
    rows = xv.shape[0] // CHUNKS
    span = rows // 8
    own = 2 * span

    def seq_of(yy, xx, cc):
        return (yy * XN + xx) * 2 + cc

    def zpeer(d):
        return (s, lax.rem(z + d, ZN))

    def xpeer(d):
        return (seq_of(y, lax.rem(x + d, XN), core), z)

    y_up = (seq_of(lax.rem(y + 1, YN), x, core), z)
    y_down = (seq_of(lax.rem(y + YN - 1, YN), x, core), z)
    sibling = (seq_of(y, x, 1 - core), z)

    loads = [
        pltpu.make_async_copy(a, b, lsem.at[i])
        for i, (a, b) in enumerate(
            ((wqkv_hbm, wqkv), (up_hbm, up), (wo_hbm, wo), (down_hbm, down), (pp_hbm, ppw),
             (gqkv_hbm, gqkv), (gout_hbm, gout), (back_hbm, back))
        )
    ]
    def xload(c):
        at = pl.ds(pl.multiple_of(c * rows, rows), rows)
        return pltpu.make_async_copy(x_hbm.at[at], xv.at[at], x_sem.at[c])

    xload(0).start()
    for load in loads[:5]:
        load.start()
    for c in range(1, CHUNKS):
        xload(c).start()

    barrier = pltpu.get_barrier_semaphore()
    plane = 2 * XN * YN

    def greet(peer):
        pl.semaphore_signal(barrier, inc=1, device_id=peer, device_id_type=MESH)

    def greet_plane(d, carry):
        greet((lax.rem(s + d, plane), z))
        return carry

    for d in (1, 2, 3):
        greet(zpeer(d))
    lax.fori_loop(1, plane, greet_plane, 0)

    def remote(src, dst, ss, rs, peer):
        return pltpu.make_async_remote_copy(
            src_ref=src, dst_ref=dst, send_sem=ss, recv_sem=rs, device_id=peer, device_id_type=MESH
        )

    def pp_copy(c, d):
        return remote(
            ppsend.at[c, lax.rem(z + d, ZN)], pprecv.at[c, d - 1], pp_s.at[0], pp_r.at[c], zpeer(d)
        )

    def ag_copy(c, d):
        rs = an_r.at[c] if d == ZN - 1 else ag_r.at[d - 1]
        return remote(pin.at[z, c], pin.at[z, c], ag_s.at[0], rs, zpeer(d))

    def ag_relay(c):
        at = pin.at[up_at, c]
        arrived(at, an_r.at[c])
        remote(at, at, ag_s.at[0], ag_r.at[1], z_down).start()

    z_up = zpeer(1)
    z_down = zpeer(ZN - 1)
    up_at = lax.rem(z + 1, ZN)
    down_at = lax.rem(z + ZN - 1, ZN)
    far_at = lax.rem(z + 2, ZN)

    def bulk_far(c):
        return (
            remote(bsend.at[c, far_at, 0], bfar.at[c, 0], bk_s.at[0], bf_r.at[0], z_up),
            remote(bsend.at[c, far_at, 1], bfar.at[c, 1], bk_s.at[0], bf_r.at[0], z_down),
        )

    def bulk_up(c, b):
        return remote(bsend.at[c, up_at, b], brecv.at[c, 0, b], bk_s.at[0], bk_r.at[0], z_up)

    def bulk_down(c, b):
        return remote(bsend.at[c, down_at, b], brecv.at[c, 1, b], bk_s.at[0], bk_r.at[0], z_down)

    def bulk_combine(c, carry):
        bsend[c, up_at, 0] = (bsend[c, up_at, 0].astype(F32) + bfar[c, 0].astype(F32)).astype(BF16)
        bulk_up(c, 0).start()
        bsend[c, down_at, 1] = (bsend[c, down_at, 1].astype(F32) + bfar[c, 1].astype(F32)).astype(BF16)
        bulk_down(c, 1).start()
        return carry

    def arrived(ref, sem):
        pltpu.make_async_copy(ref, ref, sem).wait()

    def finish_patches(c, last_one=False):
        total = ppown[c]
        arrived(pprecv.at[c], pp_r.at[c])
        for d in (1, 2, 3):
            total = total + pprecv[c, d - 1].astype(F32)
        pin[z, c] = total.astype(BF16)
        for d in (2, 1, 3) if last_one else (1, 3):
            ag_copy(c, d).start()

    row_i = lax.broadcasted_iota(jnp.int32, (rows, rows), 0)
    col_i = lax.broadcasted_iota(jnp.int32, (rows, rows), 1)
    to_byte_major = jnp.where(
        col_i == lax.rem(row_i, span) * 8 + row_i // span, 1.0, 0.0
    ).astype(BF16)

    def prepare(c, slot):
        xp = dot(to_byte_major, xv[pl.ds(pl.multiple_of(c * rows, rows), rows), :])
        xps[slot] = xp.astype(BF16)
        normed[slot] = (
            xp * lax.rsqrt(jnp.mean(xp * xp, axis=-1, keepdims=True) + EPS) * gain_ref[...]
        ).astype(BF16)

    def gelu(v):
        inner = v * (0.7978845608028654 + (0.7978845608028654 * 0.044715) * (v * v))
        half = 0.5 * v
        return (half + half * jnp.tanh(inner)).astype(BF16)

    rr = lax.broadcasted_iota(jnp.int32, (rows, rows), 0)
    cc = lax.broadcasted_iota(jnp.int32, (rows, rows), 1)
    seen = (lax.rem(rr, span) == lax.rem(cc, span)) & (cc // span <= rr // span)

    def chunk(c, ahead, first=False):
        slot = lax.rem(c, 2)
        nv = normed[slot]
        tiles = [slice(n * 256, (n + 1) * 256) for n in range(up.shape[1] // 256)]
        cuts = [slice(h * HD, (h + 1) * HD) for h in range(2)]
        q2 = dot(nv, wqkv[0])
        k2 = dot(nv, wqkv[1])
        v2 = dot(nv, wqkv[2]).astype(BF16)
        hidden = dot(nv, up[:, tiles[0]])
        qs = [unit(q2[:, cut]).astype(BF16) for cut in cuts]
        ks = [unit(k2[:, cut]).astype(BF16) for cut in cuts]
        later = dot(nv, up[:, tiles[1]])
        scores = [dot_t(qs[h], ks[h]) for h in range(2)]
        act[:, tiles[0]] = gelu(hidden)
        hidden = dot(nv, up[:, tiles[2]])
        es, totals = [], []
        for h in range(2):
            sc = jnp.where(seen, scores[h] * (lscale_ref[h] / math.sqrt(HD)), NEG)
            e = jnp.exp(sc - jnp.max(sc, axis=-1, keepdims=True))
            totals.append(jnp.sum(e, axis=-1, keepdims=True))
            es.append(e.astype(BF16))
        act[:, tiles[1]] = gelu(later)
        later = dot(nv, up[:, tiles[3]])
        heads = [(dot(es[h], v2[:, cuts[h]]) / totals[h]).astype(BF16) for h in range(2)]
        lo = jnp.concatenate(heads, axis=1)
        act[:, tiles[2]] = gelu(hidden)
        act[:, tiles[3]] = gelu(later)
        if ahead is not None:
            xload(ahead).wait()
            prepare(ahead, 1 - slot)
        if first:
            for load in loads[2:5]:
                load.wait()
            for load in loads[5:]:
                load.start()
        mine = lax.broadcasted_iota(jnp.int32, (rows, 1), 0) // own == z
        a = act[...]
        for cut in tiles:
            t = dot(lo, wo[:, cut]) + dot(a, down[:, cut])
            t = t + jnp.where(mine, xps[slot, :, cut].astype(F32), 0.0)
            part[:, cut] = t
            tb = t.astype(BF16)
            for h in range(ZN):
                for b in range(2):
                    at = h * own + b * span
                    bsend[c, h, b, :, cut] = tb[at : at + span]
        ownf[c] = part[pl.ds(pl.multiple_of(z * own, own), own), :]
        pp = dot(bsend[c].reshape(rows, part.shape[1]), ppw[...])
        ppf[...] = pp
        pb = pp.astype(BF16)
        gp = pp.shape[1]
        for h in range(ZN):
            for b in range(2):
                at = (2 * h + b) * span
                ppsend[c, h, :, b * gp : (b + 1) * gp] = pb[at : at + span]
        for b in range(2):
            at = pl.multiple_of(z * own + b * span, span)
            ppown[c, :, b * gp : (b + 1) * gp] = ppf[pl.ds(at, span), :]

        @pl.when(c == 0)
        def _():
            pl.semaphore_wait(barrier, ZN - 1 + plane - 1)

        for d in (2, 1, 3):
            pp_copy(c, d).start()

        @pl.when(c >= 1)
        def _():
            finish_patches(c - 1)

        @pl.when(c >= 2)
        def _():
            ag_relay(c - 2)


    xload(0).wait()
    prepare(jnp.int32(0), 0)
    for load in loads[:2]:
        load.wait()

    def chunk_step(c, carry):
        chunk(c, c + 1)
        return carry

    chunk(jnp.int32(0), jnp.int32(1), True)
    lax.fori_loop(1, CHUNKS - 1, chunk_step, 0)
    chunk(jnp.int32(CHUNKS - 1), None)
    finish_patches(CHUNKS - 1, True)
    ag_relay(CHUNKS - 2)
    loads[5].wait()
    patches = CHUNKS * span
    piece = pin.shape[3]
    square = jnp.zeros((patches, 1), F32)
    for d in (0, 1, 3, 2):
        h = lax.rem(z + ZN - d, ZN)
        if d:
            if d == ZN - 1:
                arrived(pin.at[h, CHUNKS - 1], an_r.at[CHUNKS - 1])
            else:
                arrived(pin.at[h], ag_r.at[d - 1])
        if d == 2:
            for c in range(CHUNKS):
                for copy in bulk_far(c):
                    copy.start()
            for c in range(CHUNKS):
                bulk_up(c, 1).start()
                bulk_down(c, 0).start()
        at = pl.ds(pl.multiple_of(h * piece, piece), piece)
        v = pin[h].reshape(patches, piece).astype(F32)
        square = square + jnp.sum(v * v, axis=-1, keepdims=True)
        g = (v * ggain_ref[:, at]).astype(BF16)
        for j in (1, 2, 0):
            for half in range(2):
                cut = slice(half * 256, (half + 1) * 256)
                r = dot(g, gqkv[j, at, cut])
                mixed_qkv[j, :, cut] = r if d == 0 else mixed_qkv[j, :, cut] + r
    inv = lax.rsqrt(square / (ZN * piece) + EPS)

    def project(j):
        for t in range(XN):
            v = mixed_qkv[j, :, t * HD : (t + 1) * HD] * inv
            if j < 2:
                v = unit(v)
            if j == 2:
                v = jnp.transpose(v)
            qkvs[t, j] = v.astype(BF16)

    def xk_copy(d):
        h = lax.rem(x + d, XN)
        return remote(qkvs.at[h, pl.ds(1, 2)], kvbuf.at[y, x], x_s.at[0], xk_r.at[d - 1], xpeer(d))

    def src(d):
        return lax.rem(x + XN - d, XN)

    def xk_arrival(d):
        at = kvbuf.at[y, src(d)]
        return pltpu.make_async_copy(at, at, xk_r.at[d - 1])

    def xq_copy(d):
        h = lax.rem(x + d, XN)
        return remote(qkvs.at[h, 0], qbuf.at[0, x], x_s.at[0], xq_r.at[0], xpeer(d))

    y1 = lax.rem(y + 1, YN)
    y2 = lax.rem(y + 2, YN)
    y3 = lax.rem(y + 3, YN)

    def up_copy(row, d, ss, rs):
        at = kvbuf.at[row, src(d)]
        return remote(at, at, ss.at[d], rs.at[d], y_up)

    def down_copy(row, d, ss, rs):
        at = kvbuf.at[row, src(d)]
        return remote(at, at, ss.at[d], rs.at[d], y_down)

    def relay_up(row, d):
        at = kvbuf.at[row, src(d)]
        return remote(at, at, ru_s.at[d // 2], ru_r.at[d // 2], y_up)

    def relay_down(row, d):
        at = kvbuf.at[row, src(d)]
        return remote(at, at, rd_s.at[d // 2], rd_r.at[d // 2], y_down)

    last = YN - 1
    inner = (y >= 1) & (y < last)
    outer = (y == 0) | (y == last)

    def spread_piece(d, act_on):
        @pl.when(y < last)
        def _():
            act_on(up_copy(y, d, yu_s, yu_r))

        @pl.when((y == 0) | ((y == 1) & (d % 2 == 1)))
        def _():
            act_on(down_copy(y, d, yd_s, yd_r))

    def start(copy):
        copy.start()

    def sent(copy):
        copy.wait_send()

    def take_down(d):
        @pl.when(y >= 1)
        def _():
            up_copy(y3, d, yu_s, yu_r).wait_recv()

        if d % 2 == 0:

            @pl.when(inner)
            def _():
                relay_up(y3, d).start()

    def take_up(d):
        @pl.when((y == last) | ((y == 0) & (d % 2 == 1)))
        def _():
            down_copy(y1, d, yd_s, yd_r).wait_recv()

        if d % 2 == 1:

            @pl.when(outer)
            def _():
                relay_down(y1, d).start()

    def take_far():
        @pl.when(y >= 2)
        def _():
            for d in (0, 2):
                relay_up(y2, d).wait_recv()
            for d in (1, 3):
                relay_down(y2, d).wait_recv()

    q_give = remote(qbuf.at[0], qbuf.at[1], c_s.at[0], c_r.at[0], sibling)
    o_give = remote(opart, oget, c_s.at[1], c_r.at[1], sibling)
    st_give = remote(stpart, stget, c_s.at[2], c_r.at[2], sibling)

    project(1)
    project(2)
    for d in (2, 1, 3):
        xk_copy(d).start()
    kvbuf[y, x] = qkvs[x, 1:3]
    spread_piece(0, start)
    project(0)
    for d in (2, 1, 3):
        xq_copy(d).start()
    qbuf[0, x] = qkvs[x, 0]
    m_ref[...] = jnp.full(m_ref.shape, NEG, F32)
    l_ref[...] = jnp.zeros(l_ref.shape, F32)
    acc[...] = jnp.zeros(acc.shape, F32)
    factor = gscale_ref[x] * (math.log2(math.e) / math.sqrt(HD))

    for d in (3, 1, 2):
        xk_arrival(d).wait()
        spread_piece(d, start)
    arrived(qbuf.at[0, pl.ds(0, XN - 1)], xq_r.at[0])
    q_give.start()

    half_q = XN * patches // 2

    def attend(yb, rels, masked):
        chains = [(rel, part_q) for rel in rels for part_q in range(2)]

        def raw(chain):
            rel, part_q = chain
            wide = (part_q + 1) * XN // 2 if masked else XN
            queries = qbuf[rel].reshape(XN * patches, HD)[part_q * half_q : (part_q + 1) * half_q]
            scores = dot_t(kvbuf[yb, 0:wide, 0].reshape(wide * patches, HD), queries)
            if masked:
                kk = lax.broadcasted_iota(jnp.int32, scores.shape, 0)
                qq = lax.broadcasted_iota(jnp.int32, scores.shape, 1) + part_q * half_q
                theirs = core + rel * (1 - 2 * core)
                k_at = kk + (kk // patches + core) * patches
                q_at = qq + (qq // patches + theirs) * patches
                scores = jnp.where(k_at <= q_at, scores, NEG)
            return scores

        def fold(op, v):
            return op(op(v.reshape(8, v.shape[0] // 8, v.shape[1]), axis=0), axis=0, keepdims=True)

        upcoming = raw(chains[0])
        for i, (rel, part_q) in enumerate(chains):
            scores = upcoming
            if i + 1 < len(chains):
                upcoming = raw(chains[i + 1])
            cut = slice(part_q * half_q, (part_q + 1) * half_q)
            old = m_ref[rel, :, cut]
            new = jnp.maximum(old, fold(jnp.max, scores))
            keep = jnp.exp2((old - new) * factor)
            e = jnp.exp2((scores - new) * factor)
            m_ref[rel, :, cut] = new
            l_ref[rel, :, cut] = l_ref[rel, :, cut] * keep + fold(jnp.sum, e)
            wide = scores.shape[0] // patches
            vt = jnp.concatenate([kvbuf[yb, k, 1] for k in range(wide)], axis=1)
            acc[rel, :, cut] = acc[rel, :, cut] * keep + dot(vt, e.astype(BF16))

    def run(yb, rels):
        @pl.when(yb < y)
        def _():
            attend(yb, rels, False)


    attend(y, (0,), True)
    take_down(0)
    take_up(0)
    q_give.wait_recv()
    attend(y, (1,), True)
    for d in (3, 1, 2):
        take_up(d)
        take_down(d)
    run(y3, (1, 0))
    run(y1, (1, 0))
    arrived(bfar, bf_r.at[0])
    lax.fori_loop(0, CHUNKS, bulk_combine, 0)
    take_far()
    run(y2, (1,))
    opart[...] = (acc[1] / l_ref[1]).astype(BF16)
    stpart[...] = jnp.zeros(stpart.shape, F32)
    stpart[0:1] = m_ref[1]
    stpart[1:2] = l_ref[1]
    o_give.start()
    st_give.start()
    run(y2, (0,))
    o_give.wait_recv()
    st_give.wait_recv()
    m0, m1 = m_ref[0], stget[0:1]
    top = jnp.maximum(m0, m1)
    w0 = jnp.exp2((m0 - top) * factor)
    w1 = jnp.exp2((m1 - top) * factor) * stget[1:2]
    mixed = (acc[0] * w0 + oget[...].astype(F32) * w1) / (l_ref[0] * w0 + w1)
    for qb in range(XN):
        osend[qb] = jnp.transpose(mixed[:, qb * patches : (qb + 1) * patches]).astype(BF16)

    def o_copy(d):
        h = lax.rem(x + d, XN)
        return remote(osend.at[h], orecv.at[x], x_s.at[0], o_r.at[0], xpeer(d))

    for d in (2, 1, 3):
        o_copy(d).start()
    orecv[x] = osend[x]
    loads[6].wait()
    arrived(orecv.at[pl.ds(0, XN - 1)], o_r.at[0])
    gattn = jnp.concatenate([orecv[h] for h in range(XN)], axis=1)

    def out_part(zz):
        return dot(gattn, gout[:, pl.ds(pl.multiple_of(zz * piece, piece), piece)])

    half_p = patches // 2
    low, high = slice(0, half_p), slice(half_p, patches)
    far_up = remote(rsend.at[2, 0], rfar.at[0], r_s.at[0], rf_r.at[0], z_up)
    far_down = remote(rsend.at[2, 1], rfar.at[1], r_s.at[0], rf_r.at[1], z_down)

    def r_up(b):
        return remote(rsend.at[0, b], rrecv.at[0, b], r_s.at[0], r_r.at[0], z_up)

    def r_down(b):
        return remote(rsend.at[1, b], rrecv.at[1, b], r_s.at[0], r_r.at[0], z_down)

    far_part = out_part(far_at).astype(BF16)
    rsend[2, 0] = far_part[low]
    far_up.start()
    rsend[2, 1] = far_part[high]
    far_down.start()
    up_part = out_part(up_at)
    rsend[0, 1] = up_part[high].astype(BF16)
    down_part = out_part(down_at)
    rsend[1, 0] = down_part[low].astype(BF16)
    update = out_part(z)

    ri = lax.broadcasted_iota(jnp.int32, (own, own), 0)
    ci = lax.broadcasted_iota(jnp.int32, (own, own), 1)
    to_patch_major = jnp.where(ci == lax.rem(ri, 2) * span + ri // 2, 1.0, 0.0).astype(BF16)
    arrived(brecv, bk_r.at[0])
    for c in range(CHUNKS):
        state = jnp.concatenate(
            [
                ownf[c, b * span : (b + 1) * span] + brecv[c, 0, b].astype(F32) + brecv[c, 1, b].astype(F32)
                for b in range(2)
            ],
            axis=0,
        ).astype(BF16)
        bst[c * own : (c + 1) * own] = dot(to_patch_major, state).astype(BF16)

    r_up(1).start()
    r_down(0).start()
    sources, blocks = owners_ref.shape
    spread = jnp.where(
        lax.broadcasted_iota(jnp.int32, (blocks, patches), 1) // 2
        == lax.broadcasted_iota(jnp.int32, (blocks, patches), 0),
        1.0,
        0.0,
    ).astype(BF16)
    listed = dot(owners_ref[...].astype(F32).astype(BF16), spread)
    is_mine = lax.broadcasted_iota(jnp.int32, listed.shape, 0) == s
    listed_row = jnp.sum(jnp.where(is_mine, listed, 0.0), axis=0, keepdims=True)
    pr = lax.broadcasted_iota(jnp.int32, (patches, patches), 0)
    pc = lax.broadcasted_iota(jnp.int32, (patches, patches), 1)
    listed_col = jnp.sum(jnp.where(pr == pc, listed_row, 0.0), axis=1, keepdims=True)
    earlier = (listed_col == listed_row) & (pr < pc) & (lax.rem(pr, 2) == lax.rem(pc, 2))
    rank = jnp.sum(jnp.where(earlier, 1.0, 0.0), axis=0, keepdims=True)
    slot = listed_row * 4.0 + rank * 2.0 + lax.rem(pc, 2).astype(F32)
    pick = jnp.where(slot == pr.astype(F32), 1.0, 0.0).astype(BF16)

    per = patches // plane
    loads[7].wait()
    far_up.wait_recv()
    rsend[0, 0] = (up_part[low] + rfar[0].astype(F32)).astype(BF16)
    r_up(0).start()
    far_down.wait_recv()
    rsend[1, 1] = (down_part[high] + rfar[1].astype(F32)).astype(BF16)
    r_down(1).start()
    arrived(rrecv, r_r.at[0])
    total = update + pin[z].reshape(patches, piece).astype(F32)
    total = total + jnp.concatenate(
        [rrecv[0, b].astype(F32) + rrecv[1, b].astype(F32) for b in range(2)], axis=0
    )
    result = total.astype(BF16)
    sorted_rows = dot(pick, result)
    for o in range(plane):
        psend[o] = sorted_rows[o * per : (o + 1) * per].astype(BF16)

    def p_copy(dy, dx, dc):
        to = seq_of(lax.rem(y + dy, YN), lax.rem(x + dx, XN), lax.rem(core + dc, 2))
        return remote(psend.at[to], state_ref.at[s], p_s.at[0], p_r.at[0], (to, z))

    hops = [0, 1, 2, 1]
    turns = [(dy, dx, dc) for dy in range(YN) for dx in range(XN) for dc in range(2) if dy or dx or dc]
    for dy, dx, dc in sorted(turns, key=lambda turn: -hops[turn[0]] - hops[turn[1]]):
        p_copy(dy, dx, dc).start()
    keep_own = pltpu.make_async_copy(psend.at[s], state_ref.at[s], lsem.at[9])
    keep_own.start()
    gp = back.shape[0]
    re = lax.broadcasted_iota(jnp.int32, (2 * patches, patches), 0)
    ce = lax.broadcasted_iota(jnp.int32, (2 * patches, patches), 1)
    shares = jnp.zeros((2 * patches, gp), F32)
    for b in range(2):
        lift = jnp.where(re == 2 * ce + b, 1.0, 0.0).astype(BF16)
        shares = shares + dot(lift, result[:, b * gp : (b + 1) * gp])
    shares = shares.astype(BF16)
    for n in range(bst.shape[1] // 256):
        cut = slice(n * 256, (n + 1) * 256)
        both = bst[:, cut].astype(F32) + dot(shares, back[:, cut])
        byte_ref[:, :, cut] = both.astype(BF16).reshape(patches, 2, 256)

    byte_put = pltpu.make_async_copy(byte_ref, byte_hbm, lsem.at[8])
    byte_put.start()
    arrived(state_ref.at[pl.ds(0, plane - 1)], p_r.at[0])

    byte_put.wait()
    keep_own.wait()
    arrived(psend.at[pl.ds(0, plane - 1)], p_s.at[0])
    arrived(ppsend.at[pl.ds(0, ZN - 1)], pp_s.at[0])
    arrived(pin.at[pl.ds(0, ZN - 1)], ag_s.at[0])
    arrived(bsend.at[pl.ds(0, ZN - 1)], bk_s.at[0])
    arrived(qkvs, x_s.at[0])
    arrived(rsend, r_s.at[0])
    for d in range(XN):
        spread_piece(d, sent)

    @pl.when(inner)
    def _():
        for d in (0, 2):
            relay_up(y3, d).wait_send()

    @pl.when(outer)
    def _():
        for d in (1, 3):
            relay_down(y1, d).wait_send()

    for copy in (q_give, o_give, st_give):
        copy.wait_send()


def settle(a_hbm, b_hbm, a_out, b_out, va, vb, wb, in_sem, out_sem):
    cut = va.shape[0] // 4
    takes, puts = [], []
    for i in range(4):
        at = pl.ds(i * cut, cut)
        takes.append(pltpu.make_async_copy(a_hbm.at[at], va.at[at], in_sem.at[i]))
        puts.append(pltpu.make_async_copy(va.at[at], a_out.at[at], out_sem.at[i]))
    last = pltpu.make_async_copy(b_hbm, vb, in_sem.at[4])
    put_last = pltpu.make_async_copy(wb, b_out, out_sem.at[4])
    last.start()
    for take in takes:
        take.start()
    last.wait()
    wb[...] = jnp.concatenate([vb[o].astype(F32) for o in range(vb.shape[0])], axis=0).astype(BF16)
    put_last.start()
    for take, put in zip(takes, puts):
        take.wait()
        put.start()
    for put in puts:
        put.wait()
    put_last.wait()


def on_device(
    byte_in, local_gain, local_qkv, local_out, mlp_up, mlp_down, local_scale, patch_proj,
    global_gain, global_qkv, global_out, global_scale, back_proj, owners,
):
    patches, span8, dl = byte_in.shape
    gw = global_out.shape[1]
    piece = gw // ZN
    ff = mlp_up.shape[1]
    rows = patches * span8 // CHUNKS
    span = patches // CHUNKS
    own = 2 * span
    gp = back_proj.shape[0]
    plane = 2 * XN * YN
    wqkv3 = jnp.transpose(local_qkv, (1, 0, 2))
    gqkv3 = jnp.transpose(global_qkv, (1, 0, 2))
    hbm = pl.BlockSpec(memory_space=pl.ANY)
    vm = pl.BlockSpec(memory_space=pltpu.VMEM)
    sm = pl.BlockSpec(memory_space=pltpu.SMEM)
    dma = pltpu.SemaphoreType.DMA

    def buf(*shape, dtype=BF16):
        return pltpu.VMEM(shape, dtype)

    big = [byte_in.reshape(patches * span8, dl), wqkv3, local_out, mlp_up, mlp_down, patch_proj, gqkv3, global_out, back_proj]
    scratch = [buf(*a.shape) for a in big] + [
        buf(2, rows, dl),
        buf(2, rows, dl),
        buf(rows, ff),
        buf(rows, dl, dtype=F32),
        buf(rows, gp, dtype=F32),
        buf(CHUNKS, ZN, 2, span, dl),
        buf(CHUNKS, 2, span, dl),
        buf(CHUNKS, 2, 2, span, dl),
        buf(CHUNKS, own, dl, dtype=F32),
        buf(CHUNKS, ZN, span, 2 * gp),
        buf(CHUNKS, ZN - 1, span, 2 * gp),
        buf(CHUNKS, span, 2 * gp, dtype=F32),
        buf(ZN, CHUNKS, span, piece),
        buf(3, patches, piece, dtype=F32),
        buf(XN, 3, patches, HD),
        buf(YN, XN, 2, patches, HD),
        buf(2, XN, patches, HD),
        buf(2, 1, XN * patches, dtype=F32),
        buf(2, 1, XN * patches, dtype=F32),
        buf(2, HD, XN * patches, dtype=F32),
        buf(HD, XN * patches),
        buf(HD, XN * patches),
        buf(8, XN * patches, dtype=F32),
        buf(8, XN * patches, dtype=F32),
        buf(XN, patches, HD),
        buf(XN, patches, HD),
        buf(2, patches // 2, piece),
        buf(3, 2, patches // 2, piece),
        buf(2, 2, patches // 2, piece),
        buf(2 * patches, dl),
        buf(plane, patches // plane, piece),
        buf(patches, 2, dl),
        dma((10,)),
        dma((CHUNKS,)),
    ]
    counts = (1, CHUNKS, 1, 3, CHUNKS, 1, 1, 1, 1, 3, 1, 4, 4, 4, 4, 2, 2, 2, 2, 3, 3, 1, 2, 1, 1, 1, 1)
    scratch += [dma((n,)) for n in counts]
    byte_out, global_state = pl.pallas_call(
        kernel,
        out_shape=(
            jax.ShapeDtypeStruct((patches, 2, dl), BF16),
            jax.ShapeDtypeStruct((plane, patches // plane, piece), BF16),
        ),
        in_specs=[hbm] * 9 + [vm] * 3 + [sm] * 2,
        out_specs=(hbm, hbm),
        scratch_shapes=scratch,
        compiler_params=pltpu.CompilerParams(
            collective_id=0, has_side_effects=True, vmem_limit_bytes=60 * 1024 * 1024
        ),
    )(*big, local_gain.reshape(1, dl), global_gain.reshape(1, gw), owners, local_scale, global_scale)
    return pl.pallas_call(
        settle,
        out_shape=(
            jax.ShapeDtypeStruct(byte_out.shape, BF16),
            jax.ShapeDtypeStruct((patches, piece), BF16),
        ),
        in_specs=[hbm] * 2,
        out_specs=(hbm, hbm),
        scratch_shapes=[buf(*byte_out.shape), buf(*global_state.shape), buf(patches, piece), dma((5,)), dma((5,))],
    )(byte_out, global_state)


def solution(mesh):
    placed = (
        P("seq", None, None),
        P(),
        P(None, None, "head"),
        P("head", None),
        P(None, "head"),
        P("head", None),
        P("head"),
        P(),
        P(),
        P(None, None, "head"),
        P("head", None),
        P("head"),
        P(),
        P(),
    )
    return jax.shard_map(
        on_device,
        mesh=mesh,
        in_specs=placed,
        out_specs=(P("seq", "head", None), P("seq", "head")),
        check_vma=False,
    )
```

```python
import functools
import math

import jax
import jax.numpy as jnp
from jax import lax
from jax.experimental import pallas as pl
from jax.experimental.pallas import tpu as pltpu
from jax.sharding import PartitionSpec as P

EPS = 1e-06
NEG = -1e30
MESH = pl.DeviceIdType.MESH
F32 = jnp.float32
BF16 = jnp.bfloat16
XN = 4
YN = 4
ZN = 4
CHUNKS = 4
HD = 128
UPWARD = (0, 3)
DOWNWARD = (1, 2)


def dot(a, b):
    return jnp.dot(a, b, preferred_element_type=F32)


def dot_t(a, b):
    return lax.dot_general(a, b, (((1,), (1,)), ((), ())), preferred_element_type=F32)


def unit(v):
    return v * lax.rsqrt(jnp.mean(v * v, axis=-1, keepdims=True) + EPS)


def kernel(
    x_hbm, wqkv_hbm, wo_hbm, up_hbm, down_hbm, pp_hbm, gqkv_hbm, gout_hbm, back_hbm,
    gain_ref, ggain_ref, owners_ref, lscale_ref, gscale_ref,
    byte_hbm, state_ref,
    xv, wqkv, wo, up, down, ppw, gqkv, gout, back,
    xps, normed, act, part, ppf, bsend, bfar, brecv, ownf, ppsend, pprecv, ppown, pin,
    mixed_qkv, qkvs, kvbuf, qbuf, m_ref, l_ref, acc, opart, oget, stpart, stget, osend, orecv, rfar, rsend, rrecv, bst, psend, byte_ref,
    lsem, x_sem, pp_s, pp_r, ag_s, ag_r, an_r, bf_r, bk_s, bk_r, x_s, xk_r, xq_r,
    yu_s, yu_r, yd_s, yd_r, ru_s, ru_r, rd_s, rd_r, c_s, c_r, o_r, rf_r, r_s, r_r, p_s, p_r,
):
    s = lax.axis_index("seq")
    z = lax.axis_index("head")
    core = lax.rem(s, 2)
    x = lax.rem(s // 2, XN)
    y = s // (2 * XN)
    rows = xv.shape[0] // CHUNKS
    span = rows // 8
    own = 2 * span

    def seq_of(yy, xx, cc):
        return (yy * XN + xx) * 2 + cc

    def zpeer(d):
        return (s, lax.rem(z + d, ZN))

    def xpeer(d):
        return (seq_of(y, lax.rem(x + d, XN), core), z)

    y_up = (seq_of(lax.rem(y + 1, YN), x, core), z)
    y_down = (seq_of(lax.rem(y + YN - 1, YN), x, core), z)
    sibling = (seq_of(y, x, 1 - core), z)

    loads = [
        pltpu.make_async_copy(a, b, lsem.at[i])
        for i, (a, b) in enumerate(
            ((wqkv_hbm, wqkv), (up_hbm, up), (wo_hbm, wo), (down_hbm, down), (pp_hbm, ppw),
             (gqkv_hbm, gqkv), (gout_hbm, gout), (back_hbm, back))
        )
    ]
    def xload(c):
        at = pl.ds(pl.multiple_of(c * rows, rows), rows)
        return pltpu.make_async_copy(x_hbm.at[at], xv.at[at], x_sem.at[c])

    xload(0).start()
    for load in loads[:5]:
        load.start()
    for c in range(1, CHUNKS):
        xload(c).start()

    barrier = pltpu.get_barrier_semaphore()
    plane = 2 * XN * YN

    def greet(peer):
        pl.semaphore_signal(barrier, inc=1, device_id=peer, device_id_type=MESH)

    def greet_plane(d, carry):
        greet((lax.rem(s + d, plane), z))
        return carry

    for d in (1, 2, 3):
        greet(zpeer(d))
    lax.fori_loop(1, plane, greet_plane, 0)

    def remote(src, dst, ss, rs, peer):
        return pltpu.make_async_remote_copy(
            src_ref=src, dst_ref=dst, send_sem=ss, recv_sem=rs, device_id=peer, device_id_type=MESH
        )

    def pp_copy(c, d):
        return remote(
            ppsend.at[c, lax.rem(z + d, ZN)], pprecv.at[c, d - 1], pp_s.at[0], pp_r.at[c], zpeer(d)
        )

    def ag_copy(c, d):
        rs = an_r.at[c] if d == ZN - 1 else ag_r.at[d - 1]
        return remote(pin.at[z, c], pin.at[z, c], ag_s.at[0], rs, zpeer(d))

    def ag_relay(c):
        at = pin.at[up_at, c]
        arrived(at, an_r.at[c])
        remote(at, at, ag_s.at[0], ag_r.at[1], z_down).start()

    z_up = zpeer(1)
    z_down = zpeer(ZN - 1)
    up_at = lax.rem(z + 1, ZN)
    down_at = lax.rem(z + ZN - 1, ZN)
    far_at = lax.rem(z + 2, ZN)

    def bulk_far(c):
        return (
            remote(bsend.at[c, far_at, 0], bfar.at[c, 0], bk_s.at[0], bf_r.at[0], z_up),
            remote(bsend.at[c, far_at, 1], bfar.at[c, 1], bk_s.at[0], bf_r.at[0], z_down),
        )

    def bulk_up(c, b):
        return remote(bsend.at[c, up_at, b], brecv.at[c, 0, b], bk_s.at[0], bk_r.at[0], z_up)

    def bulk_down(c, b):
        return remote(bsend.at[c, down_at, b], brecv.at[c, 1, b], bk_s.at[0], bk_r.at[0], z_down)

    def bulk_combine(c, carry):
        bsend[c, up_at, 0] = (bsend[c, up_at, 0].astype(F32) + bfar[c, 0].astype(F32)).astype(BF16)
        bulk_up(c, 0).start()
        bsend[c, down_at, 1] = (bsend[c, down_at, 1].astype(F32) + bfar[c, 1].astype(F32)).astype(BF16)
        bulk_down(c, 1).start()
        return carry

    def arrived(ref, sem):
        pltpu.make_async_copy(ref, ref, sem).wait()

    def finish_patches(c, last_one=False):
        total = ppown[c]
        arrived(pprecv.at[c], pp_r.at[c])
        for d in (1, 2, 3):
            total = total + pprecv[c, d - 1].astype(F32)
        pin[z, c] = total.astype(BF16)
        for d in (2, 1, 3) if last_one else (1, 3):
            ag_copy(c, d).start()

    row_i = lax.broadcasted_iota(jnp.int32, (rows, rows), 0)
    col_i = lax.broadcasted_iota(jnp.int32, (rows, rows), 1)
    to_byte_major = jnp.where(
        col_i == lax.rem(row_i, span) * 8 + row_i // span, 1.0, 0.0
    ).astype(BF16)

    def prepare(c, slot):
        xp = dot(to_byte_major, xv[pl.ds(pl.multiple_of(c * rows, rows), rows), :])
        xps[slot] = xp.astype(BF16)
        normed[slot] = (
            xp * lax.rsqrt(jnp.mean(xp * xp, axis=-1, keepdims=True) + EPS) * gain_ref[...]
        ).astype(BF16)

    def gelu(v):
        inner = v * (0.7978845608028654 + (0.7978845608028654 * 0.044715) * (v * v))
        half = 0.5 * v
        return (half + half * jnp.tanh(inner)).astype(BF16)

    rr = lax.broadcasted_iota(jnp.int32, (rows, rows), 0)
    cc = lax.broadcasted_iota(jnp.int32, (rows, rows), 1)
    seen = (lax.rem(rr, span) == lax.rem(cc, span)) & (cc // span <= rr // span)

    def chunk(c, ahead, first=False):
        slot = lax.rem(c, 2)
        nv = normed[slot]
        tiles = [slice(n * 256, (n + 1) * 256) for n in range(up.shape[1] // 256)]
        cuts = [slice(h * HD, (h + 1) * HD) for h in range(2)]
        q2 = dot(nv, wqkv[0])
        k2 = dot(nv, wqkv[1])
        v2 = dot(nv, wqkv[2]).astype(BF16)
        hidden = dot(nv, up[:, tiles[0]])
        qs = [unit(q2[:, cut]).astype(BF16) for cut in cuts]
        ks = [unit(k2[:, cut]).astype(BF16) for cut in cuts]
        later = dot(nv, up[:, tiles[1]])
        scores = [dot_t(qs[h], ks[h]) for h in range(2)]
        act[:, tiles[0]] = gelu(hidden)
        hidden = dot(nv, up[:, tiles[2]])
        es, totals = [], []
        for h in range(2):
            sc = jnp.where(seen, scores[h] * (lscale_ref[h] / math.sqrt(HD)), NEG)
            e = jnp.exp(sc - jnp.max(sc, axis=-1, keepdims=True))
            totals.append(jnp.sum(e, axis=-1, keepdims=True))
            es.append(e.astype(BF16))
        act[:, tiles[1]] = gelu(later)
        later = dot(nv, up[:, tiles[3]])
        heads = [(dot(es[h], v2[:, cuts[h]]) / totals[h]).astype(BF16) for h in range(2)]
        lo = jnp.concatenate(heads, axis=1)
        act[:, tiles[2]] = gelu(hidden)
        act[:, tiles[3]] = gelu(later)
        if ahead is not None:
            xload(ahead).wait()
            prepare(ahead, 1 - slot)
        if first:
            for load in loads[2:5]:
                load.wait()
            for load in loads[5:]:
                load.start()
        mine = lax.broadcasted_iota(jnp.int32, (rows, 1), 0) // own == z
        a = act[...]
        for cut in tiles:
            t = dot(lo, wo[:, cut]) + dot(a, down[:, cut])
            t = t + jnp.where(mine, xps[slot, :, cut].astype(F32), 0.0)
            part[:, cut] = t
            tb = t.astype(BF16)
            for h in range(ZN):
                for b in range(2):
                    at = h * own + b * span
                    bsend[c, h, b, :, cut] = tb[at : at + span]
        ownf[c] = part[pl.ds(pl.multiple_of(z * own, own), own), :]
        pp = dot(bsend[c].reshape(rows, part.shape[1]), ppw[...])
        ppf[...] = pp
        pb = pp.astype(BF16)
        gp = pp.shape[1]
        for h in range(ZN):
            for b in range(2):
                at = (2 * h + b) * span
                ppsend[c, h, :, b * gp : (b + 1) * gp] = pb[at : at + span]
        for b in range(2):
            at = pl.multiple_of(z * own + b * span, span)
            ppown[c, :, b * gp : (b + 1) * gp] = ppf[pl.ds(at, span), :]

        @pl.when(c == 0)
        def _():
            pl.semaphore_wait(barrier, ZN - 1 + plane - 1)

        for d in (2, 1, 3):
            pp_copy(c, d).start()

        @pl.when(c >= 1)
        def _():
            finish_patches(c - 1)

        @pl.when(c >= 2)
        def _():
            ag_relay(c - 2)


    xload(0).wait()
    prepare(jnp.int32(0), 0)
    for load in loads[:2]:
        load.wait()

    def chunk_step(c, carry):
        chunk(c, c + 1)
        return carry

    chunk(jnp.int32(0), jnp.int32(1), True)
    lax.fori_loop(1, CHUNKS - 1, chunk_step, 0)
    chunk(jnp.int32(CHUNKS - 1), None)
    finish_patches(CHUNKS - 1, True)
    ag_relay(CHUNKS - 2)
    loads[5].wait()
    patches = CHUNKS * span
    piece = pin.shape[3]
    square = jnp.zeros((patches, 1), F32)
    for d in (0, 1, 3, 2):
        h = lax.rem(z + ZN - d, ZN)
        if d:
            if d == ZN - 1:
                arrived(pin.at[h, CHUNKS - 1], an_r.at[CHUNKS - 1])
            else:
                arrived(pin.at[h], ag_r.at[d - 1])
        if d == 2:
            for c in range(CHUNKS):
                for copy in bulk_far(c):
                    copy.start()
            for c in range(CHUNKS):
                bulk_up(c, 1).start()
                bulk_down(c, 0).start()
        at = pl.ds(pl.multiple_of(h * piece, piece), piece)
        v = pin[h].reshape(patches, piece).astype(F32)
        square = square + jnp.sum(v * v, axis=-1, keepdims=True)
        g = (v * ggain_ref[:, at]).astype(BF16)
        for j in (1, 2, 0):
            for half in range(2):
                cut = slice(half * 256, (half + 1) * 256)
                r = dot(g, gqkv[j, at, cut])
                mixed_qkv[j, :, cut] = r if d == 0 else mixed_qkv[j, :, cut] + r
    inv = lax.rsqrt(square / (ZN * piece) + EPS)

    def project(j):
        for t in range(XN):
            v = mixed_qkv[j, :, t * HD : (t + 1) * HD] * inv
            if j < 2:
                v = unit(v)
            if j == 2:
                v = jnp.transpose(v)
            qkvs[t, j] = v.astype(BF16)

    def xk_copy(d):
        h = lax.rem(x + d, XN)
        return remote(qkvs.at[h, pl.ds(1, 2)], kvbuf.at[y, x], x_s.at[0], xk_r.at[d - 1], xpeer(d))

    def src(d):
        return lax.rem(x + XN - d, XN)

    def xk_arrival(d):
        at = kvbuf.at[y, src(d)]
        return pltpu.make_async_copy(at, at, xk_r.at[d - 1])

    def xq_copy(d):
        h = lax.rem(x + d, XN)
        return remote(qkvs.at[h, 0], qbuf.at[0, x], x_s.at[0], xq_r.at[0], xpeer(d))

    y1 = lax.rem(y + 1, YN)
    y2 = lax.rem(y + 2, YN)
    y3 = lax.rem(y + 3, YN)

    def up_copy(row, d, ss, rs):
        at = kvbuf.at[row, src(d)]
        return remote(at, at, ss.at[d], rs.at[d], y_up)

    def down_copy(row, d, ss, rs):
        at = kvbuf.at[row, src(d)]
        return remote(at, at, ss.at[d], rs.at[d], y_down)

    def relay_up(row, d):
        at = kvbuf.at[row, src(d)]
        return remote(at, at, ru_s.at[d // 2], ru_r.at[d // 2], y_up)

    def relay_down(row, d):
        at = kvbuf.at[row, src(d)]
        return remote(at, at, rd_s.at[d // 2], rd_r.at[d // 2], y_down)

    last = YN - 1
    inner = (y >= 1) & (y < last)
    outer = (y == 0) | (y == last)

    def spread_piece(d, act_on):
        @pl.when(y < last)
        def _():
            act_on(up_copy(y, d, yu_s, yu_r))

        @pl.when((y == 0) | ((y == 1) & (d in DOWNWARD)))
        def _():
            act_on(down_copy(y, d, yd_s, yd_r))

    def start(copy):
        copy.start()

    def sent(copy):
        copy.wait_send()

    def take_down(d):
        @pl.when(y >= 1)
        def _():
            up_copy(y3, d, yu_s, yu_r).wait_recv()

        if d in UPWARD:

            @pl.when(inner)
            def _():
                relay_up(y3, d).start()

    def take_up(d):
        @pl.when((y == last) | ((y == 0) & (d in DOWNWARD)))
        def _():
            down_copy(y1, d, yd_s, yd_r).wait_recv()

        if d in DOWNWARD:

            @pl.when(outer)
            def _():
                relay_down(y1, d).start()

    def take_far_up():
        @pl.when(y >= 2)
        def _():
            for d in UPWARD:
                relay_up(y2, d).wait_recv()

    def take_far_down():
        @pl.when(y >= 2)
        def _():
            for d in DOWNWARD:
                relay_down(y2, d).wait_recv()

    q_give = remote(qbuf.at[0], qbuf.at[1], c_s.at[0], c_r.at[0], sibling)
    o_give = remote(opart, oget, c_s.at[1], c_r.at[1], sibling)
    st_give = remote(stpart, stget, c_s.at[2], c_r.at[2], sibling)

    project(1)
    project(2)
    for d in (2, 1, 3):
        xk_copy(d).start()
    kvbuf[y, x] = qkvs[x, 1:3]
    spread_piece(0, start)
    project(0)
    for d in (2, 1, 3):
        xq_copy(d).start()
    qbuf[0, x] = qkvs[x, 0]
    m_ref[...] = jnp.full(m_ref.shape, NEG, F32)
    l_ref[...] = jnp.zeros(l_ref.shape, F32)
    acc[...] = jnp.zeros(acc.shape, F32)
    factor = gscale_ref[x] * (math.log2(math.e) / math.sqrt(HD))

    for d in (3, 2, 1):
        xk_arrival(d).wait()
        spread_piece(d, start)
    arrived(qbuf.at[0, pl.ds(0, XN - 1)], xq_r.at[0])
    q_give.start()

    half_q = XN * patches // 2

    def attend(yb, rels, masked, picks=None):
        chains = [(rel, part_q) for rel in rels for part_q in range(2)]

        def raw(chain):
            rel, part_q = chain
            wide = (part_q + 1) * XN // 2 if masked else XN
            queries = qbuf[rel].reshape(XN * patches, HD)[part_q * half_q : (part_q + 1) * half_q]
            if picks:
                k = jnp.concatenate([kvbuf[yb, src(d), 0] for d in picks], axis=0)
            else:
                k = kvbuf[yb, 0:wide, 0].reshape(wide * patches, HD)
            scores = dot_t(k, queries)
            if masked:
                kk = lax.broadcasted_iota(jnp.int32, scores.shape, 0)
                qq = lax.broadcasted_iota(jnp.int32, scores.shape, 1) + part_q * half_q
                theirs = core + rel * (1 - 2 * core)
                k_at = kk + (kk // patches + core) * patches
                q_at = qq + (qq // patches + theirs) * patches
                scores = jnp.where(k_at <= q_at, scores, NEG)
            return scores

        def fold(op, v):
            return op(op(v.reshape(8, v.shape[0] // 8, v.shape[1]), axis=0), axis=0, keepdims=True)

        upcoming = raw(chains[0])
        for i, (rel, part_q) in enumerate(chains):
            scores = upcoming
            if i + 1 < len(chains):
                upcoming = raw(chains[i + 1])
            cut = slice(part_q * half_q, (part_q + 1) * half_q)
            old = m_ref[rel, :, cut]
            new = jnp.maximum(old, fold(jnp.max, scores))
            keep = jnp.exp2((old - new) * factor)
            e = jnp.exp2((scores - new) * factor)
            m_ref[rel, :, cut] = new
            l_ref[rel, :, cut] = l_ref[rel, :, cut] * keep + fold(jnp.sum, e)
            wide = scores.shape[0] // patches
            slots = [src(d) for d in picks] if picks else range(wide)
            vt = jnp.concatenate([kvbuf[yb, slot, 1] for slot in slots], axis=1)
            acc[rel, :, cut] = acc[rel, :, cut] * keep + dot(vt, e.astype(BF16))

    def run(yb, rels, picks=None):
        @pl.when(yb < y)
        def _():
            attend(yb, rels, False, picks)


    attend(y, (0,), True)
    take_down(0)
    take_up(0)
    q_give.wait_recv()
    attend(y, (1,), True)
    for d in (3, 2, 1):
        take_up(d)
        take_down(d)
    run(y3, (1, 0))
    run(y1, (1, 0))
    arrived(bfar, bf_r.at[0])
    lax.fori_loop(0, CHUNKS, bulk_combine, 0)
    take_far_up()
    run(y2, (1, 0), UPWARD)
    take_far_down()
    run(y2, (1,), DOWNWARD)
    opart[...] = (acc[1] / l_ref[1]).astype(BF16)
    stpart[...] = jnp.zeros(stpart.shape, F32)
    stpart[0:1] = m_ref[1]
    stpart[1:2] = l_ref[1]
    o_give.start()
    st_give.start()
    run(y2, (0,), DOWNWARD)
    o_give.wait_recv()
    st_give.wait_recv()
    m0, m1 = m_ref[0], stget[0:1]
    top = jnp.maximum(m0, m1)
    w0 = jnp.exp2((m0 - top) * factor)
    w1 = jnp.exp2((m1 - top) * factor) * stget[1:2]
    mixed = (acc[0] * w0 + oget[...].astype(F32) * w1) / (l_ref[0] * w0 + w1)
    for qb in range(XN):
        osend[qb] = jnp.transpose(mixed[:, qb * patches : (qb + 1) * patches]).astype(BF16)

    def o_copy(d):
        h = lax.rem(x + d, XN)
        return remote(osend.at[h], orecv.at[x], x_s.at[0], o_r.at[0], xpeer(d))

    for d in (2, 1, 3):
        o_copy(d).start()
    orecv[x] = osend[x]
    loads[6].wait()
    arrived(orecv.at[pl.ds(0, XN - 1)], o_r.at[0])
    gattn = jnp.concatenate([orecv[h] for h in range(XN)], axis=1)

    def out_part(zz):
        return dot(gattn, gout[:, pl.ds(pl.multiple_of(zz * piece, piece), piece)])

    half_p = patches // 2
    low, high = slice(0, half_p), slice(half_p, patches)
    far_up = remote(rsend.at[2, 0], rfar.at[0], r_s.at[0], rf_r.at[0], z_up)
    far_down = remote(rsend.at[2, 1], rfar.at[1], r_s.at[0], rf_r.at[1], z_down)

    def r_up(b):
        return remote(rsend.at[0, b], rrecv.at[0, b], r_s.at[0], r_r.at[0], z_up)

    def r_down(b):
        return remote(rsend.at[1, b], rrecv.at[1, b], r_s.at[0], r_r.at[0], z_down)

    far_part = out_part(far_at).astype(BF16)
    rsend[2, 0] = far_part[low]
    far_up.start()
    rsend[2, 1] = far_part[high]
    far_down.start()
    up_part = out_part(up_at)
    rsend[0, 1] = up_part[high].astype(BF16)
    down_part = out_part(down_at)
    rsend[1, 0] = down_part[low].astype(BF16)
    update = out_part(z)

    ri = lax.broadcasted_iota(jnp.int32, (own, own), 0)
    ci = lax.broadcasted_iota(jnp.int32, (own, own), 1)
    to_patch_major = jnp.where(ci == lax.rem(ri, 2) * span + ri // 2, 1.0, 0.0).astype(BF16)
    arrived(brecv, bk_r.at[0])
    for c in range(CHUNKS):
        state = jnp.concatenate(
            [
                ownf[c, b * span : (b + 1) * span] + brecv[c, 0, b].astype(F32) + brecv[c, 1, b].astype(F32)
                for b in range(2)
            ],
            axis=0,
        ).astype(BF16)
        bst[c * own : (c + 1) * own] = dot(to_patch_major, state).astype(BF16)

    r_up(1).start()
    r_down(0).start()
    sources, blocks = owners_ref.shape
    spread = jnp.where(
        lax.broadcasted_iota(jnp.int32, (blocks, patches), 1) // 2
        == lax.broadcasted_iota(jnp.int32, (blocks, patches), 0),
        1.0,
        0.0,
    ).astype(BF16)
    listed = dot(owners_ref[...].astype(F32).astype(BF16), spread)
    is_mine = lax.broadcasted_iota(jnp.int32, listed.shape, 0) == s
    listed_row = jnp.sum(jnp.where(is_mine, listed, 0.0), axis=0, keepdims=True)
    pr = lax.broadcasted_iota(jnp.int32, (patches, patches), 0)
    pc = lax.broadcasted_iota(jnp.int32, (patches, patches), 1)
    listed_col = jnp.sum(jnp.where(pr == pc, listed_row, 0.0), axis=1, keepdims=True)
    earlier = (listed_col == listed_row) & (pr < pc) & (lax.rem(pr, 2) == lax.rem(pc, 2))
    rank = jnp.sum(jnp.where(earlier, 1.0, 0.0), axis=0, keepdims=True)
    slot = listed_row * 4.0 + rank * 2.0 + lax.rem(pc, 2).astype(F32)
    pick = jnp.where(slot == pr.astype(F32), 1.0, 0.0).astype(BF16)

    per = patches // plane
    loads[7].wait()
    far_up.wait_recv()
    rsend[0, 0] = (up_part[low] + rfar[0].astype(F32)).astype(BF16)
    r_up(0).start()
    far_down.wait_recv()
    rsend[1, 1] = (down_part[high] + rfar[1].astype(F32)).astype(BF16)
    r_down(1).start()
    arrived(rrecv, r_r.at[0])
    total = update + pin[z].reshape(patches, piece).astype(F32)
    total = total + jnp.concatenate(
        [rrecv[0, b].astype(F32) + rrecv[1, b].astype(F32) for b in range(2)], axis=0
    )
    result = total.astype(BF16)
    sorted_rows = dot(pick, result)
    for o in range(plane):
        psend[o] = sorted_rows[o * per : (o + 1) * per].astype(BF16)

    def p_copy(dy, dx, dc):
        to = seq_of(lax.rem(y + dy, YN), lax.rem(x + dx, XN), lax.rem(core + dc, 2))
        return remote(psend.at[to], state_ref.at[s], p_s.at[0], p_r.at[0], (to, z))

    hops = [0, 1, 2, 1]
    turns = [(dy, dx, dc) for dy in range(YN) for dx in range(XN) for dc in range(2) if dy or dx or dc]
    for dy, dx, dc in sorted(turns, key=lambda turn: -hops[turn[0]] - hops[turn[1]]):
        p_copy(dy, dx, dc).start()
    keep_own = pltpu.make_async_copy(psend.at[s], state_ref.at[s], lsem.at[9])
    keep_own.start()
    gp = back.shape[0]
    re = lax.broadcasted_iota(jnp.int32, (2 * patches, patches), 0)
    ce = lax.broadcasted_iota(jnp.int32, (2 * patches, patches), 1)
    shares = jnp.zeros((2 * patches, gp), F32)
    for b in range(2):
        lift = jnp.where(re == 2 * ce + b, 1.0, 0.0).astype(BF16)
        shares = shares + dot(lift, result[:, b * gp : (b + 1) * gp])
    shares = shares.astype(BF16)
    for n in range(bst.shape[1] // 256):
        cut = slice(n * 256, (n + 1) * 256)
        both = bst[:, cut].astype(F32) + dot(shares, back[:, cut])
        byte_ref[:, :, cut] = both.astype(BF16).reshape(patches, 2, 256)

    byte_put = pltpu.make_async_copy(byte_ref, byte_hbm, lsem.at[8])
    byte_put.start()
    arrived(state_ref.at[pl.ds(0, plane - 1)], p_r.at[0])

    byte_put.wait()
    keep_own.wait()
    arrived(psend.at[pl.ds(0, plane - 1)], p_s.at[0])
    arrived(ppsend.at[pl.ds(0, ZN - 1)], pp_s.at[0])
    arrived(pin.at[pl.ds(0, ZN - 1)], ag_s.at[0])
    arrived(bsend.at[pl.ds(0, ZN - 1)], bk_s.at[0])
    arrived(qkvs, x_s.at[0])
    arrived(rsend, r_s.at[0])
    for d in range(XN):
        spread_piece(d, sent)

    @pl.when(inner)
    def _():
        for d in UPWARD:
            relay_up(y3, d).wait_send()

    @pl.when(outer)
    def _():
        for d in DOWNWARD:
            relay_down(y1, d).wait_send()

    for copy in (q_give, o_give, st_give):
        copy.wait_send()


def settle(a_hbm, b_hbm, a_out, b_out, va, vb, wb, in_sem, out_sem):
    cut = va.shape[0] // 4
    takes, puts = [], []
    for i in range(4):
        at = pl.ds(i * cut, cut)
        takes.append(pltpu.make_async_copy(a_hbm.at[at], va.at[at], in_sem.at[i]))
        puts.append(pltpu.make_async_copy(va.at[at], a_out.at[at], out_sem.at[i]))
    last = pltpu.make_async_copy(b_hbm, vb, in_sem.at[4])
    put_last = pltpu.make_async_copy(wb, b_out, out_sem.at[4])
    last.start()
    for take in takes:
        take.start()
    last.wait()
    wb[...] = jnp.concatenate([vb[o].astype(F32) for o in range(vb.shape[0])], axis=0).astype(BF16)
    put_last.start()
    for take, put in zip(takes, puts):
        take.wait()
        put.start()
    for put in puts:
        put.wait()
    put_last.wait()


def on_device(
    byte_in, local_gain, local_qkv, local_out, mlp_up, mlp_down, local_scale, patch_proj,
    global_gain, global_qkv, global_out, global_scale, back_proj, owners,
):
    patches, span8, dl = byte_in.shape
    gw = global_out.shape[1]
    piece = gw // ZN
    ff = mlp_up.shape[1]
    rows = patches * span8 // CHUNKS
    span = patches // CHUNKS
    own = 2 * span
    gp = back_proj.shape[0]
    plane = 2 * XN * YN
    wqkv3 = jnp.transpose(local_qkv, (1, 0, 2))
    gqkv3 = jnp.transpose(global_qkv, (1, 0, 2))
    hbm = pl.BlockSpec(memory_space=pl.ANY)
    vm = pl.BlockSpec(memory_space=pltpu.VMEM)
    sm = pl.BlockSpec(memory_space=pltpu.SMEM)
    dma = pltpu.SemaphoreType.DMA

    def buf(*shape, dtype=BF16):
        return pltpu.VMEM(shape, dtype)

    big = [byte_in.reshape(patches * span8, dl), wqkv3, local_out, mlp_up, mlp_down, patch_proj, gqkv3, global_out, back_proj]
    scratch = [buf(*a.shape) for a in big] + [
        buf(2, rows, dl),
        buf(2, rows, dl),
        buf(rows, ff),
        buf(rows, dl, dtype=F32),
        buf(rows, gp, dtype=F32),
        buf(CHUNKS, ZN, 2, span, dl),
        buf(CHUNKS, 2, span, dl),
        buf(CHUNKS, 2, 2, span, dl),
        buf(CHUNKS, own, dl, dtype=F32),
        buf(CHUNKS, ZN, span, 2 * gp),
        buf(CHUNKS, ZN - 1, span, 2 * gp),
        buf(CHUNKS, span, 2 * gp, dtype=F32),
        buf(ZN, CHUNKS, span, piece),
        buf(3, patches, piece, dtype=F32),
        buf(XN, 3, patches, HD),
        buf(YN, XN, 2, patches, HD),
        buf(2, XN, patches, HD),
        buf(2, 1, XN * patches, dtype=F32),
        buf(2, 1, XN * patches, dtype=F32),
        buf(2, HD, XN * patches, dtype=F32),
        buf(HD, XN * patches),
        buf(HD, XN * patches),
        buf(8, XN * patches, dtype=F32),
        buf(8, XN * patches, dtype=F32),
        buf(XN, patches, HD),
        buf(XN, patches, HD),
        buf(2, patches // 2, piece),
        buf(3, 2, patches // 2, piece),
        buf(2, 2, patches // 2, piece),
        buf(2 * patches, dl),
        buf(plane, patches // plane, piece),
        buf(patches, 2, dl),
        dma((10,)),
        dma((CHUNKS,)),
    ]
    counts = (1, CHUNKS, 1, 3, CHUNKS, 1, 1, 1, 1, 3, 1, 4, 4, 4, 4, 2, 2, 2, 2, 3, 3, 1, 2, 1, 1, 1, 1)
    scratch += [dma((n,)) for n in counts]
    byte_out, global_state = pl.pallas_call(
        kernel,
        out_shape=(
            jax.ShapeDtypeStruct((patches, 2, dl), BF16),
            jax.ShapeDtypeStruct((plane, patches // plane, piece), BF16),
        ),
        in_specs=[hbm] * 9 + [vm] * 3 + [sm] * 2,
        out_specs=(hbm, hbm),
        scratch_shapes=scratch,
        compiler_params=pltpu.CompilerParams(
            collective_id=0, has_side_effects=True, vmem_limit_bytes=60 * 1024 * 1024
        ),
    )(*big, local_gain.reshape(1, dl), global_gain.reshape(1, gw), owners, local_scale, global_scale)
    return pl.pallas_call(
        settle,
        out_shape=(
            jax.ShapeDtypeStruct(byte_out.shape, BF16),
            jax.ShapeDtypeStruct((patches, piece), BF16),
        ),
        in_specs=[hbm] * 2,
        out_specs=(hbm, hbm),
        scratch_shapes=[buf(*byte_out.shape), buf(*global_state.shape), buf(patches, piece), dma((5,)), dma((5,))],
    )(byte_out, global_state)


def solution(mesh):
    placed = (
        P("seq", None, None),
        P(),
        P(None, None, "head"),
        P("head", None),
        P(None, "head"),
        P("head", None),
        P("head"),
        P(),
        P(),
        P(None, None, "head"),
        P("head", None),
        P("head"),
        P(),
        P(),
    )
    return jax.shard_map(
        on_device,
        mesh=mesh,
        in_specs=placed,
        out_specs=(P("seq", "head", None), P("seq", "head")),
        check_vma=False,
    )
```

```python
import functools
import math

import jax
import jax.numpy as jnp
from jax import lax
from jax.experimental import pallas as pl
from jax.experimental.pallas import tpu as pltpu
from jax.sharding import PartitionSpec as P

EPS = 1e-06
NEG = -1e30
MESH = pl.DeviceIdType.MESH
F32 = jnp.float32
BF16 = jnp.bfloat16
XN = 4
YN = 4
ZN = 4
CHUNKS = 4
HD = 128
UPWARD = (0, 3)
DOWNWARD = (1, 2)


def dot(a, b):
    return jnp.dot(a, b, preferred_element_type=F32)


def dot_t(a, b):
    return lax.dot_general(a, b, (((1,), (1,)), ((), ())), preferred_element_type=F32)


def unit(v):
    return v * lax.rsqrt(jnp.mean(v * v, axis=-1, keepdims=True) + EPS)


def kernel(
    x_hbm, wqkv_hbm, wo_hbm, up_hbm, down_hbm, pp_hbm, gqkv_hbm, gout_hbm, back_hbm,
    gain_ref, ggain_ref, owners_ref, lscale_ref, gscale_ref,
    byte_hbm, state_ref,
    xv, wqkv, wo, up, down, ppw, gqkv, gout, back,
    xps, normed, act, part, ppf, bsend, bfar, brecv, ownf, ppsend, pprecv, ppown, pin,
    mixed_qkv, qkvs, kvbuf, qbuf, m_ref, l_ref, acc, opart, oget, stpart, stget, osend, orecv, rfar, rsend, rrecv, bst, psend, byte_ref,
    lsem, x_sem, pp_s, pp_r, ag_s, ag_r, an_r, bf_r, bk_s, bk_r, x_s, xk_r, xq_r,
    yu_s, yu_r, yd_s, yd_r, ru_s, ru_r, rd_s, rd_r, c_s, c_r, o_r, rf_r, r_s, r_r, p_s, p_r,
):
    s = lax.axis_index("seq")
    z = lax.axis_index("head")
    core = lax.rem(s, 2)
    x = lax.rem(s // 2, XN)
    y = s // (2 * XN)
    rows = xv.shape[0] // CHUNKS
    span = rows // 8
    own = 2 * span

    def seq_of(yy, xx, cc):
        return (yy * XN + xx) * 2 + cc

    def zpeer(d):
        return (s, lax.rem(z + d, ZN))

    def xpeer(d):
        return (seq_of(y, lax.rem(x + d, XN), core), z)

    y_up = (seq_of(lax.rem(y + 1, YN), x, core), z)
    y_down = (seq_of(lax.rem(y + YN - 1, YN), x, core), z)
    sibling = (seq_of(y, x, 1 - core), z)

    loads = [
        pltpu.make_async_copy(a, b, lsem.at[i])
        for i, (a, b) in enumerate(
            ((wqkv_hbm, wqkv), (up_hbm, up), (wo_hbm, wo), (down_hbm, down), (pp_hbm, ppw),
             (gqkv_hbm, gqkv), (gout_hbm, gout), (back_hbm, back))
        )
    ]
    def xload(c):
        at = pl.ds(pl.multiple_of(c * rows, rows), rows)
        return pltpu.make_async_copy(x_hbm.at[at], xv.at[at], x_sem.at[c])

    xload(0).start()
    for load in loads[:5]:
        load.start()
    for c in range(1, CHUNKS):
        xload(c).start()

    barrier = pltpu.get_barrier_semaphore()
    plane = 2 * XN * YN

    def greet(peer):
        pl.semaphore_signal(barrier, inc=1, device_id=peer, device_id_type=MESH)

    def greet_plane(d, carry):
        greet((lax.rem(s + d, plane), z))
        return carry

    for d in (1, 2, 3):
        greet(zpeer(d))
    lax.fori_loop(1, plane, greet_plane, 0)

    def remote(src, dst, ss, rs, peer):
        return pltpu.make_async_remote_copy(
            src_ref=src, dst_ref=dst, send_sem=ss, recv_sem=rs, device_id=peer, device_id_type=MESH
        )

    def pp_copy(c, d):
        return remote(
            ppsend.at[c, lax.rem(z + d, ZN)], pprecv.at[c, d - 1], pp_s.at[0], pp_r.at[c], zpeer(d)
        )

    def ag_copy(c, d):
        rs = an_r.at[c] if d == ZN - 1 else ag_r.at[d - 1]
        return remote(pin.at[z, c], pin.at[z, c], ag_s.at[0], rs, zpeer(d))

    def ag_relay(c):
        at = pin.at[up_at, c]
        arrived(at, an_r.at[c])
        remote(at, at, ag_s.at[0], ag_r.at[1], z_down).start()

    z_up = zpeer(1)
    z_down = zpeer(ZN - 1)
    up_at = lax.rem(z + 1, ZN)
    down_at = lax.rem(z + ZN - 1, ZN)
    far_at = lax.rem(z + 2, ZN)

    def bulk_far(c):
        return (
            remote(bsend.at[c, far_at, 0], bfar.at[c, 0], bk_s.at[0], bf_r.at[0], z_up),
            remote(bsend.at[c, far_at, 1], bfar.at[c, 1], bk_s.at[0], bf_r.at[0], z_down),
        )

    def bulk_up(c, b):
        return remote(bsend.at[c, up_at, b], brecv.at[c, 0, b], bk_s.at[0], bk_r.at[0], z_up)

    def bulk_down(c, b):
        return remote(bsend.at[c, down_at, b], brecv.at[c, 1, b], bk_s.at[0], bk_r.at[0], z_down)

    def bulk_combine(c, carry):
        bsend[c, up_at, 0] = (bsend[c, up_at, 0].astype(F32) + bfar[c, 0].astype(F32)).astype(BF16)
        bulk_up(c, 0).start()
        bsend[c, down_at, 1] = (bsend[c, down_at, 1].astype(F32) + bfar[c, 1].astype(F32)).astype(BF16)
        bulk_down(c, 1).start()
        return carry

    def arrived(ref, sem):
        pltpu.make_async_copy(ref, ref, sem).wait()

    def finish_patches(c, last_one=False):
        total = ppown[c]
        arrived(pprecv.at[c], pp_r.at[c])
        for d in (1, 2, 3):
            total = total + pprecv[c, d - 1].astype(F32)
        pin[z, c] = total.astype(BF16)
        for d in (2, 1, 3) if last_one else (1, 3):
            ag_copy(c, d).start()

    row_i = lax.broadcasted_iota(jnp.int32, (rows, rows), 0)
    col_i = lax.broadcasted_iota(jnp.int32, (rows, rows), 1)
    to_byte_major = jnp.where(
        col_i == lax.rem(row_i, span) * 8 + row_i // span, 1.0, 0.0
    ).astype(BF16)

    def prepare(c, slot):
        xp = dot(to_byte_major, xv[pl.ds(pl.multiple_of(c * rows, rows), rows), :])
        xps[slot] = xp.astype(BF16)
        normed[slot] = (
            xp * lax.rsqrt(jnp.mean(xp * xp, axis=-1, keepdims=True) + EPS) * gain_ref[...]
        ).astype(BF16)

    def gelu(v):
        inner = v * (0.7978845608028654 + (0.7978845608028654 * 0.044715) * (v * v))
        half = 0.5 * v
        return (half + half * jnp.tanh(inner)).astype(BF16)

    rr = lax.broadcasted_iota(jnp.int32, (rows, rows), 0)
    cc = lax.broadcasted_iota(jnp.int32, (rows, rows), 1)
    seen = (lax.rem(rr, span) == lax.rem(cc, span)) & (cc // span <= rr // span)

    def chunk(c, ahead, first=False):
        slot = lax.rem(c, 2)
        nv = normed[slot]
        tiles = [slice(n * 256, (n + 1) * 256) for n in range(up.shape[1] // 256)]
        cuts = [slice(h * HD, (h + 1) * HD) for h in range(2)]
        q2 = dot(nv, wqkv[0])
        k2 = dot(nv, wqkv[1])
        v2 = dot(nv, wqkv[2]).astype(BF16)
        hidden = dot(nv, up[:, tiles[0]])
        qs = [unit(q2[:, cut]).astype(BF16) for cut in cuts]
        ks = [unit(k2[:, cut]).astype(BF16) for cut in cuts]
        later = dot(nv, up[:, tiles[1]])
        scores = [dot_t(qs[h], ks[h]) for h in range(2)]
        act[:, tiles[0]] = gelu(hidden)
        hidden = dot(nv, up[:, tiles[2]])
        es, totals = [], []
        for h in range(2):
            sc = jnp.where(seen, scores[h] * (lscale_ref[h] / math.sqrt(HD)), NEG)
            e = jnp.exp(sc - jnp.max(sc, axis=-1, keepdims=True))
            totals.append(jnp.sum(e, axis=-1, keepdims=True))
            es.append(e.astype(BF16))
        act[:, tiles[1]] = gelu(later)
        later = dot(nv, up[:, tiles[3]])
        heads = [(dot(es[h], v2[:, cuts[h]]) / totals[h]).astype(BF16) for h in range(2)]
        lo = jnp.concatenate(heads, axis=1)
        act[:, tiles[2]] = gelu(hidden)
        act[:, tiles[3]] = gelu(later)
        if ahead is not None:
            xload(ahead).wait()
            prepare(ahead, 1 - slot)
        if first:
            for load in loads[2:5]:
                load.wait()
            for load in loads[5:]:
                load.start()
        mine = lax.broadcasted_iota(jnp.int32, (rows, 1), 0) // own == z
        a = act[...]
        for cut in tiles:
            t = dot(lo, wo[:, cut]) + dot(a, down[:, cut])
            t = t + jnp.where(mine, xps[slot, :, cut].astype(F32), 0.0)
            part[:, cut] = t
            tb = t.astype(BF16)
            for h in range(ZN):
                for b in range(2):
                    at = h * own + b * span
                    bsend[c, h, b, :, cut] = tb[at : at + span]
        ownf[c] = part[pl.ds(pl.multiple_of(z * own, own), own), :]
        pp = dot(bsend[c].reshape(rows, part.shape[1]), ppw[...])
        ppf[...] = pp
        pb = pp.astype(BF16)
        gp = pp.shape[1]
        for h in range(ZN):
            for b in range(2):
                at = (2 * h + b) * span
                ppsend[c, h, :, b * gp : (b + 1) * gp] = pb[at : at + span]
        for b in range(2):
            at = pl.multiple_of(z * own + b * span, span)
            ppown[c, :, b * gp : (b + 1) * gp] = ppf[pl.ds(at, span), :]

        @pl.when(c == 0)
        def _():
            pl.semaphore_wait(barrier, ZN - 1 + plane - 1)

        for d in (2, 1, 3):
            pp_copy(c, d).start()

        @pl.when(c >= 1)
        def _():
            finish_patches(c - 1)

        @pl.when(c >= 2)
        def _():
            ag_relay(c - 2)


    xload(0).wait()
    prepare(jnp.int32(0), 0)
    for load in loads[:2]:
        load.wait()

    def chunk_step(c, carry):
        chunk(c, c + 1)
        return carry

    chunk(jnp.int32(0), jnp.int32(1), True)
    lax.fori_loop(1, CHUNKS - 1, chunk_step, 0)
    chunk(jnp.int32(CHUNKS - 1), None)
    finish_patches(CHUNKS - 1, True)
    ag_relay(CHUNKS - 2)
    loads[5].wait()
    patches = CHUNKS * span
    piece = pin.shape[3]
    square = jnp.zeros((patches, 1), F32)
    for d in (0, 1, 3, 2):
        h = lax.rem(z + ZN - d, ZN)
        if d:
            if d == ZN - 1:
                arrived(pin.at[h, CHUNKS - 1], an_r.at[CHUNKS - 1])
            else:
                arrived(pin.at[h], ag_r.at[d - 1])
        at = pl.ds(pl.multiple_of(h * piece, piece), piece)
        v = pin[h].reshape(patches, piece).astype(F32)
        square = square + jnp.sum(v * v, axis=-1, keepdims=True)
        g = (v * ggain_ref[:, at]).astype(BF16)
        for j in (1, 2, 0):
            for half in range(2):
                cut = slice(half * 256, (half + 1) * 256)
                r = dot(g, gqkv[j, at, cut])
                mixed_qkv[j, :, cut] = r if d == 0 else mixed_qkv[j, :, cut] + r
    inv = lax.rsqrt(square / (ZN * piece) + EPS)

    def project(j):
        for t in range(XN):
            v = mixed_qkv[j, :, t * HD : (t + 1) * HD] * inv
            if j < 2:
                v = unit(v)
            if j == 2:
                v = jnp.transpose(v)
            qkvs[t, j] = v.astype(BF16)

    def xk_copy(d):
        h = lax.rem(x + d, XN)
        return remote(qkvs.at[h, pl.ds(1, 2)], kvbuf.at[y, x], x_s.at[0], xk_r.at[d - 1], xpeer(d))

    def src(d):
        return lax.rem(x + XN - d, XN)

    def xk_arrival(d):
        at = kvbuf.at[y, src(d)]
        return pltpu.make_async_copy(at, at, xk_r.at[d - 1])

    def xq_copy(d):
        h = lax.rem(x + d, XN)
        return remote(qkvs.at[h, 0], qbuf.at[0, x], x_s.at[0], xq_r.at[0], xpeer(d))

    y1 = lax.rem(y + 1, YN)
    y2 = lax.rem(y + 2, YN)
    y3 = lax.rem(y + 3, YN)

    def up_copy(row, d, ss, rs):
        at = kvbuf.at[row, src(d)]
        return remote(at, at, ss.at[d], rs.at[d], y_up)

    def down_copy(row, d, ss, rs):
        at = kvbuf.at[row, src(d)]
        return remote(at, at, ss.at[d], rs.at[d], y_down)

    def relay_up(row, d):
        at = kvbuf.at[row, src(d)]
        return remote(at, at, ru_s.at[d // 2], ru_r.at[d // 2], y_up)

    def relay_down(row, d):
        at = kvbuf.at[row, src(d)]
        return remote(at, at, rd_s.at[d // 2], rd_r.at[d // 2], y_down)

    last = YN - 1
    inner = (y >= 1) & (y < last)
    outer = (y == 0) | (y == last)

    def spread_piece(d, act_on):
        @pl.when(y < last)
        def _():
            act_on(up_copy(y, d, yu_s, yu_r))

        @pl.when((y == 0) | ((y == 1) & (d in DOWNWARD)))
        def _():
            act_on(down_copy(y, d, yd_s, yd_r))

    def start(copy):
        copy.start()

    def sent(copy):
        copy.wait_send()

    def take_down(d):
        @pl.when(y >= 1)
        def _():
            up_copy(y3, d, yu_s, yu_r).wait_recv()

        if d in UPWARD:

            @pl.when(inner)
            def _():
                relay_up(y3, d).start()

    def take_up(d):
        @pl.when((y == last) | ((y == 0) & (d in DOWNWARD)))
        def _():
            down_copy(y1, d, yd_s, yd_r).wait_recv()

        if d in DOWNWARD:

            @pl.when(outer)
            def _():
                relay_down(y1, d).start()

    def take_far_up():
        @pl.when(y >= 2)
        def _():
            for d in UPWARD:
                relay_up(y2, d).wait_recv()

    def take_far_down():
        @pl.when(y >= 2)
        def _():
            for d in DOWNWARD:
                relay_down(y2, d).wait_recv()

    q_give = remote(qbuf.at[0], qbuf.at[1], c_s.at[0], c_r.at[0], sibling)
    o_give = remote(opart, oget, c_s.at[1], c_r.at[1], sibling)
    st_give = remote(stpart, stget, c_s.at[2], c_r.at[2], sibling)

    project(1)
    project(2)
    for d in (2, 1, 3):
        xk_copy(d).start()
    kvbuf[y, x] = qkvs[x, 1:3]
    spread_piece(0, start)
    project(0)
    for d in (2, 1, 3):
        xq_copy(d).start()
    qbuf[0, x] = qkvs[x, 0]
    for c in range(CHUNKS):
        for copy in bulk_far(c):
            copy.start()
    for c in range(CHUNKS):
        bulk_up(c, 1).start()
        bulk_down(c, 0).start()
    m_ref[...] = jnp.full(m_ref.shape, NEG, F32)
    l_ref[...] = jnp.zeros(l_ref.shape, F32)
    acc[...] = jnp.zeros(acc.shape, F32)
    factor = gscale_ref[x] * (math.log2(math.e) / math.sqrt(HD))

    for d in (3, 2, 1):
        xk_arrival(d).wait()
        spread_piece(d, start)
    arrived(qbuf.at[0, pl.ds(0, XN - 1)], xq_r.at[0])
    q_give.start()

    half_q = XN * patches // 2

    def attend(yb, rels, masked, picks=None):
        chains = [(rel, part_q) for rel in rels for part_q in range(2)]

        def raw(chain):
            rel, part_q = chain
            wide = (part_q + 1) * XN // 2 if masked else XN
            queries = qbuf[rel].reshape(XN * patches, HD)[part_q * half_q : (part_q + 1) * half_q]
            if picks:
                k = jnp.concatenate([kvbuf[yb, src(d), 0] for d in picks], axis=0)
            else:
                k = kvbuf[yb, 0:wide, 0].reshape(wide * patches, HD)
            scores = dot_t(k, queries)
            if masked:
                kk = lax.broadcasted_iota(jnp.int32, scores.shape, 0)
                qq = lax.broadcasted_iota(jnp.int32, scores.shape, 1) + part_q * half_q
                theirs = core + rel * (1 - 2 * core)
                k_at = kk + (kk // patches + core) * patches
                q_at = qq + (qq // patches + theirs) * patches
                scores = jnp.where(k_at <= q_at, scores, NEG)
            return scores

        def fold(op, v):
            return op(op(v.reshape(8, v.shape[0] // 8, v.shape[1]), axis=0), axis=0, keepdims=True)

        upcoming = raw(chains[0])
        for i, (rel, part_q) in enumerate(chains):
            scores = upcoming
            if i + 1 < len(chains):
                upcoming = raw(chains[i + 1])
            cut = slice(part_q * half_q, (part_q + 1) * half_q)
            old = m_ref[rel, :, cut]
            new = jnp.maximum(old, fold(jnp.max, scores))
            keep = jnp.exp2((old - new) * factor)
            e = jnp.exp2((scores - new) * factor)
            m_ref[rel, :, cut] = new
            l_ref[rel, :, cut] = l_ref[rel, :, cut] * keep + fold(jnp.sum, e)
            wide = scores.shape[0] // patches
            slots = [src(d) for d in picks] if picks else range(wide)
            vt = jnp.concatenate([kvbuf[yb, slot, 1] for slot in slots], axis=1)
            acc[rel, :, cut] = acc[rel, :, cut] * keep + dot(vt, e.astype(BF16))

    def run(yb, rels, picks=None):
        @pl.when(yb < y)
        def _():
            attend(yb, rels, False, picks)


    attend(y, (0,), True)
    take_down(0)
    take_up(0)
    q_give.wait_recv()
    attend(y, (1,), True)
    for d in (3, 2, 1):
        take_up(d)
        take_down(d)
    run(y3, (1, 0))
    run(y1, (1, 0))
    arrived(bfar, bf_r.at[0])
    lax.fori_loop(0, CHUNKS, bulk_combine, 0)
    take_far_up()
    run(y2, (1, 0), UPWARD)
    take_far_down()
    run(y2, (1,), DOWNWARD)
    opart[...] = (acc[1] / l_ref[1]).astype(BF16)
    stpart[...] = jnp.zeros(stpart.shape, F32)
    stpart[0:1] = m_ref[1]
    stpart[1:2] = l_ref[1]
    o_give.start()
    st_give.start()
    run(y2, (0,), DOWNWARD)
    o_give.wait_recv()
    st_give.wait_recv()
    m0, m1 = m_ref[0], stget[0:1]
    top = jnp.maximum(m0, m1)
    w0 = jnp.exp2((m0 - top) * factor)
    w1 = jnp.exp2((m1 - top) * factor) * stget[1:2]
    mixed = (acc[0] * w0 + oget[...].astype(F32) * w1) / (l_ref[0] * w0 + w1)
    for qb in range(XN):
        osend[qb] = jnp.transpose(mixed[:, qb * patches : (qb + 1) * patches]).astype(BF16)

    def o_copy(d):
        h = lax.rem(x + d, XN)
        return remote(osend.at[h], orecv.at[x], x_s.at[0], o_r.at[0], xpeer(d))

    for d in (2, 1, 3):
        o_copy(d).start()
    orecv[x] = osend[x]
    loads[6].wait()
    arrived(orecv.at[pl.ds(0, XN - 1)], o_r.at[0])
    gattn = jnp.concatenate([orecv[h] for h in range(XN)], axis=1)

    def out_part(zz):
        return dot(gattn, gout[:, pl.ds(pl.multiple_of(zz * piece, piece), piece)])

    half_p = patches // 2
    low, high = slice(0, half_p), slice(half_p, patches)
    far_up = remote(rsend.at[2, 0], rfar.at[0], r_s.at[0], rf_r.at[0], z_up)
    far_down = remote(rsend.at[2, 1], rfar.at[1], r_s.at[0], rf_r.at[1], z_down)

    def r_up(b):
        return remote(rsend.at[0, b], rrecv.at[0, b], r_s.at[0], r_r.at[0], z_up)

    def r_down(b):
        return remote(rsend.at[1, b], rrecv.at[1, b], r_s.at[0], r_r.at[0], z_down)

    far_part = out_part(far_at).astype(BF16)
    rsend[2, 0] = far_part[low]
    far_up.start()
    rsend[2, 1] = far_part[high]
    far_down.start()
    up_part = out_part(up_at)
    rsend[0, 1] = up_part[high].astype(BF16)
    down_part = out_part(down_at)
    rsend[1, 0] = down_part[low].astype(BF16)
    update = out_part(z)

    ri = lax.broadcasted_iota(jnp.int32, (own, own), 0)
    ci = lax.broadcasted_iota(jnp.int32, (own, own), 1)
    to_patch_major = jnp.where(ci == lax.rem(ri, 2) * span + ri // 2, 1.0, 0.0).astype(BF16)
    arrived(brecv, bk_r.at[0])
    for c in range(CHUNKS):
        state = jnp.concatenate(
            [
                ownf[c, b * span : (b + 1) * span] + brecv[c, 0, b].astype(F32) + brecv[c, 1, b].astype(F32)
                for b in range(2)
            ],
            axis=0,
        ).astype(BF16)
        bst[c * own : (c + 1) * own] = dot(to_patch_major, state).astype(BF16)

    r_up(1).start()
    r_down(0).start()
    sources, blocks = owners_ref.shape
    spread = jnp.where(
        lax.broadcasted_iota(jnp.int32, (blocks, patches), 1) // 2
        == lax.broadcasted_iota(jnp.int32, (blocks, patches), 0),
        1.0,
        0.0,
    ).astype(BF16)
    listed = dot(owners_ref[...].astype(F32).astype(BF16), spread)
    is_mine = lax.broadcasted_iota(jnp.int32, listed.shape, 0) == s
    listed_row = jnp.sum(jnp.where(is_mine, listed, 0.0), axis=0, keepdims=True)
    pr = lax.broadcasted_iota(jnp.int32, (patches, patches), 0)
    pc = lax.broadcasted_iota(jnp.int32, (patches, patches), 1)
    listed_col = jnp.sum(jnp.where(pr == pc, listed_row, 0.0), axis=1, keepdims=True)
    earlier = (listed_col == listed_row) & (pr < pc) & (lax.rem(pr, 2) == lax.rem(pc, 2))
    rank = jnp.sum(jnp.where(earlier, 1.0, 0.0), axis=0, keepdims=True)
    slot = listed_row * 4.0 + rank * 2.0 + lax.rem(pc, 2).astype(F32)
    pick = jnp.where(slot == pr.astype(F32), 1.0, 0.0).astype(BF16)

    per = patches // plane
    loads[7].wait()
    far_up.wait_recv()
    rsend[0, 0] = (up_part[low] + rfar[0].astype(F32)).astype(BF16)
    r_up(0).start()
    far_down.wait_recv()
    rsend[1, 1] = (down_part[high] + rfar[1].astype(F32)).astype(BF16)
    r_down(1).start()
    arrived(rrecv, r_r.at[0])
    total = update + pin[z].reshape(patches, piece).astype(F32)
    total = total + jnp.concatenate(
        [rrecv[0, b].astype(F32) + rrecv[1, b].astype(F32) for b in range(2)], axis=0
    )
    result = total.astype(BF16)
    sorted_rows = dot(pick, result)
    for o in range(plane):
        psend[o] = sorted_rows[o * per : (o + 1) * per].astype(BF16)

    def p_copy(dy, dx, dc):
        to = seq_of(lax.rem(y + dy, YN), lax.rem(x + dx, XN), lax.rem(core + dc, 2))
        return remote(psend.at[to], state_ref.at[s], p_s.at[0], p_r.at[0], (to, z))

    hops = [0, 1, 2, 1]
    turns = [(dy, dx, dc) for dy in range(YN) for dx in range(XN) for dc in range(2) if dy or dx or dc]
    for dy, dx, dc in sorted(turns, key=lambda turn: -hops[turn[0]] - hops[turn[1]]):
        p_copy(dy, dx, dc).start()
    keep_own = pltpu.make_async_copy(psend.at[s], state_ref.at[s], lsem.at[9])
    keep_own.start()
    gp = back.shape[0]
    re = lax.broadcasted_iota(jnp.int32, (2 * patches, patches), 0)
    ce = lax.broadcasted_iota(jnp.int32, (2 * patches, patches), 1)
    shares = jnp.zeros((2 * patches, gp), F32)
    for b in range(2):
        lift = jnp.where(re == 2 * ce + b, 1.0, 0.0).astype(BF16)
        shares = shares + dot(lift, result[:, b * gp : (b + 1) * gp])
    shares = shares.astype(BF16)
    for n in range(bst.shape[1] // 256):
        cut = slice(n * 256, (n + 1) * 256)
        both = bst[:, cut].astype(F32) + dot(shares, back[:, cut])
        byte_ref[:, :, cut] = both.astype(BF16).reshape(patches, 2, 256)

    byte_put = pltpu.make_async_copy(byte_ref, byte_hbm, lsem.at[8])
    byte_put.start()
    arrived(state_ref.at[pl.ds(0, plane - 1)], p_r.at[0])

    byte_put.wait()
    keep_own.wait()
    arrived(psend.at[pl.ds(0, plane - 1)], p_s.at[0])
    arrived(ppsend.at[pl.ds(0, ZN - 1)], pp_s.at[0])
    arrived(pin.at[pl.ds(0, ZN - 1)], ag_s.at[0])
    arrived(bsend.at[pl.ds(0, ZN - 1)], bk_s.at[0])
    arrived(qkvs, x_s.at[0])
    arrived(rsend, r_s.at[0])
    for d in range(XN):
        spread_piece(d, sent)

    @pl.when(inner)
    def _():
        for d in UPWARD:
            relay_up(y3, d).wait_send()

    @pl.when(outer)
    def _():
        for d in DOWNWARD:
            relay_down(y1, d).wait_send()

    for copy in (q_give, o_give, st_give):
        copy.wait_send()


def settle(a_hbm, b_hbm, a_out, b_out, va, vb, wb, in_sem, out_sem):
    cut = va.shape[0] // 4
    takes, puts = [], []
    for i in range(4):
        at = pl.ds(i * cut, cut)
        takes.append(pltpu.make_async_copy(a_hbm.at[at], va.at[at], in_sem.at[i]))
        puts.append(pltpu.make_async_copy(va.at[at], a_out.at[at], out_sem.at[i]))
    last = pltpu.make_async_copy(b_hbm, vb, in_sem.at[4])
    put_last = pltpu.make_async_copy(wb, b_out, out_sem.at[4])
    last.start()
    for take in takes:
        take.start()
    last.wait()
    wb[...] = jnp.concatenate([vb[o].astype(F32) for o in range(vb.shape[0])], axis=0).astype(BF16)
    put_last.start()
    for take, put in zip(takes, puts):
        take.wait()
        put.start()
    for put in puts:
        put.wait()
    put_last.wait()


def on_device(
    byte_in, local_gain, local_qkv, local_out, mlp_up, mlp_down, local_scale, patch_proj,
    global_gain, global_qkv, global_out, global_scale, back_proj, owners,
):
    patches, span8, dl = byte_in.shape
    gw = global_out.shape[1]
    piece = gw // ZN
    ff = mlp_up.shape[1]
    rows = patches * span8 // CHUNKS
    span = patches // CHUNKS
    own = 2 * span
    gp = back_proj.shape[0]
    plane = 2 * XN * YN
    wqkv3 = jnp.transpose(local_qkv, (1, 0, 2))
    gqkv3 = jnp.transpose(global_qkv, (1, 0, 2))
    hbm = pl.BlockSpec(memory_space=pl.ANY)
    vm = pl.BlockSpec(memory_space=pltpu.VMEM)
    sm = pl.BlockSpec(memory_space=pltpu.SMEM)
    dma = pltpu.SemaphoreType.DMA

    def buf(*shape, dtype=BF16):
        return pltpu.VMEM(shape, dtype)

    big = [byte_in.reshape(patches * span8, dl), wqkv3, local_out, mlp_up, mlp_down, patch_proj, gqkv3, global_out, back_proj]
    scratch = [buf(*a.shape) for a in big] + [
        buf(2, rows, dl),
        buf(2, rows, dl),
        buf(rows, ff),
        buf(rows, dl, dtype=F32),
        buf(rows, gp, dtype=F32),
        buf(CHUNKS, ZN, 2, span, dl),
        buf(CHUNKS, 2, span, dl),
        buf(CHUNKS, 2, 2, span, dl),
        buf(CHUNKS, own, dl, dtype=F32),
        buf(CHUNKS, ZN, span, 2 * gp),
        buf(CHUNKS, ZN - 1, span, 2 * gp),
        buf(CHUNKS, span, 2 * gp, dtype=F32),
        buf(ZN, CHUNKS, span, piece),
        buf(3, patches, piece, dtype=F32),
        buf(XN, 3, patches, HD),
        buf(YN, XN, 2, patches, HD),
        buf(2, XN, patches, HD),
        buf(2, 1, XN * patches, dtype=F32),
        buf(2, 1, XN * patches, dtype=F32),
        buf(2, HD, XN * patches, dtype=F32),
        buf(HD, XN * patches),
        buf(HD, XN * patches),
        buf(8, XN * patches, dtype=F32),
        buf(8, XN * patches, dtype=F32),
        buf(XN, patches, HD),
        buf(XN, patches, HD),
        buf(2, patches // 2, piece),
        buf(3, 2, patches // 2, piece),
        buf(2, 2, patches // 2, piece),
        buf(2 * patches, dl),
        buf(plane, patches // plane, piece),
        buf(patches, 2, dl),
        dma((10,)),
        dma((CHUNKS,)),
    ]
    counts = (1, CHUNKS, 1, 3, CHUNKS, 1, 1, 1, 1, 3, 1, 4, 4, 4, 4, 2, 2, 2, 2, 3, 3, 1, 2, 1, 1, 1, 1)
    scratch += [dma((n,)) for n in counts]
    byte_out, global_state = pl.pallas_call(
        kernel,
        out_shape=(
            jax.ShapeDtypeStruct((patches, 2, dl), BF16),
            jax.ShapeDtypeStruct((plane, patches // plane, piece), BF16),
        ),
        in_specs=[hbm] * 9 + [vm] * 3 + [sm] * 2,
        out_specs=(hbm, hbm),
        scratch_shapes=scratch,
        compiler_params=pltpu.CompilerParams(
            collective_id=0, has_side_effects=True, vmem_limit_bytes=60 * 1024 * 1024
        ),
    )(*big, local_gain.reshape(1, dl), global_gain.reshape(1, gw), owners, local_scale, global_scale)
    return pl.pallas_call(
        settle,
        out_shape=(
            jax.ShapeDtypeStruct(byte_out.shape, BF16),
            jax.ShapeDtypeStruct((patches, piece), BF16),
        ),
        in_specs=[hbm] * 2,
        out_specs=(hbm, hbm),
        scratch_shapes=[buf(*byte_out.shape), buf(*global_state.shape), buf(patches, piece), dma((5,)), dma((5,))],
    )(byte_out, global_state)


def solution(mesh):
    placed = (
        P("seq", None, None),
        P(),
        P(None, None, "head"),
        P("head", None),
        P(None, "head"),
        P("head", None),
        P("head"),
        P(),
        P(),
        P(None, None, "head"),
        P("head", None),
        P("head"),
        P(),
        P(),
    )
    return jax.shard_map(
        on_device,
        mesh=mesh,
        in_specs=placed,
        out_specs=(P("seq", "head", None), P("seq", "head")),
        check_vma=False,
    )
```
